32 devices in a mesh: fsdp: 2 (over x), ctx: 4 (over y, core), tp: 4 (over z).
Axes of the slice: x: 2, y: 2, z: 4, core: 2. Of those that a mesh axis runs over, the one named last changes fastest.
Arguments:
- hidden_in: bfloat16 [2, 2048, 2304], P('fsdp', 'ctx'), may hold values from -6 to 6
- out_cotangent: bfloat16 [2, 2048, 2304], P('fsdp', 'ctx'), may hold values from -6 to 6
- attn_gain: bfloat16 [2304], P(('fsdp', 'ctx')), may hold values from 0.5 to 1.5
- qkv_weight: bfloat16 [2304, 3, 2304], P(('fsdp', 'ctx'), None, 'tp'), may hold values from -1.66666667 to 1.66666667
- out_weight: bfloat16 [2304, 2304], P('tp', ('fsdp', 'ctx')), may hold values from -16 to 16
- ffn_gain: bfloat16 [2304], P(('fsdp', 'ctx')), may hold values from 0.5 to 1.5
- gate_weight: bfloat16 [8, 2304, 5760], P(None, ('fsdp', 'ctx'), 'tp'), may hold values from -0.125 to 0.125
- up_weight: bfloat16 [8, 2304, 5760], P(None, ('fsdp', 'ctx'), 'tp'), may hold values from -0.125 to 0.125
- down_weight: bfloat16 [8, 5760, 2304], P(None, 'tp', ('fsdp', 'ctx')), may hold values from -0.75 to 0.75
- expert_ids: int32 [2, 2048, 2], P('fsdp', 'ctx'), may hold values from 0 to 7, all different within a row
- route_weights: float32 [2, 2048, 2], P('fsdp', 'ctx'), may hold values from 0.1 to 1
Outputs:
- block_out: bfloat16 [2, 2048, 2304], P('fsdp', 'ctx')
- input_grad: float32 [2, 2048, 2304], P('fsdp', 'ctx')
- attn_gain_grad: float32 [2304], P(('fsdp', 'ctx'))
- qkv_weight_grad: float32 [2304, 3, 2304], P(('fsdp', 'ctx'), None, 'tp')
- out_weight_grad: float32 [2304, 2304], P('tp', ('fsdp', 'ctx'))
- ffn_gain_grad: float32 [2304], P(('fsdp', 'ctx'))
- gate_weight_grad: float32 [8, 2304, 5760], P(None, ('fsdp', 'ctx'), 'tp')
- up_weight_grad: float32 [8, 2304, 5760], P(None, ('fsdp', 'ctx'), 'tp')
- down_weight_grad: float32 [8, 5760, 2304], P(None, 'tp', ('fsdp', 'ctx'))
The draws below stay inside these ranges and needn't reach their ends.
Inputs may be any that keep to these rules, and one draw needn't show every extreme that they name: `expert_ids`: each token names 2 different experts, and every expert is named somewhere.
All inputs are finite; a program needn't handle non-finite values.
Results may differ from the reference program's by a relative error of at most 0.025.
Values may be sent and summed in bfloat16 or wider, within the bound.
No kernel may reach another device: no remote copies, remote signals or barrier semaphores. Data moves between devices by JAX's collectives and lax.ppermute only.
A program may use at most 896 MiB of HBM per device.

```python
import math
import jax
import jax.numpy as jnp
from jax import lax

D = 2304
HEADS = 36
HEAD_DIM = 64
EXPERTS = 8
FF = 5760
TOPK = 2
BLOCK = 128
SEQ_LEN = 2048
BATCH = 2


def draw_qkv_weight(key, part):
    inner = HEADS * HEAD_DIM
    key_query, key_key, key_value = jax.random.split(key, 3)
    scale = D ** (-0.5)
    query_part = jnp.clip(jax.random.normal(key_query, (D, inner), jnp.float32), -5.0, 5.0) * scale
    key_part = jnp.clip(jax.random.normal(key_key, (D, inner), jnp.float32), -5.0, 5.0) * scale
    value_part = jnp.clip(jax.random.normal(key_value, (D, inner), jnp.float32), -5.0, 5.0) * scale
    return jnp.stack([query_part, key_part, value_part], axis=1).astype(jnp.bfloat16)


def block_levels(rng, extent, cuts, least, largest):
    def one(dim, blocks):
        draws = jax.random.uniform(jax.random.fold_in(jax.random.fold_in(rng, 6), dim), (blocks,), jnp.float32, least / len(cuts), largest / len(cuts))
        return jnp.repeat(jnp.exp(draws), extent[dim] // blocks).reshape((-1,) + (1,) * (len(extent) - dim - 1))

    level = one(*cuts[0])
    for cut in cuts[1:]:
        level = level * one(*cut)
    return level


def picks_of(rng, rows, number_of, top, lift):
    order = jax.random.permutation(jax.random.fold_in(rng, 1), number_of)
    favour = order
    for power in range(3):
        favour = favour * favour // number_of
    favour = favour * lift // number_of
    tickets = jax.random.randint(jax.random.fold_in(rng, 2), (rows, number_of), 0, 4096) + favour
    sure = jax.random.permutation(jax.random.fold_in(rng, 3), rows)[jnp.arange(number_of) % rows]
    tickets = jnp.where(jnp.arange(rows)[:, None] == sure[None, :], 1 << 14, tickets)
    score = tickets * number_of + jnp.arange(number_of)
    return lax.top_k(score.astype(jnp.int32), top)[1].astype(jnp.int32)


def centred(stream_key, dims, scale, most, cuts=(), held_as=jnp.bfloat16):
    result = jax.random.normal(stream_key, dims, jnp.float32) * scale
    if len(cuts) > 0:
        result = block_levels(stream_key, dims, cuts, -0.22, 0.18) * result
    return jnp.clip(result, min=-most, max=most).astype(held_as)


def setup_inputs(seed: int = 0) -> dict:
    arg_keys = jax.random.split(jax.random.key(seed), 12)
    hidden_in = centred(arg_keys[0], (BATCH, SEQ_LEN, D), 1.0, 6.0, ((0, 2), (1, 4)))
    out_cotangent = centred(arg_keys[1], (BATCH, SEQ_LEN, D), 1.0, 6.0, ((0, 2), (1, 4)))
    attn_gain = jnp.clip(1.0 + 0.1 * jax.random.normal(arg_keys[2], (D,), jnp.float32), 0.5, 1.5).astype(jnp.bfloat16)
    qkv_weight = draw_qkv_weight(jax.random.fold_in(arg_keys[11], 71), 0)
    out_weight = centred(arg_keys[4], (HEADS * HEAD_DIM, D), (3.0 * SEQ_LEN ** 0.5 * (HEADS * HEAD_DIM) ** -0.5), 16.0, ((0, 4), (1, 8)))
    ffn_gain = jnp.clip(1.0 + 0.1 * jax.random.normal(arg_keys[5], (D,), jnp.float32), 0.5, 1.5).astype(jnp.bfloat16)
    gate_weight = centred(arg_keys[6], (EXPERTS, D, FF), D ** -0.5, 0.125, ((1, 8), (2, 4)))
    up_weight = centred(arg_keys[7], (EXPERTS, D, FF), D ** -0.5, 0.125, ((1, 8), (2, 4)))
    down_weight = centred(arg_keys[8], (EXPERTS, FF, D), (10.0 * FF ** -0.5), 0.75, ((1, 4), (2, 8)))
    expert_ids = picks_of(arg_keys[9], BATCH * SEQ_LEN, EXPERTS, TOPK, 4096).reshape((BATCH, SEQ_LEN, TOPK))
    route_weights = jnp.clip(0.1 + 0.9 * jax.random.uniform(arg_keys[10], (BATCH, SEQ_LEN, TOPK), jnp.float32) ** block_levels(arg_keys[10], (BATCH, SEQ_LEN, TOPK), ((0, 2), (1, 4)), -0.2, 0.2), 0.1, 1.0)
    return dict(hidden_in=hidden_in, out_cotangent=out_cotangent, attn_gain=attn_gain, qkv_weight=qkv_weight, out_weight=out_weight, ffn_gain=ffn_gain, gate_weight=gate_weight, up_weight=up_weight, down_weight=down_weight, expert_ids=expert_ids, route_weights=route_weights)


EPS = 1e-05
RESIDUAL_SCALE = 1.4 / math.sqrt(40.0)
ROPE_BASE = 10000.0

def rope_tables(positions, head_dim):
    half = head_dim // 2
    freqs = ROPE_BASE ** (-2.0 * jnp.arange(half, dtype=jnp.float32) / head_dim)
    angles = positions.astype(jnp.float32)[:, None] * freqs[None, :]
    return (jnp.cos(angles)[:, None, :], jnp.sin(angles)[:, None, :])

def rotate(values, cosine, sine):
    half = values.shape[-1] // 2
    first, second = (values[..., :half], values[..., half:])
    return jnp.concatenate([first * cosine - second * sine, first * sine + second * cosine], -1)

def rotate_back(grads, cosine, sine):
    half = grads.shape[-1] // 2
    first, second = (grads[..., :half], grads[..., half:])
    return jnp.concatenate([first * cosine + second * sine, second * cosine - first * sine], -1)

def head_forward(query, keys, values, allowed):
    scale = query.shape[-1] ** (-0.5)
    scores = jnp.dot(query, keys.T, preferred_element_type=jnp.float32) * scale
    scores = jnp.where(allowed, scores, -jnp.inf)
    highest = lax.optimization_barrier(jnp.max(scores, -1, keepdims=True))
    log_norm = highest[:, 0] + jnp.log(lax.optimization_barrier(jnp.sum(jnp.exp(scores - highest), -1)))
    probs = jnp.exp(scores - log_norm[:, None]).astype(jnp.bfloat16)
    return (jnp.dot(probs, values, preferred_element_type=jnp.float32).astype(jnp.bfloat16), log_norm)

def head_backward(query, keys, values, output, grad_out, log_norm, allowed):
    scale = query.shape[-1] ** (-0.5)
    scores = jnp.dot(query, keys.T, preferred_element_type=jnp.float32) * scale
    scores = jnp.where(allowed, scores, -jnp.inf)
    probs = jnp.exp(scores - log_norm[:, None])
    grad_values = jnp.dot(probs.astype(jnp.bfloat16).T, grad_out, preferred_element_type=jnp.float32)
    grad_probs = jnp.dot(grad_out, values.T, preferred_element_type=jnp.float32)
    row_dot = lax.optimization_barrier(jnp.sum(grad_out.astype(jnp.float32) * output.astype(jnp.float32), -1, keepdims=True))
    grad_scores = (probs * (grad_probs - row_dot)).astype(jnp.bfloat16)
    grad_query = jnp.dot(grad_scores, keys, preferred_element_type=jnp.float32) * scale
    grad_keys = jnp.dot(grad_scores.T, query, preferred_element_type=jnp.float32) * scale
    return (grad_query, grad_keys, grad_values)

def norm_backward(inputs, inverse, gain, grad_normed):
    scaled = gain.astype(jnp.float32)[None, :] * grad_normed
    gain_grad = lax.optimization_barrier(jnp.sum(grad_normed * inputs * inverse[:, None], 0))
    input_part = inverse[:, None] * scaled - inputs * (inverse ** 3)[:, None] * lax.optimization_barrier(jnp.mean(scaled * inputs, -1, keepdims=True))
    return (gain_grad, input_part)

def dispatch(route_ids, num_experts, block_rows, capacity):
    flat_ids = route_ids.reshape(-1).astype(jnp.int32)
    assigned = flat_ids.shape[0]
    onehot = (flat_ids[:, None] == jnp.arange(num_experts, dtype=jnp.int32)[None, :]).astype(jnp.int32)
    counts = lax.optimization_barrier(jnp.sum(onehot, 0)).astype(jnp.int32)
    padded = ((counts + block_rows - 1) // block_rows * block_rows).astype(jnp.int32)
    ends = jnp.cumsum(padded).astype(jnp.int32)
    starts = (ends - padded).astype(jnp.int32)
    ranks = lax.optimization_barrier(jnp.sum((jnp.cumsum(onehot, 0).astype(jnp.int32) - onehot) * onehot, 1)).astype(jnp.int32)
    target = (lax.optimization_barrier(jnp.sum(onehot * starts[None, :], 1)).astype(jnp.int32) + ranks).astype(jnp.int32)
    source = jnp.full((capacity,), assigned, jnp.int32).at[target].set(jnp.arange(assigned, dtype=jnp.int32))
    block_starts = jnp.arange(capacity // block_rows, dtype=jnp.int32) * block_rows
    block_expert = jnp.minimum(lax.optimization_barrier(jnp.sum((ends[None, :] <= block_starts[:, None]).astype(jnp.int32), 1)), num_experts - 1).astype(jnp.int32)
    return (target, source, block_expert)

def fill_rows(values, source, assigned):
    valid = source < assigned
    picked = values[jnp.minimum(source, assigned - 1)]
    return jnp.where(valid[:, None], picked, jnp.zeros_like(picked))

def experts_forward(buffer, block_expert, gate_all, up_all, down_all, block_rows):
    blocks = buffer.reshape(-1, block_rows, buffer.shape[-1])

    def step(carry, inputs):
        rows, expert = inputs
        gate_val = jnp.dot(rows, gate_all[expert], preferred_element_type=jnp.float32)
        up_val = jnp.dot(rows, up_all[expert], preferred_element_type=jnp.float32)
        inner = (gate_val * jax.nn.sigmoid(gate_val) * up_val).astype(jnp.bfloat16)
        return (carry, jnp.dot(inner, down_all[expert], preferred_element_type=jnp.float32))
    _, outputs = lax.scan(step, jnp.zeros((), jnp.float32), (blocks, block_expert))
    return outputs.reshape(-1, buffer.shape[-1])

def experts_backward(buffer, grad_buffer, block_expert, gate_all, up_all, down_all, block_rows):
    width = buffer.shape[-1]
    blocks = buffer.reshape(-1, block_rows, width)
    grad_blocks = grad_buffer.reshape(-1, block_rows, width)
    start = (jnp.zeros(gate_all.shape, jnp.float32), jnp.zeros(up_all.shape, jnp.float32), jnp.zeros(down_all.shape, jnp.float32))

    def step(carry, inputs):
        rows, grad_rows, expert = inputs
        gate_w, up_w, down_w = (gate_all[expert], up_all[expert], down_all[expert])
        gate_val = jnp.dot(rows, gate_w, preferred_element_type=jnp.float32)
        up_val = jnp.dot(rows, up_w, preferred_element_type=jnp.float32)
        sigma = jax.nn.sigmoid(gate_val)
        active = gate_val * sigma
        inner = (active * up_val).astype(jnp.bfloat16)
        down_part = jnp.dot(inner.T, grad_rows, preferred_element_type=jnp.float32)
        grad_inner = jnp.dot(grad_rows, down_w.T, preferred_element_type=jnp.float32)
        grad_gate = (grad_inner * up_val * sigma * (1.0 + gate_val * (1.0 - sigma))).astype(jnp.bfloat16)
        grad_up = (grad_inner * active).astype(jnp.bfloat16)
        gate_part = jnp.dot(rows.T, grad_gate, preferred_element_type=jnp.float32)
        up_part = jnp.dot(rows.T, grad_up, preferred_element_type=jnp.float32)
        grad_in = jnp.dot(grad_gate, gate_w.T, preferred_element_type=jnp.float32) + jnp.dot(grad_up, up_w.T, preferred_element_type=jnp.float32)
        carry = (carry[0].at[expert].add(gate_part), carry[1].at[expert].add(up_part), carry[2].at[expert].add(down_part))
        return (carry, grad_in)
    totals, grad_rows_all = lax.scan(step, start, (blocks, grad_blocks, block_expert))
    return (totals, grad_rows_all.reshape(-1, width))

def reference(hidden_in, out_cotangent, attn_gain, qkv_weight, out_weight, ffn_gain, gate_weight, up_weight, down_weight, expert_ids, route_weights):
    inner_width = HEADS * HEAD_DIM
    qkv_matrix = qkv_weight.reshape(D, 3 * inner_width)
    positions = jnp.arange(SEQ_LEN, dtype=jnp.int32)
    cosine, sine = rope_tables(positions, HEAD_DIM)
    allowed = positions[None, :] <= positions[:, None]
    capacity = TOPK * SEQ_LEN + EXPERTS * BLOCK
    assigned = TOPK * SEQ_LEN

    def one_sequence(totals, inputs):
        tokens, cotangent, route_ids, route_scale = inputs
        tokens = tokens.astype(jnp.float32)
        inverse1 = lax.rsqrt(lax.optimization_barrier(jnp.mean(tokens * tokens, -1)) + EPS)
        normed1 = (tokens * inverse1[:, None] * attn_gain.astype(jnp.float32)[None, :]).astype(jnp.bfloat16)
        projected = jnp.dot(normed1, qkv_matrix, preferred_element_type=jnp.float32).reshape(SEQ_LEN, 3, HEADS, HEAD_DIM)
        query_rot = rotate(projected[:, 0], cosine, sine).astype(jnp.bfloat16).transpose(1, 0, 2)
        key_rot = rotate(projected[:, 1], cosine, sine).astype(jnp.bfloat16).transpose(1, 0, 2)
        value_low = projected[:, 2].astype(jnp.bfloat16).transpose(1, 0, 2)
        attended, log_norm = lax.map(lambda items: head_forward(items[0], items[1], items[2], allowed), (query_rot, key_rot, value_low))
        att_flat = attended.transpose(1, 0, 2).reshape(SEQ_LEN, inner_width)
        resid = tokens + RESIDUAL_SCALE * jnp.dot(att_flat, out_weight, preferred_element_type=jnp.float32)
        inverse2 = lax.rsqrt(lax.optimization_barrier(jnp.mean(resid * resid, -1)) + EPS)
        normed2 = (resid * inverse2[:, None] * ffn_gain.astype(jnp.float32)[None, :]).astype(jnp.bfloat16)
        target, source, block_expert = dispatch(route_ids, EXPERTS, BLOCK, capacity)
        token_rows = jnp.repeat(normed2, TOPK, axis=0)
        buffer = fill_rows(token_rows, source, assigned)
        expert_out = experts_forward(buffer, block_expert, gate_weight, up_weight, down_weight, BLOCK)
        picked = expert_out[target].reshape(SEQ_LEN, TOPK, D)
        mixed = lax.optimization_barrier(jnp.sum(route_scale[:, :, None] * picked, 1))
        block_out = (resid + RESIDUAL_SCALE * mixed).astype(jnp.bfloat16)
        grad_top = cotangent.astype(jnp.float32)
        grad_mix = RESIDUAL_SCALE * grad_top
        grad_assign = (route_scale[:, :, None] * grad_mix[:, None, :]).reshape(assigned, D).astype(jnp.bfloat16)
        grad_buffer = fill_rows(grad_assign, source, assigned)
        expert_totals, grad_rows = experts_backward(buffer, grad_buffer, block_expert, gate_weight, up_weight, down_weight, BLOCK)
        grad_n2 = lax.optimization_barrier(jnp.sum(grad_rows[target].reshape(SEQ_LEN, TOPK, D), 1))
        ffn_part, resid_part = norm_backward(resid, inverse2, ffn_gain, grad_n2)
        grad_resid = grad_top + resid_part
        grad_att = (RESIDUAL_SCALE * grad_resid).astype(jnp.bfloat16)
        out_part = jnp.dot(att_flat.T, grad_att, preferred_element_type=jnp.float32)
        grad_attended = jnp.dot(grad_att, out_weight.T, preferred_element_type=jnp.float32).astype(jnp.bfloat16)
        grad_heads = grad_attended.reshape(SEQ_LEN, HEADS, HEAD_DIM).transpose(1, 0, 2)
        grad_query, grad_keys, grad_values = lax.map(lambda items: head_backward(items[0], items[1], items[2], items[3], items[4], items[5], allowed), (query_rot, key_rot, value_low, attended, grad_heads, log_norm))
        grad_query = rotate_back(grad_query.transpose(1, 0, 2), cosine, sine)
        grad_keys = rotate_back(grad_keys.transpose(1, 0, 2), cosine, sine)
        grad_values = grad_values.transpose(1, 0, 2)
        grad_proj = jnp.stack([grad_query, grad_keys, grad_values], 1).reshape(SEQ_LEN, 3 * inner_width).astype(jnp.bfloat16)
        qkv_part = jnp.dot(normed1.T, grad_proj, preferred_element_type=jnp.float32).reshape(D, 3, inner_width)
        grad_n1 = jnp.dot(grad_proj, qkv_matrix.T, preferred_element_type=jnp.float32)
        attn_part, input_part = norm_backward(tokens, inverse1, attn_gain, grad_n1)
        input_grad = grad_resid + input_part
        totals = (totals[0] + attn_part, totals[1] + qkv_part, totals[2] + out_part, totals[3] + ffn_part, totals[4] + expert_totals[0], totals[5] + expert_totals[1], totals[6] + expert_totals[2])
        return (totals, (block_out, input_grad))
    start = (jnp.zeros((D,), jnp.float32), jnp.zeros((D, 3, inner_width), jnp.float32), jnp.zeros((inner_width, D), jnp.float32), jnp.zeros((D,), jnp.float32), jnp.zeros((EXPERTS, D, FF), jnp.float32), jnp.zeros((EXPERTS, D, FF), jnp.float32), jnp.zeros((EXPERTS, FF, D), jnp.float32))
    totals, outputs = lax.scan(one_sequence, start, (hidden_in, out_cotangent, expert_ids, route_weights))
    return (outputs[0], outputs[1], totals[0], totals[1], totals[2], totals[3], totals[4], totals[5], totals[6])
```

```python
import math

import jax
import jax.numpy as jnp
from jax import lax
from jax.sharding import PartitionSpec as P

HEAD_DIM = 64
EPS = 1e-05
RESIDUAL_SCALE = 1.4 / math.sqrt(40.0)
ROPE_BASE = 10000.0
GROUP = ("fsdp", "ctx")
BF16 = jnp.bfloat16
F32 = jnp.float32


def dot(a, b, ca, cb):
    return lax.dot_general(a, b, (((ca,), (cb,)), ((), ())), preferred_element_type=F32)


def rope_tables(positions, head_dim):
    half = head_dim // 2
    freqs = ROPE_BASE ** (-2.0 * jnp.arange(half, dtype=F32) / head_dim)
    angles = positions.astype(F32)[:, None] * freqs[None, :]
    return (jnp.cos(angles)[:, None, :], jnp.sin(angles)[:, None, :])


def rotate(values, cosine, sine):
    half = values.shape[-1] // 2
    first, second = (values[..., :half], values[..., half:])
    return jnp.concatenate([first * cosine - second * sine, first * sine + second * cosine], -1)


def rotate_back(grads, cosine, sine):
    half = grads.shape[-1] // 2
    first, second = (grads[..., :half], grads[..., half:])
    return jnp.concatenate([first * cosine + second * sine, second * cosine - first * sine], -1)


def head_forward(query, keys, values, allowed):
    scale = query.shape[-1] ** (-0.5)
    scores = jnp.dot(query, keys.T, preferred_element_type=F32) * scale
    scores = jnp.where(allowed, scores, -jnp.inf)
    highest = jnp.max(scores, -1, keepdims=True)
    log_norm = highest[:, 0] + jnp.log(jnp.sum(jnp.exp(scores - highest), -1))
    probs = jnp.exp(scores - log_norm[:, None]).astype(BF16)
    return (jnp.dot(probs, values, preferred_element_type=F32).astype(BF16), log_norm)


def head_backward(query, keys, values, output, grad_out, log_norm, allowed):
    scale = query.shape[-1] ** (-0.5)
    scores = jnp.dot(query, keys.T, preferred_element_type=F32) * scale
    scores = jnp.where(allowed, scores, -jnp.inf)
    probs = jnp.exp(scores - log_norm[:, None])
    grad_values = jnp.dot(probs.astype(BF16).T, grad_out, preferred_element_type=F32)
    grad_probs = jnp.dot(grad_out, values.T, preferred_element_type=F32)
    row_dot = jnp.sum(grad_out.astype(F32) * output.astype(F32), -1, keepdims=True)
    grad_scores = (probs * (grad_probs - row_dot)).astype(BF16)
    grad_query = jnp.dot(grad_scores, keys, preferred_element_type=F32) * scale
    grad_keys = jnp.dot(grad_scores.T, query, preferred_element_type=F32) * scale
    return (grad_query, grad_keys, grad_values)


def norm_backward(inputs, inverse, gain, grad_normed):
    scaled = gain.astype(F32)[None, :] * grad_normed
    gain_grad = jnp.sum(grad_normed * inputs * inverse[:, None], 0)
    input_part = inverse[:, None] * scaled - inputs * (inverse**3)[:, None] * jnp.mean(
        scaled * inputs, -1, keepdims=True
    )
    return (gain_grad, input_part)


def make_body(experts, ep_axes, rest):
    def fetch(weight):
        mine = lax.all_to_all(weight, ep_axes, 0, 0, tiled=True)
        if rest is not None:
            mine = lax.all_gather(mine, rest, axis=1, tiled=True)
        return mine.reshape(-1, mine.shape[-1])

    def give_back(grad, shard):
        blocks = grad.reshape(experts, -1, grad.shape[-1])
        if rest is not None:
            blocks = lax.psum_scatter(blocks, rest, scatter_dimension=1, tiled=True)
        return lax.all_to_all(blocks, ep_axes, 0, 0, tiled=True)

    def body(
        hidden_in,
        out_cotangent,
        attn_gain,
        qkv_weight,
        out_weight,
        ffn_gain,
        gate_weight,
        up_weight,
        down_weight,
        expert_ids,
        route_weights,
    ):
        tokens = hidden_in[0].astype(F32)
        tok_count, width = tokens.shape
        shard = qkv_weight.shape[0]
        positions = lax.axis_index("ctx") * tok_count + jnp.arange(tok_count, dtype=jnp.int32)
        cosine, sine = rope_tables(positions, HEAD_DIM)
        gains = lax.all_gather(jnp.stack([attn_gain, ffn_gain], 0), GROUP, axis=1, tiled=True)
        gain_one, gain_two = gains[0], gains[1]
        qkv_full = lax.all_gather(qkv_weight, GROUP, axis=0, tiled=True)
        out_full = lax.all_gather(out_weight, GROUP, axis=1, tiled=True)
        local_width = qkv_full.shape[2]
        heads_here = local_width // HEAD_DIM

        down_t = fetch(down_weight.swapaxes(1, 2))
        gate_w = fetch(gate_weight)
        up_w = fetch(up_weight)
        cot_all = lax.all_gather(out_cotangent[0], ep_axes, axis=0, tiled=True)
        hit = expert_ids[0][None] == jnp.arange(experts, dtype=jnp.int32)[:, None, None]
        share = jnp.sum(jnp.where(hit, route_weights[0][None], 0.0), -1)
        share = lax.all_to_all(share, ep_axes, 0, 0, tiled=True).reshape(-1)
        grad_y = (share[:, None] * (RESIDUAL_SCALE * cot_all.astype(F32))).astype(BF16)
        grad_inner = dot(grad_y, down_t, 1, 0)

        inverse1 = lax.rsqrt(jnp.mean(tokens * tokens, -1) + EPS)
        normed1 = (tokens * inverse1[:, None] * gain_one.astype(F32)[None, :]).astype(BF16)
        qkv_mat = qkv_full.reshape(width, 3 * local_width)
        projected = dot(normed1, qkv_mat, 1, 0).reshape(tok_count, 3, heads_here, HEAD_DIM)
        query_rot = rotate(projected[:, 0], cosine, sine).astype(BF16)
        key_flat = rotate(projected[:, 1], cosine, sine).astype(BF16).reshape(tok_count, local_width)
        value_flat = projected[:, 2].astype(BF16).reshape(tok_count, local_width)
        kv_all = lax.all_gather(
            jnp.concatenate([key_flat, value_flat], 1), "ctx", axis=0, tiled=True
        )
        seq_total = kv_all.shape[0]
        allowed = jnp.arange(seq_total, dtype=jnp.int32)[None, :] <= positions[:, None]
        query_heads = query_rot.transpose(1, 0, 2)
        kv_heads = kv_all.reshape(seq_total, 2, heads_here, HEAD_DIM).transpose(1, 2, 0, 3)
        key_heads, value_heads = kv_heads[0], kv_heads[1]
        attended, log_norm = lax.map(
            lambda items: head_forward(items[0], items[1], items[2], allowed),
            (query_heads, key_heads, value_heads),
        )
        att_flat = attended.transpose(1, 0, 2).reshape(tok_count, local_width)
        attn_total = lax.psum(dot(att_flat, out_full, 1, 0).astype(BF16), "tp").astype(F32)
        resid = tokens + RESIDUAL_SCALE * attn_total
        inverse2 = lax.rsqrt(jnp.mean(resid * resid, -1) + EPS)
        normed2 = (resid * inverse2[:, None] * gain_two.astype(F32)[None, :]).astype(BF16)

        normed_all = lax.all_gather(normed2, ep_axes, axis=0, tiled=True)
        gate_val = dot(normed_all, gate_w, 1, 0)
        up_val = dot(normed_all, up_w, 1, 0)
        sigma = jax.nn.sigmoid(gate_val)
        active = gate_val * sigma
        inner = (active * up_val).astype(BF16)
        grad_gate = (grad_inner * up_val * sigma * (1.0 + gate_val * (1.0 - sigma))).astype(BF16)
        grad_up = (grad_inner * active).astype(BF16)
        grad_in = (dot(grad_gate, gate_w, 1, 1) + dot(grad_up, up_w, 1, 1)).astype(BF16)
        grad_n2 = lax.psum_scatter(grad_in, ep_axes, scatter_dimension=0, tiled=True)
        grad_n2 = lax.psum(grad_n2, "tp").astype(F32)
        expert_y = (share[:, None] * dot(inner, down_t, 1, 1)).astype(BF16)
        mixed = lax.psum_scatter(expert_y, ep_axes, scatter_dimension=0, tiled=True)
        mixed = lax.psum(mixed, "tp").astype(F32)
        block_out = (resid + RESIDUAL_SCALE * mixed).astype(BF16)

        gate_weight_grad = give_back(dot(normed_all, grad_gate, 0, 0).astype(BF16), shard)
        up_weight_grad = give_back(dot(normed_all, grad_up, 0, 0).astype(BF16), shard)
        down_weight_grad = give_back(dot(grad_y, inner, 0, 0).astype(BF16), shard)

        grad_top = out_cotangent[0].astype(F32)
        ffn_part, resid_part = norm_backward(resid, inverse2, gain_two, grad_n2)
        grad_resid = grad_top + resid_part
        grad_att = (RESIDUAL_SCALE * grad_resid).astype(BF16)
        out_part = dot(att_flat, grad_att, 0, 0)
        grad_attended = dot(grad_att, out_full, 1, 1).astype(BF16)
        grad_heads = grad_attended.reshape(tok_count, heads_here, HEAD_DIM).transpose(1, 0, 2)
        grad_query, grad_keys, grad_values = lax.map(
            lambda items: head_backward(*items, allowed),
            (query_heads, key_heads, value_heads, attended, grad_heads, log_norm),
        )
        kv_grad = jnp.stack([grad_keys, grad_values], 0).astype(BF16)
        kv_grad = kv_grad.transpose(2, 0, 1, 3).reshape(seq_total, 2 * local_width)
        kv_here = lax.psum_scatter(kv_grad, "ctx", scatter_dimension=0, tiled=True).astype(F32)
        kv_here = kv_here.reshape(tok_count, 2, heads_here, HEAD_DIM)
        query_back = rotate_back(grad_query.transpose(1, 0, 2), cosine, sine)
        key_back = rotate_back(kv_here[:, 0], cosine, sine)
        grad_proj = (
            jnp.stack([query_back, key_back, kv_here[:, 1]], 1)
            .reshape(tok_count, 3 * local_width)
            .astype(BF16)
        )
        qkv_part = dot(normed1, grad_proj, 0, 0).reshape(width, 3, local_width)
        grad_n1 = lax.psum(dot(grad_proj, qkv_mat, 1, 1).astype(BF16), "tp").astype(F32)
        attn_part, input_part = norm_backward(tokens, inverse1, gain_one, grad_n1)
        input_grad = grad_resid + input_part
        gain_grads = lax.psum_scatter(
            jnp.stack([attn_part, ffn_part], 0).astype(BF16),
            GROUP,
            scatter_dimension=1,
            tiled=True,
        ).astype(F32)
        qkv_weight_grad = lax.psum_scatter(
            qkv_part.astype(BF16), GROUP, scatter_dimension=0, tiled=True
        )
        out_weight_grad = lax.psum_scatter(
            out_part.astype(BF16), GROUP, scatter_dimension=1, tiled=True
        )
        return (
            block_out[None],
            input_grad[None],
            gain_grads[0],
            qkv_weight_grad.astype(F32),
            out_weight_grad.astype(F32),
            gain_grads[1],
            gate_weight_grad.astype(F32),
            up_weight_grad.astype(F32),
            down_weight_grad.astype(F32).swapaxes(1, 2),
        )

    return body


def solution(mesh):
    experts = 8
    if mesh.shape["fsdp"] * mesh.shape["ctx"] == experts:
        ep_axes, rest = GROUP, None
    else:
        assert mesh.shape["fsdp"] == experts
        ep_axes, rest = ("fsdp",), "ctx"
    in_specs = (
        P("fsdp", "ctx", None),
        P("fsdp", "ctx", None),
        P(GROUP),
        P(GROUP, None, "tp"),
        P("tp", GROUP),
        P(GROUP),
        P(None, GROUP, "tp"),
        P(None, GROUP, "tp"),
        P(None, "tp", GROUP),
        P("fsdp", "ctx", None),
        P("fsdp", "ctx", None),
    )
    out_specs = (
        P("fsdp", "ctx", None),
        P("fsdp", "ctx", None),
        P(GROUP),
        P(GROUP, None, "tp"),
        P("tp", GROUP),
        P(GROUP),
        P(None, GROUP, "tp"),
        P(None, GROUP, "tp"),
        P(None, "tp", GROUP),
    )
    body = make_body(experts, ep_axes, rest)
    return jax.shard_map(body, mesh=mesh, in_specs=in_specs, out_specs=out_specs, check_vma=False)
```

```python
import functools
import math

import jax
import jax.numpy as jnp
from jax import lax
from jax.experimental import pallas as pl
from jax.experimental.pallas import tpu as pltpu
from jax.sharding import PartitionSpec as P

HEAD_DIM = 64
EPS = 1e-05
RESIDUAL_SCALE = 1.4 / math.sqrt(40.0)
ROPE_BASE = 10000.0
GROUP = ("fsdp", "ctx")
BF16 = jnp.bfloat16
F32 = jnp.float32


def mm(a, b, ca, cb):
    return lax.dot_general(a, b, (((ca,), (cb,)), ((), ())), preferred_element_type=F32)


def swap_halves(x):
    lane = lax.broadcasted_iota(jnp.int32, x.shape, 1)
    return jnp.where(lane % 64 < 32, pltpu.roll(x, 96, 1), pltpu.roll(x, 32, 1))

def rope_kernel(proj_ref, cos_ref, sin_ref, q_ref, kv_ref):
    width = q_ref.shape[1]
    cosine, sine = cos_ref[...], sin_ref[...]
    parts = []
    for j in range(2 * width // 128):
        x = proj_ref[:, 128 * j : 128 * (j + 1)]
        parts.append((x * cosine + swap_halves(x) * sine).astype(BF16))
    both = jnp.concatenate(parts, 1)
    q_ref[...] = both[:, :width]
    kv_ref[:, :width] = both[:, width:]
    kv_ref[:, width:] = proj_ref[:, 2 * width :].astype(BF16)

def rope(proj, cosine, sine, width, tile=256):
    rows = proj.shape[0]
    return pl.pallas_call(
        rope_kernel,
        grid=(rows // tile,),
        in_specs=[
            pl.BlockSpec((tile, 3 * width), lambda i: (i, 0)),
            pl.BlockSpec((tile, 128), lambda i: (i, 0)),
            pl.BlockSpec((tile, 128), lambda i: (i, 0)),
        ],
        out_specs=[
            pl.BlockSpec((tile, width), lambda i: (i, 0)),
            pl.BlockSpec((tile, 2 * width), lambda i: (i, 0)),
        ],
        out_shape=[
            jax.ShapeDtypeStruct((rows, width), BF16),
            jax.ShapeDtypeStruct((rows, 2 * width), BF16),
        ],
        cost_estimate=pl.CostEstimate(flops=8 * rows * 2 * width, bytes_accessed=rows * 3 * width * 6, transcendentals=0),
        name="rope",
    )(proj, cosine, sine)

def rope_back_kernel(dq_ref, dkv_ref, cos_ref, sin_ref, out_ref):
    width = dq_ref.shape[1]
    cosine, sine = cos_ref[...], sin_ref[...]
    both = jnp.concatenate([dq_ref[...], dkv_ref[:, :width].astype(F32)], 1)
    for j in range(2 * width // 128):
        x = both[:, 128 * j : 128 * (j + 1)]
        out_ref[:, 128 * j : 128 * (j + 1)] = (x * cosine - swap_halves(x) * sine).astype(BF16)
    out_ref[:, 2 * width :] = dkv_ref[:, width:]

def rope_back(dq, dkv, cosine, sine, tile=256):
    rows, width = dq.shape
    return pl.pallas_call(
        rope_back_kernel,
        grid=(rows // tile,),
        in_specs=[
            pl.BlockSpec((tile, width), lambda i: (i, 0)),
            pl.BlockSpec((tile, 2 * width), lambda i: (i, 0)),
            pl.BlockSpec((tile, 128), lambda i: (i, 0)),
            pl.BlockSpec((tile, 128), lambda i: (i, 0)),
        ],
        out_specs=pl.BlockSpec((tile, 3 * width), lambda i: (i, 0)),
        out_shape=jax.ShapeDtypeStruct((rows, 3 * width), BF16),
        cost_estimate=pl.CostEstimate(flops=8 * rows * 2 * width, bytes_accessed=rows * 3 * width * 5, transcendentals=0),
        name="rope_back",
    )(dq, dkv, cosine, sine)

SCALE = HEAD_DIM ** -0.5
NEG = -1e30

def attn_fwd_kernel(c_ref, q_ref, kv_ref, o_ref, lse_ref, *, kb):
    rows, width = q_ref.shape
    heads = width // HEAD_DIM
    steps = rows // kb
    c = c_ref[0]
    for h in range(heads):
        lanes = slice(h * HEAD_DIM, (h + 1) * HEAD_DIM)
        vlanes = slice(width + h * HEAD_DIM, width + (h + 1) * HEAD_DIM)
        q = q_ref[:, lanes] * SCALE

        def block(j, carry, masked, q=q, lanes=lanes, vlanes=vlanes):
            top, total, acc = carry
            at = pl.ds(pl.multiple_of(j * kb, kb), kb)
            s = mm(kv_ref[at, lanes], q, 1, 1)
            if masked is not None:
                key = lax.broadcasted_iota(jnp.int32, s.shape, 0) + masked * kb
                s = jnp.where(key <= lax.broadcasted_iota(jnp.int32, s.shape, 1), s, NEG)
            new_top = jnp.maximum(top, jnp.max(s, 0, keepdims=True))
            p = jnp.exp(s - new_top)
            alpha = jnp.exp(top - new_top)
            total = total * alpha + jnp.sum(p, 0, keepdims=True)
            acc = acc * alpha + mm(kv_ref[at, vlanes], p.astype(BF16), 0, 0)
            return new_top, total, acc

        carry = (jnp.full((1, rows), NEG, F32), jnp.zeros((1, rows), F32), jnp.zeros((HEAD_DIM, rows), F32))
        carry = lax.fori_loop(0, c * steps, lambda j, x: block(j, x, None), carry)
        for i in range(steps):
            carry = block(c * steps + i, carry, i)
        top, total, acc = carry
        o_ref[:, lanes] = (acc / total).T.astype(BF16)
        lse_ref[h : h + 1, :] = top + jnp.log(total)

def attn_fwd(c, q, kv, kb=512):
    rows, width = q.shape
    heads = width // HEAD_DIM
    n = rows * kv.shape[0] * heads
    return pl.pallas_call(
        functools.partial(attn_fwd_kernel, kb=kb),
        in_specs=[pl.BlockSpec(memory_space=pltpu.SMEM), pl.BlockSpec(memory_space=pltpu.VMEM), pl.BlockSpec(memory_space=pltpu.VMEM)],
        out_specs=[pl.BlockSpec(memory_space=pltpu.VMEM), pl.BlockSpec(memory_space=pltpu.VMEM)],
        out_shape=[jax.ShapeDtypeStruct((rows, width), BF16), jax.ShapeDtypeStruct((heads, rows), F32)],
        cost_estimate=pl.CostEstimate(flops=4 * n * HEAD_DIM * 4, bytes_accessed=2 * (q.size * 2 + kv.size), transcendentals=n),
        name="attn_fwd",
    )(c, q, kv)

def attn_bwd_kernel(c_ref, q_ref, kv_ref, o_ref, do_ref, lse_ref, dq_ref, dkv_ref, *, kb):
    rows, width = q_ref.shape
    heads = width // HEAD_DIM
    steps = rows // kb
    c = c_ref[0]
    total_steps = kv_ref.shape[0] // kb

    def clear(j, x):
        at = pl.ds(pl.multiple_of(j * kb, kb), kb)
        dkv_ref[at, :] = jnp.zeros((kb, 2 * width), BF16)
        return x

    lax.fori_loop((c + 1) * steps, total_steps, clear, 0)
    for h in range(heads):
        lanes = slice(h * HEAD_DIM, (h + 1) * HEAD_DIM)
        vlanes = slice(width + h * HEAD_DIM, width + (h + 1) * HEAD_DIM)
        q = q_ref[:, lanes] * SCALE
        do = do_ref[:, lanes]
        lse = lse_ref[h : h + 1, :]
        prod = do.astype(F32) * o_ref[:, lanes].astype(F32)
        delta = jnp.sum(prod.T, 0, keepdims=True)

        def block(j, dq, masked, q=q, do=do, lse=lse, delta=delta, lanes=lanes, vlanes=vlanes):
            at = pl.ds(pl.multiple_of(j * kb, kb), kb)
            k = kv_ref[at, lanes]
            s = mm(k, q, 1, 1)
            if masked is not None:
                key = lax.broadcasted_iota(jnp.int32, s.shape, 0) + masked * kb
                s = jnp.where(key <= lax.broadcasted_iota(jnp.int32, s.shape, 1), s, NEG)
            p = jnp.exp(s - lse)
            dp = mm(kv_ref[at, vlanes], do, 1, 1)
            ds = (p * (dp - delta)).astype(BF16)
            dkv_ref[at, vlanes] = mm(p.astype(BF16), do, 1, 0).astype(BF16)
            dkv_ref[at, lanes] = mm(ds, q, 1, 0).astype(BF16)
            return dq + mm(k, ds, 0, 0)

        dq = jnp.zeros((HEAD_DIM, rows), F32)
        dq = lax.fori_loop(0, c * steps, lambda j, x: block(j, x, None), dq)
        for i in range(steps):
            dq = block(c * steps + i, dq, i)
        dq_ref[:, lanes] = dq.T * SCALE

def attn_bwd(c, q, kv, o, do, lse, kb=512):
    rows, width = q.shape
    heads = width // HEAD_DIM
    n = rows * kv.shape[0] * heads
    vm = pl.BlockSpec(memory_space=pltpu.VMEM)
    return pl.pallas_call(
        functools.partial(attn_bwd_kernel, kb=kb),
        in_specs=[pl.BlockSpec(memory_space=pltpu.SMEM)] + [vm] * 5,
        out_specs=[vm, vm],
        out_shape=[jax.ShapeDtypeStruct((rows, width), F32), jax.ShapeDtypeStruct(kv.shape, BF16)],
        cost_estimate=pl.CostEstimate(flops=10 * n * HEAD_DIM * 4, bytes_accessed=2 * (q.size * 5 + 2 * kv.size), transcendentals=n),
        name="attn_bwd",
    )(c, q, kv, o, do, lse)


def expert_kernel(x_ref, gi_ref, gate_hbm, up_hbm, inner_ref, gg_ref, gu_ref, gn_ref, gate_v, up_v, sems):
    gate_copy = pltpu.make_async_copy(gate_hbm, gate_v, sems.at[0])
    up_copy = pltpu.make_async_copy(up_hbm, up_v, sems.at[1])
    first = pl.program_id(0) == 0

    @pl.when(first)
    def _():
        gate_copy.start()
        up_copy.start()
        gate_copy.wait()

    x = x_ref[...]
    gate = mm(x, gate_v[...], 1, 0)

    @pl.when(first)
    def _():
        up_copy.wait()

    up = mm(x, up_v[...], 1, 0)
    gi = gi_ref[...].astype(F32)
    sigma = jax.nn.sigmoid(gate)
    active = gate * sigma
    inner_ref[...] = (active * up).astype(BF16)
    gg = (gi * up * sigma * (1.0 + gate * (1.0 - sigma))).astype(BF16)
    gu = (gi * active).astype(BF16)
    gg_ref[...] = gg
    gu_ref[...] = gu
    gn_ref[...] = (mm(gg, gate_v[...], 1, 1) + mm(gu, up_v[...], 1, 1)).astype(BF16)

def expert_core(x, gi, gate_w, up_w, tile=256):
    rows, width = x.shape
    hidden = gate_w.shape[1]
    row = lambda n: pl.BlockSpec((tile, n), lambda i: (i, 0))
    anyspec = pl.BlockSpec(memory_space=pl.ANY)
    return pl.pallas_call(
        expert_kernel,
        grid=(rows // tile,),
        in_specs=[row(width), row(hidden), anyspec, anyspec],
        out_specs=[row(hidden), row(hidden), row(hidden), row(width)],
        out_shape=[jax.ShapeDtypeStruct((rows, hidden), BF16)] * 3 + [jax.ShapeDtypeStruct((rows, width), BF16)],
        scratch_shapes=[pltpu.VMEM((width, hidden), BF16), pltpu.VMEM((width, hidden), BF16), pltpu.SemaphoreType.DMA((2,))],
        compiler_params=pltpu.CompilerParams(vmem_limit_bytes=60 << 20),
        cost_estimate=pl.CostEstimate(flops=8 * rows * width * hidden, bytes_accessed=4 * width * hidden + rows * (4 * width + 8 * hidden), transcendentals=rows * hidden),
        name="expert_core",
    )(x, gi, gate_w, up_w)


def norm_backward(inputs, inverse, gain, grad_normed):
    scaled = gain.astype(F32)[None, :] * grad_normed
    gain_grad = jnp.sum(grad_normed * inputs * inverse[:, None], 0)
    input_part = inverse[:, None] * scaled - inputs * (inverse**3)[:, None] * jnp.mean(
        scaled * inputs, -1, keepdims=True
    )
    return (gain_grad, input_part)


class Direct:
    def __init__(self, axes):
        self.axes = axes

    def order(self, share):
        return share.reshape(-1)

    def gather(self, x):
        whole = lax.all_gather(x, self.axes, axis=0, tiled=True)
        size = whole.shape[0] // 4
        return [whole[i * size : (i + 1) * size] for i in range(4)]

    def scatter(self, groups):
        whole = jnp.concatenate(groups, 0)
        return lax.psum_scatter(whole, self.axes, scatter_dimension=0, tiled=True)


class Paired:
    def move(self, x, bits):
        return lax.ppermute(x, GROUP, [(j, j ^ bits) for j in range(8)])

    def order(self, share):
        me = lax.axis_index(GROUP)
        count = share.shape[1] // 2
        mine = share[jnp.bitwise_xor(me, jnp.arange(8, dtype=jnp.int32))].reshape(16, count)
        blocks = (0, 1, 2, 3, 8, 5, 10, 7, 12, 13, 14, 15, 9, 4, 11, 6)
        return jnp.concatenate([mine[b] for b in blocks], 0)

    def pair(self, a, b):
        both = a if b is None else jnp.concatenate([a, b], 0)
        return jnp.concatenate([both, self.move(both, 1)], 0)

    def gather(self, x):
        half = x.shape[0] // 2
        lo, hi = x[:half], x[half:]
        x_lo, y_hi = self.move(lo, 4), self.move(hi, 2)
        d_lo, d_hi = self.move(x_lo, 2), self.move(y_hi, 4)
        x_hi, y_lo = self.move(hi, 4), self.move(lo, 2)
        return [
            self.pair(x, None),
            self.pair(x_lo, y_hi),
            self.pair(d_lo, d_hi),
            self.pair(x_hi, y_lo),
        ]

    def scatter(self, groups):
        half = groups[0].shape[0] // 4

        def merge(group):
            both = group[: 2 * half] + self.move(group[2 * half :], 1)
            return both[:half], both[half:]

        d_lo, d_hi = merge(groups[2])
        x_hi, y_lo = merge(groups[3])
        y_lo = y_lo + self.move(d_lo, 4)
        x_hi = x_hi + self.move(d_hi, 2)
        x_lo, y_hi = merge(groups[1])
        lo, hi = merge(groups[0])
        lo = lo + self.move(x_lo, 4) + self.move(y_lo, 2)
        hi = hi + self.move(x_hi, 4) + self.move(y_hi, 2)
        return jnp.concatenate([lo, hi], 0)


def make_body(experts, ep_axes, rest, tokens_by):
    def fetch(weight):
        mine = lax.all_to_all(weight, ep_axes, 0, 0, tiled=True)
        if rest is not None:
            mine = lax.all_gather(mine, rest, axis=1, tiled=True)
        return mine.reshape(-1, mine.shape[-1])

    def give_back(grad):
        blocks = grad.reshape(experts, -1, grad.shape[-1])
        if rest is not None:
            blocks = lax.psum_scatter(blocks, rest, scatter_dimension=1, tiled=True)
        return lax.all_to_all(blocks, ep_axes, 0, 0, tiled=True)

    def body(
        hidden_in,
        out_cotangent,
        attn_gain,
        qkv_weight,
        out_weight,
        ffn_gain,
        gate_weight,
        up_weight,
        down_weight,
        expert_ids,
        route_weights,
    ):
        tokens = hidden_in[0].astype(F32)
        tok_count, width = tokens.shape
        shard = qkv_weight.shape[0]
        local_width = qkv_weight.shape[2]
        ctx = lax.axis_index("ctx")

        qkv_mat = lax.all_gather(
            qkv_weight.reshape(shard, 3 * local_width), GROUP, axis=0, tiled=True
        )
        gains = lax.all_gather(jnp.stack([attn_gain, ffn_gain], 0), GROUP, axis=1, tiled=True)
        hit = expert_ids[0][None] == jnp.arange(experts, dtype=jnp.int32)[:, None, None]
        share = jnp.sum(jnp.where(hit, route_weights[0][None], 0.0), -1)
        share = lax.all_to_all(share, ep_axes, 0, 0, tiled=True)
        gate_w = fetch(gate_weight)
        qkv_mat, gains, share = lax.optimization_barrier((qkv_mat, gains, share))
        share = tokens_by.order(share)
        out_full = lax.all_gather(out_weight, GROUP, axis=1, tiled=True)
        gain_one, gain_two = gains[0], gains[1]

        half = HEAD_DIM // 2
        positions = ctx * tok_count + jnp.arange(tok_count, dtype=jnp.int32)
        freqs = ROPE_BASE ** (-2.0 * jnp.arange(half, dtype=F32) / HEAD_DIM)
        angles = positions.astype(F32)[:, None] * freqs[None, :]
        cosine, sine = jnp.cos(angles), jnp.sin(angles)
        cosine = jnp.concatenate([cosine] * 4, 1)
        sine = jnp.concatenate([-sine, sine] * 2, 1)

        inverse1 = lax.rsqrt(jnp.mean(tokens * tokens, -1) + EPS)
        normed1 = (tokens * inverse1[:, None] * gain_one.astype(F32)[None, :]).astype(BF16)
        query, kv_here = rope(mm(normed1, qkv_mat, 1, 0), cosine, sine, local_width)
        kv_all = lax.all_gather(kv_here, "ctx", axis=0, tiled=True)
        kv_all, gate_w = lax.optimization_barrier((kv_all, gate_w))
        up_w = fetch(up_weight)
        cot_groups = tokens_by.gather(out_cotangent[0])
        block = ctx.astype(jnp.int32).reshape(1)
        attended, log_norm = attn_fwd(block, query, kv_all)
        attn_total = lax.psum(mm(attended, out_full, 1, 0).astype(BF16), "tp")
        attn_total, up_w = lax.optimization_barrier((attn_total, up_w))
        resid = tokens + RESIDUAL_SCALE * attn_total.astype(F32)
        inverse2 = lax.rsqrt(jnp.mean(resid * resid, -1) + EPS)
        normed2 = (resid * inverse2[:, None] * gain_two.astype(F32)[None, :]).astype(BF16)

        down_t = fetch(down_weight.swapaxes(1, 2))
        cot_all = jnp.concatenate(cot_groups, 0)
        grad_y = (share[:, None] * (RESIDUAL_SCALE * cot_all.astype(F32))).astype(BF16)
        grad_inner = mm(grad_y, down_t, 1, 0).astype(BF16)

        normed_groups = tokens_by.gather(normed2)
        size = normed_groups[0].shape[0]
        results = [
            expert_core(x, grad_inner[i * size : (i + 1) * size], gate_w, up_w)
            for i, x in enumerate(normed_groups)
        ]
        grad_n2 = lax.psum(tokens_by.scatter([r[3] for r in results]), "tp")

        normed_all = jnp.concatenate(normed_groups, 0)
        inner, grad_gate, grad_up = (
            jnp.concatenate([r[k] for r in results], 0) for k in range(3)
        )
        gate_grad = mm(normed_all, grad_gate, 0, 0).astype(BF16)
        up_grad = mm(normed_all, grad_up, 0, 0).astype(BF16)
        grad_n2, gate_grad, up_grad = lax.optimization_barrier((grad_n2, gate_grad, up_grad))
        gate_weight_grad = give_back(gate_grad)
        up_weight_grad = give_back(up_grad)

        grad_n2 = grad_n2.astype(F32)
        grad_top = out_cotangent[0].astype(F32)
        ffn_part, resid_part = norm_backward(resid, inverse2, gain_two, grad_n2)
        grad_resid = grad_top + resid_part
        grad_att = (RESIDUAL_SCALE * grad_resid).astype(BF16)
        grad_attended = mm(grad_att, out_full, 1, 1).astype(BF16)
        grad_query, kv_grad = attn_bwd(block, query, kv_all, attended, grad_attended, log_norm)
        kv_grad_here = lax.psum_scatter(kv_grad, "ctx", scatter_dimension=0, tiled=True)
        down_grad = mm(grad_y, inner, 0, 0).astype(BF16)
        kv_grad_here, down_grad = lax.optimization_barrier((kv_grad_here, down_grad))
        down_weight_grad = give_back(down_grad)
        grad_proj = rope_back(grad_query, kv_grad_here, cosine, sine)
        grad_n1 = lax.psum(mm(grad_proj, qkv_mat, 1, 1).astype(BF16), "tp")

        expert_y = (share[:, None] * mm(inner, down_t, 1, 1)).astype(BF16)
        mixed = tokens_by.scatter([expert_y[i * size : (i + 1) * size] for i in range(4)])
        grad_n1, mixed = lax.optimization_barrier((grad_n1, mixed))
        mixed = lax.psum(mixed, "tp").astype(F32)
        block_out = (resid + RESIDUAL_SCALE * mixed).astype(BF16)

        out_part = mm(attended, grad_att, 0, 0)
        qkv_part = mm(normed1, grad_proj, 0, 0)
        attn_part, input_part = norm_backward(tokens, inverse1, gain_one, grad_n1.astype(F32))
        input_grad = grad_resid + input_part
        gain_grads = lax.psum_scatter(
            jnp.stack([attn_part, ffn_part], 0).astype(BF16),
            GROUP,
            scatter_dimension=1,
            tiled=True,
        ).astype(F32)
        qkv_weight_grad = lax.psum_scatter(
            qkv_part.astype(BF16), GROUP, scatter_dimension=0, tiled=True
        )
        out_weight_grad = lax.psum_scatter(
            out_part.astype(BF16), GROUP, scatter_dimension=1, tiled=True
        )
        return (
            block_out[None],
            input_grad[None],
            gain_grads[0],
            qkv_weight_grad.astype(F32).reshape(shard, 3, local_width),
            out_weight_grad.astype(F32),
            gain_grads[1],
            gate_weight_grad.astype(F32),
            up_weight_grad.astype(F32),
            down_weight_grad.astype(F32).swapaxes(1, 2),
        )

    return body


def solution(mesh):
    experts = 8
    sizes = (mesh.shape["fsdp"], mesh.shape["ctx"])
    if sizes == (2, 4):
        ep_axes, rest, tokens_by = GROUP, None, Paired()
    elif sizes[0] * sizes[1] == experts:
        ep_axes, rest, tokens_by = GROUP, None, Direct(GROUP)
    else:
        assert sizes[0] == experts
        ep_axes, rest, tokens_by = ("fsdp",), "ctx", Direct(("fsdp",))
    in_specs = (
        P("fsdp", "ctx", None),
        P("fsdp", "ctx", None),
        P(GROUP),
        P(GROUP, None, "tp"),
        P("tp", GROUP),
        P(GROUP),
        P(None, GROUP, "tp"),
        P(None, GROUP, "tp"),
        P(None, "tp", GROUP),
        P("fsdp", "ctx", None),
        P("fsdp", "ctx", None),
    )
    out_specs = (
        P("fsdp", "ctx", None),
        P("fsdp", "ctx", None),
        P(GROUP),
        P(GROUP, None, "tp"),
        P("tp", GROUP),
        P(GROUP),
        P(None, GROUP, "tp"),
        P(None, GROUP, "tp"),
        P(None, "tp", GROUP),
    )
    body = make_body(experts, ep_axes, rest, tokens_by)
    return jax.shard_map(body, mesh=mesh, in_specs=in_specs, out_specs=out_specs, check_vma=False)
```

```python
import functools
import math

import jax
import jax.numpy as jnp
from jax import lax
from jax.experimental import pallas as pl
from jax.experimental.pallas import tpu as pltpu
from jax.sharding import PartitionSpec as P

HEAD_DIM = 64
EPS = 1e-05
RESIDUAL_SCALE = 1.4 / math.sqrt(40.0)
ROPE_BASE = 10000.0
GROUP = ("fsdp", "ctx")
BF16 = jnp.bfloat16
F32 = jnp.float32


def mm(a, b, ca, cb):
    return lax.dot_general(a, b, (((ca,), (cb,)), ((), ())), preferred_element_type=F32)


def swap_halves(x):
    lane = lax.broadcasted_iota(jnp.int32, x.shape, 1)
    return jnp.where(lane % 64 < 32, pltpu.roll(x, 96, 1), pltpu.roll(x, 32, 1))

def rope_kernel(proj_ref, cos_ref, sin_ref, q_ref, kv_ref):
    width = q_ref.shape[1]
    cosine, sine = cos_ref[...], sin_ref[...]
    parts = []
    for j in range(2 * width // 128):
        x = proj_ref[:, 128 * j : 128 * (j + 1)]
        parts.append((x * cosine + swap_halves(x) * sine).astype(BF16))
    both = jnp.concatenate(parts, 1)
    q_ref[...] = both[:, :width]
    kv_ref[:, :width] = both[:, width:]
    kv_ref[:, width:] = proj_ref[:, 2 * width :].astype(BF16)

def rope(proj, cosine, sine, width, tile=256):
    rows = proj.shape[0]
    return pl.pallas_call(
        rope_kernel,
        grid=(rows // tile,),
        in_specs=[
            pl.BlockSpec((tile, 3 * width), lambda i: (i, 0)),
            pl.BlockSpec((tile, 128), lambda i: (i, 0)),
            pl.BlockSpec((tile, 128), lambda i: (i, 0)),
        ],
        out_specs=[
            pl.BlockSpec((tile, width), lambda i: (i, 0)),
            pl.BlockSpec((tile, 2 * width), lambda i: (i, 0)),
        ],
        out_shape=[
            jax.ShapeDtypeStruct((rows, width), BF16),
            jax.ShapeDtypeStruct((rows, 2 * width), BF16),
        ],
        cost_estimate=pl.CostEstimate(flops=8 * rows * 2 * width, bytes_accessed=rows * 3 * width * 6, transcendentals=0),
        name="rope",
    )(proj, cosine, sine)

def rope_back_kernel(dq_ref, dkv_ref, cos_ref, sin_ref, out_ref):
    width = dq_ref.shape[1]
    cosine, sine = cos_ref[...], sin_ref[...]
    both = jnp.concatenate([dq_ref[...], dkv_ref[:, :width].astype(F32)], 1)
    for j in range(2 * width // 128):
        x = both[:, 128 * j : 128 * (j + 1)]
        out_ref[:, 128 * j : 128 * (j + 1)] = (x * cosine - swap_halves(x) * sine).astype(BF16)
    out_ref[:, 2 * width :] = dkv_ref[:, width:]

def rope_back(dq, dkv, cosine, sine, tile=256):
    rows, width = dq.shape
    return pl.pallas_call(
        rope_back_kernel,
        grid=(rows // tile,),
        in_specs=[
            pl.BlockSpec((tile, width), lambda i: (i, 0)),
            pl.BlockSpec((tile, 2 * width), lambda i: (i, 0)),
            pl.BlockSpec((tile, 128), lambda i: (i, 0)),
            pl.BlockSpec((tile, 128), lambda i: (i, 0)),
        ],
        out_specs=pl.BlockSpec((tile, 3 * width), lambda i: (i, 0)),
        out_shape=jax.ShapeDtypeStruct((rows, 3 * width), BF16),
        cost_estimate=pl.CostEstimate(flops=8 * rows * 2 * width, bytes_accessed=rows * 3 * width * 5, transcendentals=0),
        name="rope_back",
    )(dq, dkv, cosine, sine)

SCALE = HEAD_DIM ** -0.5
NEG = -1e30

def attn_fwd_kernel(c_ref, q_ref, kv_ref, o_ref, lse_ref, *, kb):
    rows, width = q_ref.shape
    heads = width // HEAD_DIM
    steps = rows // kb
    c = c_ref[0]
    for h in range(heads):
        lanes = slice(h * HEAD_DIM, (h + 1) * HEAD_DIM)
        vlanes = slice(width + h * HEAD_DIM, width + (h + 1) * HEAD_DIM)
        q = q_ref[:, lanes] * SCALE

        def block(j, carry, masked, q=q, lanes=lanes, vlanes=vlanes):
            top, total, acc = carry
            at = pl.ds(pl.multiple_of(j * kb, kb), kb)
            s = mm(kv_ref[at, lanes], q, 1, 1)
            if masked is not None:
                key = lax.broadcasted_iota(jnp.int32, s.shape, 0) + masked * kb
                s = jnp.where(key <= lax.broadcasted_iota(jnp.int32, s.shape, 1), s, NEG)
            new_top = jnp.maximum(top, jnp.max(s, 0, keepdims=True))
            p = jnp.exp(s - new_top)
            alpha = jnp.exp(top - new_top)
            total = total * alpha + jnp.sum(p, 0, keepdims=True)
            acc = acc * alpha + mm(kv_ref[at, vlanes], p.astype(BF16), 0, 0)
            return new_top, total, acc

        carry = (jnp.full((1, rows), NEG, F32), jnp.zeros((1, rows), F32), jnp.zeros((HEAD_DIM, rows), F32))
        carry = lax.fori_loop(0, c * steps, lambda j, x: block(j, x, None), carry)
        for i in range(steps):
            carry = block(c * steps + i, carry, i)
        top, total, acc = carry
        o_ref[:, lanes] = (acc / total).T.astype(BF16)
        lse_ref[h : h + 1, :] = top + jnp.log(total)

def attn_fwd(c, q, kv, kb=512):
    rows, width = q.shape
    heads = width // HEAD_DIM
    n = rows * kv.shape[0] * heads
    return pl.pallas_call(
        functools.partial(attn_fwd_kernel, kb=kb),
        in_specs=[pl.BlockSpec(memory_space=pltpu.SMEM), pl.BlockSpec(memory_space=pltpu.VMEM), pl.BlockSpec(memory_space=pltpu.VMEM)],
        out_specs=[pl.BlockSpec(memory_space=pltpu.VMEM), pl.BlockSpec(memory_space=pltpu.VMEM)],
        out_shape=[jax.ShapeDtypeStruct((rows, width), BF16), jax.ShapeDtypeStruct((heads, rows), F32)],
        cost_estimate=pl.CostEstimate(flops=4 * n * HEAD_DIM * 4, bytes_accessed=2 * (q.size * 2 + kv.size), transcendentals=n),
        name="attn_fwd",
    )(c, q, kv)

def attn_bwd_kernel(c_ref, q_ref, kv_ref, o_ref, do_ref, lse_ref, dq_ref, dkv_ref, *, kb):
    rows, width = q_ref.shape
    heads = width // HEAD_DIM
    steps = rows // kb
    c = c_ref[0]
    total_steps = kv_ref.shape[0] // kb

    def clear(j, x):
        at = pl.ds(pl.multiple_of(j * kb, kb), kb)
        dkv_ref[at, :] = jnp.zeros((kb, 2 * width), BF16)
        return x

    lax.fori_loop((c + 1) * steps, total_steps, clear, 0)
    for h in range(heads):
        lanes = slice(h * HEAD_DIM, (h + 1) * HEAD_DIM)
        vlanes = slice(width + h * HEAD_DIM, width + (h + 1) * HEAD_DIM)
        q = q_ref[:, lanes] * SCALE
        do = do_ref[:, lanes]
        lse = lse_ref[h : h + 1, :]
        prod = do.astype(F32) * o_ref[:, lanes].astype(F32)
        delta = jnp.sum(prod.T, 0, keepdims=True)

        def block(j, dq, masked, q=q, do=do, lse=lse, delta=delta, lanes=lanes, vlanes=vlanes):
            at = pl.ds(pl.multiple_of(j * kb, kb), kb)
            k = kv_ref[at, lanes]
            s = mm(k, q, 1, 1)
            if masked is not None:
                key = lax.broadcasted_iota(jnp.int32, s.shape, 0) + masked * kb
                s = jnp.where(key <= lax.broadcasted_iota(jnp.int32, s.shape, 1), s, NEG)
            p = jnp.exp(s - lse)
            dp = mm(kv_ref[at, vlanes], do, 1, 1)
            ds = (p * (dp - delta)).astype(BF16)
            dkv_ref[at, vlanes] = mm(p.astype(BF16), do, 1, 0).astype(BF16)
            dkv_ref[at, lanes] = mm(ds, q, 1, 0).astype(BF16)
            return dq + mm(k, ds, 0, 0)

        dq = jnp.zeros((HEAD_DIM, rows), F32)
        dq = lax.fori_loop(0, c * steps, lambda j, x: block(j, x, None), dq)
        for i in range(steps):
            dq = block(c * steps + i, dq, i)
        dq_ref[:, lanes] = dq.T * SCALE

def attn_bwd(c, q, kv, o, do, lse, kb=512):
    rows, width = q.shape
    heads = width // HEAD_DIM
    n = rows * kv.shape[0] * heads
    vm = pl.BlockSpec(memory_space=pltpu.VMEM)
    return pl.pallas_call(
        functools.partial(attn_bwd_kernel, kb=kb),
        in_specs=[pl.BlockSpec(memory_space=pltpu.SMEM)] + [vm] * 5,
        out_specs=[vm, vm],
        out_shape=[jax.ShapeDtypeStruct((rows, width), F32), jax.ShapeDtypeStruct(kv.shape, BF16)],
        cost_estimate=pl.CostEstimate(flops=10 * n * HEAD_DIM * 4, bytes_accessed=2 * (q.size * 5 + 2 * kv.size), transcendentals=n),
        name="attn_bwd",
    )(c, q, kv, o, do, lse)


def expert_kernel(*refs):
    x_ref, gi_ref, gate_hbm, up_hbm = refs[:4]
    inner_ref, gg_ref, gu_ref, x_out_ref, gn_ref, gate_v, up_v, sems = refs[-8:]
    gate_copy = pltpu.make_async_copy(gate_hbm, gate_v, sems.at[0])
    up_copy = pltpu.make_async_copy(up_hbm, up_v, sems.at[1])
    first = pl.program_id(0) == 0

    @pl.when(first)
    def _():
        gate_copy.start()
        up_copy.start()
        gate_copy.wait()

    x = x_ref[...]
    x_out_ref[...] = x
    gate = mm(x, gate_v[...], 1, 0)

    @pl.when(first)
    def _():
        up_copy.wait()

    up = mm(x, up_v[...], 1, 0)
    gi = gi_ref[...].astype(F32)
    sigma = jax.nn.sigmoid(gate)
    active = gate * sigma
    inner_ref[...] = (active * up).astype(BF16)
    gg = (gi * up * sigma * (1.0 + gate * (1.0 - sigma))).astype(BF16)
    gu = (gi * active).astype(BF16)
    gg_ref[...] = gg
    gu_ref[...] = gu
    gn_ref[...] = (mm(gg, gate_v[...], 1, 1) + mm(gu, up_v[...], 1, 1)).astype(BF16)


def expert_core(x, gi, gate_w, up_w, blocks, earlier):
    rows, width = x.shape
    hidden = gate_w.shape[1]
    tile = rows // len(blocks)
    total = gi.shape[0]

    def place(i):
        at = jnp.int32(blocks[0])
        for k, b in enumerate(blocks[1:]):
            at = jnp.where(i == k + 1, jnp.int32(b), at)
        return (at, 0)

    group = pl.BlockSpec((tile, width), lambda i: (i, 0))
    hbm = pl.BlockSpec(memory_space=pl.ANY)
    in_place = pl.BlockSpec((tile, hidden), place)
    return pl.pallas_call(
        expert_kernel,
        grid=(len(blocks),),
        in_specs=[group, in_place, hbm, hbm] + [hbm] * len(earlier),
        out_specs=[in_place, in_place, in_place, pl.BlockSpec((tile, width), place), group],
        out_shape=[jax.ShapeDtypeStruct((total, hidden), BF16)] * 3
        + [jax.ShapeDtypeStruct((total, width), BF16), jax.ShapeDtypeStruct((rows, width), BF16)],
        input_output_aliases={4 + k: k for k in range(len(earlier))},
        scratch_shapes=[
            pltpu.VMEM((width, hidden), BF16),
            pltpu.VMEM((width, hidden), BF16),
            pltpu.SemaphoreType.DMA((2,)),
        ],
        compiler_params=pltpu.CompilerParams(vmem_limit_bytes=60 << 20),
        cost_estimate=pl.CostEstimate(
            flops=8 * rows * width * hidden,
            bytes_accessed=4 * width * hidden + rows * (6 * width + 8 * hidden),
            transcendentals=rows * hidden,
        ),
        name="expert_core",
    )(x, gi, gate_w, up_w, *earlier)


def norm_backward(inputs, inverse, gain, grad_normed):
    scaled = gain[None, :] * grad_normed
    gain_grad = jnp.sum(grad_normed * inputs * inverse[:, None], 0)
    input_part = inverse[:, None] * scaled - inputs * (inverse**3)[:, None] * jnp.mean(
        scaled * inputs, -1, keepdims=True
    )
    return (gain_grad, input_part)


def together(*values):
    return lax.optimization_barrier(values)


def after(value, *earlier):
    return lax.optimization_barrier((value, *earlier))[0]


class Direct:
    def __init__(self, axes):
        self.axes = axes

    def order(self, share):
        return share.reshape(-1)

    def spread(self, x):
        whole = lax.all_gather(x, self.axes, axis=0, tiled=True)
        return (lambda *values: values), (lambda: whole)

    def exchange(self, x, core):
        whole = lax.all_gather(x, self.axes, axis=0, tiled=True)
        size = whole.shape[0] // 4
        sums, kept = [], ()
        for i in range(4):
            *kept, part = core(
                whole[i * size : (i + 1) * size], tuple(range(4 * i, 4 * i + 4)), kept
            )
            sums.append(part)
        return kept, (lambda work: (self.scatter(jnp.concatenate(sums, 0), ())[0], work()))

    def scatter(self, whole, work):
        done = [w() for w in work]
        return lax.psum_scatter(whole, self.axes, scatter_dimension=0, tiled=True), *done


class Paired:
    near = (0, 4, 2, 6, 1, 5, 3, 7)

    def move(self, x, bits):
        return lax.ppermute(x, GROUP, [(j, j ^ bits) for j in range(8)])

    def order(self, share):
        me = lax.axis_index(GROUP)
        return share[jnp.bitwise_xor(me, jnp.array(self.near, jnp.int32))].reshape(-1)

    def pair(self, a, b):
        both = a if b is None else jnp.concatenate([a, b], 0)
        return jnp.concatenate([both, self.move(both, 1)], 0)

    def merge(self, group):
        half = group.shape[0] // 4
        both = group[: 2 * half] + self.move(group[2 * half :], 1)
        return both[:half], both[half:]

    def exchange(self, x, core):
        half = x.shape[0] // 2
        lo, hi = x[:half], x[half:]
        x_lo, y_hi = self.move(lo, 4), self.move(hi, 2)
        *kept, out0 = core(self.pair(x, None), (0, 1, 8, 9), ())
        out0, x_lo, y_hi = together(out0, x_lo, y_hi)
        d_lo, d_hi = self.move(x_lo, 2), self.move(y_hi, 4)
        x_hi, y_lo = self.move(after(hi, out0), 4), self.move(after(lo, out0), 2)
        *kept, out1 = core(self.pair(x_lo, y_hi), (2, 5, 10, 13), kept)
        out1, d_lo, d_hi = together(out1, d_lo, d_hi)
        third = self.pair(d_lo, d_hi)
        third, px_lo, py_hi, p_lo, p_hi = together(third, *self.merge(out1), *self.merge(out0))
        px_lo, py_hi = self.move(px_lo, 4), self.move(py_hi, 2)
        *kept, out2 = core(third, (6, 7, 14, 15), kept)
        out2, x_hi, y_lo, px_lo, py_hi = together(out2, x_hi, y_lo, px_lo, py_hi)
        fourth = self.pair(x_hi, y_lo)
        fourth, pd_lo, pd_hi = together(fourth, *self.merge(out2))
        pd_lo, pd_hi = self.move(pd_lo, 4), self.move(pd_hi, 2)
        *kept, out3 = core(fourth, (3, 4, 11, 12), kept)
        out3, pd_lo, pd_hi = together(out3, pd_lo, pd_hi)

        def finish(work):
            px_hi, py_lo = self.merge(out3)
            px_hi, py_lo = together(px_hi + pd_hi, py_lo + pd_lo)
            done = work(px_hi)
            px_hi, py_lo = self.move(px_hi, 4), self.move(py_lo, 2)
            px_hi, py_lo, done = together(px_hi, py_lo, done)
            return jnp.concatenate([p_lo + px_lo + py_lo, p_hi + px_hi + py_hi], 0), done

        return kept, finish

    def spread(self, x):
        rows = x.shape[0] // 4
        depth = lax.axis_index("tp")
        mine = lax.dynamic_slice_in_dim(x, depth * rows, rows, 0)
        here = jnp.stack([mine, self.move(mine, 4), self.move(mine, 2), self.move(mine, 6)], 0)
        below, above = [here], [here]

        def step(*values):
            if len(below) == 1:
                values = together(here, *values)
                below[0] = above[0] = values[0]
                values = values[1:]
            else:
                values = together(below[-1], above[-1], *values)
                below[-1], above[-1] = values[:2]
                values = values[2:]
            if len(below) < 4:
                below.append(lax.ppermute(below[-1], "tp", [(0, 1), (1, 2), (2, 3)]))
                above.append(lax.ppermute(above[-1], "tp", [(3, 2), (2, 1), (1, 0)]))
            return values

        def finish():
            whole = jnp.zeros((here.shape[0], 4, *here.shape[1:]), here.dtype)
            for i in (3, 2, 1):
                whole = lax.dynamic_update_slice_in_dim(whole, below[i][:, None], depth - i, 1)
            for i in (3, 2, 1):
                whole = lax.dynamic_update_slice_in_dim(whole, above[i][:, None], depth + i, 1)
            whole = lax.dynamic_update_slice_in_dim(whole, here[:, None], depth, 1)
            whole = whole.reshape(-1, x.shape[1])
            return jnp.concatenate([whole, self.move(whole, 1)], 0)

        return step, finish

    def scatter(self, whole, work):
        size = whole.shape[0] // 8
        half = size // 2
        both = whole[: 4 * size] + self.move(whole[4 * size :], 1)
        part = lambda i: together(both[i * half : (i + 1) * half])[0]
        lo, hi, x_lo, x_hi, y_lo, y_hi, d_lo, d_hi = (part(i) for i in range(8))
        done0 = work[0](d_lo)
        d_lo, d_hi = self.move(d_lo, 4), self.move(d_hi, 2)
        d_lo, d_hi, done0 = together(d_lo, d_hi, done0)
        x_hi, y_lo = together(x_hi + d_hi, y_lo + d_lo)
        done1 = work[1](x_hi)
        x_hi, y_lo = self.move(x_hi, 4), self.move(y_lo, 2)
        x_lo, y_hi = self.move(x_lo, 4), self.move(y_hi, 2)
        x_lo, y_hi, x_hi, y_lo, done1 = together(x_lo, y_hi, x_hi, y_lo, done1)
        return jnp.concatenate([lo + x_lo + y_lo, hi + x_hi + y_hi], 0), done0, done1


def make_body(experts, ep_axes, rest, tokens_by):
    def fetch(weight):
        mine = lax.all_to_all(weight, ep_axes, 0, 0, tiled=True)
        if rest is not None:
            mine = lax.all_gather(mine, rest, axis=1, tiled=True)
        return mine.reshape(-1, mine.shape[-1])

    def give_back(grad):
        blocks = grad.reshape(experts, -1, grad.shape[-1])
        if rest is not None:
            blocks = lax.psum_scatter(blocks, rest, scatter_dimension=1, tiled=True)
        return lax.all_to_all(blocks, ep_axes, 0, 0, tiled=True)

    def body(
        hidden_in,
        out_cotangent,
        attn_gain,
        qkv_weight,
        out_weight,
        ffn_gain,
        gate_weight,
        up_weight,
        down_weight,
        expert_ids,
        route_weights,
    ):
        tokens = hidden_in[0].astype(F32)
        tok_count, width = tokens.shape
        shard = qkv_weight.shape[0]
        local_width = qkv_weight.shape[2]
        ctx = lax.axis_index("ctx")

        qkv_mat = lax.all_gather(
            qkv_weight.reshape(shard, 3 * local_width), GROUP, axis=0, tiled=True
        )
        cot_step, cot_finish = tokens_by.spread(out_cotangent[0])
        small = jnp.concatenate(
            [
                attn_gain.astype(F32),
                ffn_gain.astype(F32),
                expert_ids[0].astype(F32).reshape(-1),
                route_weights[0].reshape(-1),
            ]
        )
        small = jnp.broadcast_to(small, (lax.axis_size(GROUP), 1, small.shape[0]))
        small = lax.all_to_all(small, GROUP, 0, 0, tiled=True)[:, 0]
        small, down_in = cot_step(small, down_weight.swapaxes(1, 2))
        down_t = fetch(down_in)
        (small,) = cot_step(small)
        qkv_mat, small, down_t = together(qkv_mat, small, down_t)
        gain_one = small[:, :shard].reshape(-1)
        gain_two = small[:, shard : 2 * shard].reshape(-1)
        routes = small[:, 2 * shard :].reshape(-1, 2, tok_count, expert_ids.shape[2])
        if rest is not None:
            routes = routes.reshape(experts, -1, *routes.shape[1:])
            routes = lax.dynamic_index_in_dim(routes, lax.axis_index(rest), 1, keepdims=False)
        mine = lax.axis_index(ep_axes).astype(F32)
        share = jnp.sum(jnp.where(routes[:, 0] == mine, routes[:, 1], 0.0), -1)
        share = tokens_by.order(share)

        half = HEAD_DIM // 2
        positions = ctx * tok_count + jnp.arange(tok_count, dtype=jnp.int32)
        freqs = ROPE_BASE ** (-2.0 * jnp.arange(half, dtype=F32) / HEAD_DIM)
        angles = positions.astype(F32)[:, None] * freqs[None, :]
        cosine, sine = jnp.cos(angles), jnp.sin(angles)
        cosine = jnp.concatenate([cosine] * 4, 1)
        sine = jnp.concatenate([-sine, sine] * 2, 1)
        inverse1 = lax.rsqrt(jnp.mean(tokens * tokens, -1) + EPS)
        normed1 = (tokens * inverse1[:, None] * gain_one[None, :]).astype(BF16)
        query, kv_here = rope(mm(normed1, qkv_mat, 1, 0), cosine, sine, local_width)

        kv_all = lax.all_gather(kv_here, "ctx", axis=0, tiled=True)
        gate_w = fetch(after(gate_weight, qkv_mat))
        (held,) = cot_step(kv_here)
        cot_step(held)
        cot_all = cot_finish()
        kv_all, gate_w, cot_all = together(kv_all, gate_w, cot_all)

        out_full = lax.all_gather(after(out_weight, kv_all), GROUP, axis=1, tiled=True)
        block = ctx.astype(jnp.int32).reshape(1)
        attended, log_norm = attn_fwd(block, query, kv_all)
        attended, out_full, up_in = together(attended, out_full, up_weight)
        attn_total = lax.psum(mm(attended, out_full, 1, 0).astype(BF16), "tp")
        up_w = fetch(up_in)
        grad_y = (share[:, None] * (RESIDUAL_SCALE * cot_all.astype(F32))).astype(BF16)
        (grad_y,) = together(after(grad_y, attended))
        grad_inner = mm(grad_y, down_t, 1, 0).astype(BF16)
        attn_total, grad_inner, up_w = together(attn_total, grad_inner, up_w)
        resid = tokens + RESIDUAL_SCALE * attn_total.astype(F32)
        inverse2 = lax.rsqrt(jnp.mean(resid * resid, -1) + EPS)
        normed2 = (resid * inverse2[:, None] * gain_two[None, :]).astype(BF16)

        kept, finish = tokens_by.exchange(
            normed2,
            lambda x, blocks, earlier: expert_core(
                x, grad_inner, gate_w, up_w, blocks, tuple(earlier)
            ),
        )
        inner, grad_gate, grad_up, normed_all = kept
        grad_n2, expert_y = finish(
            lambda hold=None: (share[:, None] * mm(after(inner, hold), down_t, 1, 1)).astype(BF16)
        )

        grad_n2 = lax.psum(grad_n2, "tp")
        mixed, down_grad, gate_grad = tokens_by.scatter(
            expert_y,
            (
                lambda hold=None: mm(after(grad_y, hold), inner, 0, 0).astype(BF16),
                lambda hold=None: mm(after(normed_all, hold), grad_gate, 0, 0).astype(BF16),
            ),
        )
        grad_n2, mixed, down_grad, gate_grad = together(grad_n2, mixed, down_grad, gate_grad)

        down_weight_grad = give_back(down_grad)
        grad_top = out_cotangent[0].astype(F32)
        ffn_part, resid_part = norm_backward(resid, inverse2, gain_two, grad_n2.astype(F32))
        grad_resid = grad_top + resid_part
        grad_att = (RESIDUAL_SCALE * grad_resid).astype(BF16)
        grad_attended = mm(grad_att, out_full, 1, 1).astype(BF16)
        out_part = mm(attended, grad_att, 0, 0).astype(BF16)
        grad_attended, out_part = together(grad_attended, out_part)
        out_weight_grad = lax.psum_scatter(out_part, GROUP, scatter_dimension=1, tiled=True)
        grad_query, kv_grad = attn_bwd(block, query, kv_all, attended, grad_attended, log_norm)
        kv_grad, out_weight_grad = together(kv_grad, out_weight_grad)
        kv_grad_here = lax.psum_scatter(kv_grad, "ctx", scatter_dimension=0, tiled=True)
        up_grad = mm(after(normed_all, kv_grad), grad_up, 0, 0).astype(BF16)
        kv_grad_here, up_grad, down_weight_grad = together(kv_grad_here, up_grad, down_weight_grad)

        grad_proj = rope_back(grad_query, kv_grad_here, cosine, sine)
        part_n1 = mm(grad_proj, qkv_mat, 1, 1).astype(BF16)
        grad_n1 = lax.psum(part_n1, "tp")
        gate_weight_grad = give_back(after(gate_grad, kv_grad_here))
        qkv_part = mm(after(normed1, part_n1), grad_proj, 0, 0).astype(BF16)
        grad_n1, qkv_part, gate_weight_grad = together(grad_n1, qkv_part, gate_weight_grad)

        up_weight_grad = give_back(after(up_grad, grad_n1))
        qkv_weight_grad = lax.psum_scatter(qkv_part, GROUP, scatter_dimension=0, tiled=True)
        mixed = lax.psum(after(mixed, grad_n1), "tp").astype(F32)
        block_out = (resid + RESIDUAL_SCALE * mixed).astype(BF16)
        attn_part, input_part = norm_backward(tokens, inverse1, gain_one, grad_n1.astype(F32))
        input_grad = grad_resid + input_part
        parts = jnp.stack([attn_part, ffn_part], 0).reshape(2, -1, shard).swapaxes(0, 1)
        gain_grads = jnp.sum(lax.all_to_all(parts, GROUP, 0, 0, tiled=True), 0)
        return (
            block_out[None],
            input_grad[None],
            gain_grads[0],
            qkv_weight_grad.astype(F32).reshape(shard, 3, local_width),
            out_weight_grad.astype(F32),
            gain_grads[1],
            gate_weight_grad.astype(F32),
            up_weight_grad.astype(F32),
            down_weight_grad.astype(F32).swapaxes(1, 2),
        )

    return body


def solution(mesh):
    experts = 8
    sizes = (mesh.shape["fsdp"], mesh.shape["ctx"])
    if sizes == (2, 4) and mesh.shape["tp"] == 4:
        ep_axes, rest, tokens_by = GROUP, None, Paired()
    elif sizes[0] * sizes[1] == experts:
        ep_axes, rest, tokens_by = GROUP, None, Direct(GROUP)
    else:
        assert sizes[0] == experts
        ep_axes, rest, tokens_by = ("fsdp",), "ctx", Direct(("fsdp",))
    in_specs = (
        P("fsdp", "ctx", None),
        P("fsdp", "ctx", None),
        P(GROUP),
        P(GROUP, None, "tp"),
        P("tp", GROUP),
        P(GROUP),
        P(None, GROUP, "tp"),
        P(None, GROUP, "tp"),
        P(None, "tp", GROUP),
        P("fsdp", "ctx", None),
        P("fsdp", "ctx", None),
    )
    out_specs = (
        P("fsdp", "ctx", None),
        P("fsdp", "ctx", None),
        P(GROUP),
        P(GROUP, None, "tp"),
        P("tp", GROUP),
        P(GROUP),
        P(None, GROUP, "tp"),
        P(None, GROUP, "tp"),
        P(None, "tp", GROUP),
    )
    body = make_body(experts, ep_axes, rest, tokens_by)
    return jax.shard_map(body, mesh=mesh, in_specs=in_specs, out_specs=out_specs, check_vma=False)
```

```python
import functools
import math

import jax
import jax.numpy as jnp
from jax import lax
from jax.experimental import pallas as pl
from jax.experimental.pallas import tpu as pltpu
from jax.sharding import PartitionSpec as P

HEAD_DIM = 64
EPS = 1e-05
RESIDUAL_SCALE = 1.4 / math.sqrt(40.0)
ROPE_BASE = 10000.0
GROUP = ("fsdp", "ctx")
BF16 = jnp.bfloat16
F32 = jnp.float32


def mm(a, b, ca, cb):
    return lax.dot_general(a, b, (((ca,), (cb,)), ((), ())), preferred_element_type=F32)


def swap_halves(x):
    lane = lax.broadcasted_iota(jnp.int32, x.shape, 1)
    return jnp.where(lane % 64 < 32, pltpu.roll(x, 96, 1), pltpu.roll(x, 32, 1))

def rope_kernel(proj_ref, cos_ref, sin_ref, q_ref, kv_ref):
    width = q_ref.shape[1]
    cosine, sine = cos_ref[...], sin_ref[...]
    parts = []
    for j in range(2 * width // 128):
        x = proj_ref[:, 128 * j : 128 * (j + 1)]
        parts.append((x * cosine + swap_halves(x) * sine).astype(BF16))
    both = jnp.concatenate(parts, 1)
    q_ref[...] = both[:, :width]
    kv_ref[:, :width] = both[:, width:]
    kv_ref[:, width:] = proj_ref[:, 2 * width :].astype(BF16)

def rope(proj, cosine, sine, width, tile=256):
    rows = proj.shape[0]
    return pl.pallas_call(
        rope_kernel,
        grid=(rows // tile,),
        in_specs=[
            pl.BlockSpec((tile, 3 * width), lambda i: (i, 0)),
            pl.BlockSpec((tile, 128), lambda i: (i, 0)),
            pl.BlockSpec((tile, 128), lambda i: (i, 0)),
        ],
        out_specs=[
            pl.BlockSpec((tile, width), lambda i: (i, 0)),
            pl.BlockSpec((tile, 2 * width), lambda i: (i, 0)),
        ],
        out_shape=[
            jax.ShapeDtypeStruct((rows, width), BF16),
            jax.ShapeDtypeStruct((rows, 2 * width), BF16),
        ],
        cost_estimate=pl.CostEstimate(flops=8 * rows * 2 * width, bytes_accessed=rows * 3 * width * 6, transcendentals=0),
        name="rope",
    )(proj, cosine, sine)

def rope_back_kernel(dq_ref, dkv_ref, cos_ref, sin_ref, out_ref):
    width = dq_ref.shape[1]
    cosine, sine = cos_ref[...], sin_ref[...]
    both = jnp.concatenate([dq_ref[...], dkv_ref[:, :width].astype(F32)], 1)
    for j in range(2 * width // 128):
        x = both[:, 128 * j : 128 * (j + 1)]
        out_ref[:, 128 * j : 128 * (j + 1)] = (x * cosine - swap_halves(x) * sine).astype(BF16)
    out_ref[:, 2 * width :] = dkv_ref[:, width:]

def rope_back(dq, dkv, cosine, sine, tile=256):
    rows, width = dq.shape
    return pl.pallas_call(
        rope_back_kernel,
        grid=(rows // tile,),
        in_specs=[
            pl.BlockSpec((tile, width), lambda i: (i, 0)),
            pl.BlockSpec((tile, 2 * width), lambda i: (i, 0)),
            pl.BlockSpec((tile, 128), lambda i: (i, 0)),
            pl.BlockSpec((tile, 128), lambda i: (i, 0)),
        ],
        out_specs=pl.BlockSpec((tile, 3 * width), lambda i: (i, 0)),
        out_shape=jax.ShapeDtypeStruct((rows, 3 * width), BF16),
        cost_estimate=pl.CostEstimate(flops=8 * rows * 2 * width, bytes_accessed=rows * 3 * width * 5, transcendentals=0),
        name="rope_back",
    )(dq, dkv, cosine, sine)

SCALE = HEAD_DIM ** -0.5
NEG = -1e30

def attn_fwd_kernel(c_ref, q_ref, kv_ref, o_ref, lse_ref, *, kb):
    rows, width = q_ref.shape
    heads = width // HEAD_DIM
    steps = rows // kb
    c = c_ref[0]
    for h in range(heads):
        lanes = slice(h * HEAD_DIM, (h + 1) * HEAD_DIM)
        vlanes = slice(width + h * HEAD_DIM, width + (h + 1) * HEAD_DIM)
        q = q_ref[:, lanes] * SCALE

        def block(j, carry, masked, q=q, lanes=lanes, vlanes=vlanes):
            top, total, acc = carry
            at = pl.ds(pl.multiple_of(j * kb, kb), kb)
            s = mm(kv_ref[at, lanes], q, 1, 1)
            if masked is not None:
                key = lax.broadcasted_iota(jnp.int32, s.shape, 0) + masked * kb
                s = jnp.where(key <= lax.broadcasted_iota(jnp.int32, s.shape, 1), s, NEG)
            new_top = jnp.maximum(top, jnp.max(s, 0, keepdims=True))
            p = jnp.exp(s - new_top)
            alpha = jnp.exp(top - new_top)
            total = total * alpha + jnp.sum(p, 0, keepdims=True)
            acc = acc * alpha + mm(kv_ref[at, vlanes], p.astype(BF16), 0, 0)
            return new_top, total, acc

        carry = (jnp.full((1, rows), NEG, F32), jnp.zeros((1, rows), F32), jnp.zeros((HEAD_DIM, rows), F32))
        carry = lax.fori_loop(0, c * steps, lambda j, x: block(j, x, None), carry)
        for i in range(steps):
            carry = block(c * steps + i, carry, i)
        top, total, acc = carry
        o_ref[:, lanes] = (acc / total).T.astype(BF16)
        lse_ref[h : h + 1, :] = top + jnp.log(total)

def attn_fwd(c, q, kv, kb=512):
    rows, width = q.shape
    heads = width // HEAD_DIM
    n = rows * kv.shape[0] * heads
    return pl.pallas_call(
        functools.partial(attn_fwd_kernel, kb=kb),
        in_specs=[pl.BlockSpec(memory_space=pltpu.SMEM), pl.BlockSpec(memory_space=pltpu.VMEM), pl.BlockSpec(memory_space=pltpu.VMEM)],
        out_specs=[pl.BlockSpec(memory_space=pltpu.VMEM), pl.BlockSpec(memory_space=pltpu.VMEM)],
        out_shape=[jax.ShapeDtypeStruct((rows, width), BF16), jax.ShapeDtypeStruct((heads, rows), F32)],
        cost_estimate=pl.CostEstimate(flops=4 * n * HEAD_DIM * 4, bytes_accessed=2 * (q.size * 2 + kv.size), transcendentals=n),
        name="attn_fwd",
    )(c, q, kv)

def attn_bwd_kernel(c_ref, q_ref, kv_ref, o_ref, do_ref, lse_ref, dq_ref, dkv_ref, *, kb):
    rows, width = q_ref.shape
    heads = width // HEAD_DIM
    steps = rows // kb
    c = c_ref[0]
    total_steps = kv_ref.shape[0] // kb

    def clear(j, x):
        at = pl.ds(pl.multiple_of(j * kb, kb), kb)
        dkv_ref[at, :] = jnp.zeros((kb, 2 * width), BF16)
        return x

    lax.fori_loop((c + 1) * steps, total_steps, clear, 0)
    for h in range(heads):
        lanes = slice(h * HEAD_DIM, (h + 1) * HEAD_DIM)
        vlanes = slice(width + h * HEAD_DIM, width + (h + 1) * HEAD_DIM)
        q = q_ref[:, lanes] * SCALE
        do = do_ref[:, lanes]
        lse = lse_ref[h : h + 1, :]
        prod = do.astype(F32) * o_ref[:, lanes].astype(F32)
        delta = jnp.sum(prod.T, 0, keepdims=True)

        def block(j, dq, masked, q=q, do=do, lse=lse, delta=delta, lanes=lanes, vlanes=vlanes):
            at = pl.ds(pl.multiple_of(j * kb, kb), kb)
            k = kv_ref[at, lanes]
            s = mm(k, q, 1, 1)
            if masked is not None:
                key = lax.broadcasted_iota(jnp.int32, s.shape, 0) + masked * kb
                s = jnp.where(key <= lax.broadcasted_iota(jnp.int32, s.shape, 1), s, NEG)
            p = jnp.exp(s - lse)
            dp = mm(kv_ref[at, vlanes], do, 1, 1)
            ds = (p * (dp - delta)).astype(BF16)
            dkv_ref[at, vlanes] = mm(p.astype(BF16), do, 1, 0).astype(BF16)
            dkv_ref[at, lanes] = mm(ds, q, 1, 0).astype(BF16)
            return dq + mm(k, ds, 0, 0)

        dq = jnp.zeros((HEAD_DIM, rows), F32)
        dq = lax.fori_loop(0, c * steps, lambda j, x: block(j, x, None), dq)
        for i in range(steps):
            dq = block(c * steps + i, dq, i)
        dq_ref[:, lanes] = dq.T * SCALE

def attn_bwd(c, q, kv, o, do, lse, kb=512):
    rows, width = q.shape
    heads = width // HEAD_DIM
    n = rows * kv.shape[0] * heads
    vm = pl.BlockSpec(memory_space=pltpu.VMEM)
    return pl.pallas_call(
        functools.partial(attn_bwd_kernel, kb=kb),
        in_specs=[pl.BlockSpec(memory_space=pltpu.SMEM)] + [vm] * 5,
        out_specs=[vm, vm],
        out_shape=[jax.ShapeDtypeStruct((rows, width), F32), jax.ShapeDtypeStruct(kv.shape, BF16)],
        cost_estimate=pl.CostEstimate(flops=10 * n * HEAD_DIM * 4, bytes_accessed=2 * (q.size * 5 + 2 * kv.size), transcendentals=n),
        name="attn_bwd",
    )(c, q, kv, o, do, lse)


def expert_kernel(*refs):
    x_ref, gi_ref, first_hbm, gate_hbm, up_hbm = refs[:5]
    inner_ref, gg_ref, gu_ref, x_out_ref, gn_ref, gate_v, up_v, sems = refs[-8:]
    shard = up_v.shape[1]
    cut = first_hbm.shape[1] - shard
    gate_copies = [pltpu.make_async_copy(gate_hbm, gate_v.at[:, cut:], sems.at[0])]
    if cut:
        gate_copies.append(
            pltpu.make_async_copy(first_hbm.at[:, shard:], gate_v.at[:, :cut], sems.at[1])
        )
    up_copy = pltpu.make_async_copy(up_hbm, up_v, sems.at[2])
    first = pl.program_id(0) == 0

    @pl.when(first)
    def _():
        for copy in gate_copies:
            copy.start()
        up_copy.start()
        for copy in gate_copies:
            copy.wait()

    x = x_ref[...]
    x_out_ref[...] = x
    gate = mm(x, rows_of(gate_v), 1, 0)

    @pl.when(first)
    def _():
        up_copy.wait()

    up = mm(x, rows_of(up_v), 1, 0)
    gi = gi_ref[...].astype(F32)
    sigma = jax.nn.sigmoid(gate)
    active = gate * sigma
    inner_ref[...] = (active * up).astype(BF16)
    gg = (gi * up * sigma * (1.0 + gate * (1.0 - sigma))).astype(BF16)
    gu = (gi * active).astype(BF16)
    gg_ref[...] = gg
    gu_ref[...] = gu
    gn_ref[...] = (mm(gg, rows_of(gate_v), 1, 1) + mm(gu, rows_of(up_v), 1, 1)).astype(BF16)


def expert_core(x, gi, first, gate_rest, up_w, blocks, earlier):
    rows, width = x.shape
    shards, shard, hidden = up_w.shape
    tile = rows // len(blocks)
    total = gi.shape[0]

    def place(i):
        at = jnp.int32(blocks[0])
        for k, b in enumerate(blocks[1:]):
            at = jnp.where(i == k + 1, jnp.int32(b), at)
        return (at, 0)

    group = pl.BlockSpec((tile, width), lambda i: (i, 0))
    hbm = pl.BlockSpec(memory_space=pl.ANY)
    in_place = pl.BlockSpec((tile, hidden), place)
    return pl.pallas_call(
        expert_kernel,
        grid=(len(blocks),),
        in_specs=[group, in_place, hbm, hbm, hbm] + [hbm] * len(earlier),
        out_specs=[in_place, in_place, in_place, pl.BlockSpec((tile, width), place), group],
        out_shape=[jax.ShapeDtypeStruct((total, hidden), BF16)] * 3
        + [jax.ShapeDtypeStruct((total, width), BF16), jax.ShapeDtypeStruct((rows, width), BF16)],
        input_output_aliases={5 + k: k for k in range(len(earlier))},
        scratch_shapes=[
            pltpu.VMEM((shards, shard, hidden), BF16),
            pltpu.VMEM((shards, shard, hidden), BF16),
            pltpu.SemaphoreType.DMA((3,)),
        ],
        compiler_params=pltpu.CompilerParams(vmem_limit_bytes=60 << 20),
        cost_estimate=pl.CostEstimate(
            flops=8 * rows * width * hidden,
            bytes_accessed=4 * width * hidden + rows * (6 * width + 8 * hidden),
            transcendentals=rows * hidden,
        ),
        name="expert_core",
    )(x, gi, first, gate_rest, up_w, *earlier)


BRIEF = pl.CostEstimate(flops=1 << 20, bytes_accessed=1 << 16, transcendentals=0)


def rows_of(ref):
    return ref[...].reshape(-1, ref.shape[-1])


def grad_inner_kernel(*refs, tiles):
    *parts, share_ref, first_hbm, gy_ref, gi_ref, down_v, sem = refs
    i = pl.program_id(0)
    copy = pltpu.make_async_copy(first_hbm.at[:, : down_v.shape[1]], down_v, sem)

    @pl.when(i == 0)
    def _():
        copy.start()

    for k, part in enumerate(parts):

        @pl.when((i >= k * tiles) & (i < (k + 1) * tiles))
        def _(part=part):
            gy_ref[...] = (share_ref[...] * (RESIDUAL_SCALE * part[...].astype(F32))).astype(BF16)

    @pl.when(i == 0)
    def _():
        copy.wait()

    gi_ref[...] = mm(gy_ref[...], rows_of(down_v), 1, 0).astype(BF16)

def grad_inner_call(parts, share, first, tile=256):
    rows, width = parts[0].shape
    blocks, _, hidden = first.shape
    total = rows * len(parts)
    tiles = rows // tile
    row = lambda n: pl.BlockSpec((tile, n), lambda i: (i, 0))
    of = lambda k: pl.BlockSpec((tile, width), lambda i: (jnp.clip(i - k * tiles, 0, tiles - 1), 0))
    return pl.pallas_call(
        functools.partial(grad_inner_kernel, tiles=tiles),
        grid=(total // tile,),
        in_specs=[of(k) for k in range(len(parts))] + [row(1), pl.BlockSpec(memory_space=pl.ANY)],
        out_specs=[row(width), row(hidden)],
        out_shape=[jax.ShapeDtypeStruct((total, width), BF16), jax.ShapeDtypeStruct((total, hidden), BF16)],
        scratch_shapes=[
            pltpu.VMEM((blocks, width // blocks, hidden), BF16),
            pltpu.SemaphoreType.DMA,
        ],
        compiler_params=pltpu.CompilerParams(vmem_limit_bytes=56 << 20),
        cost_estimate=BRIEF,
        name="grad_inner",
    )(*parts, share[:, None], first)


def output_kernel(*refs):
    inner_ref, share_ref = refs[:2]
    first_hbm, y_ref, down_v, sem = refs[-4:]
    copy = pltpu.make_async_copy(first_hbm.at[:, : down_v.shape[1]], down_v, sem)

    @pl.when(pl.program_id(0) == 0)
    def _():
        copy.start()
        copy.wait()

    y = share_ref[...] * mm(inner_ref[...], rows_of(down_v), 1, 1)
    if len(refs) == 7:
        y = y + refs[2][...].astype(F32)
    y_ref[...] = y.astype(BF16)


def output_call(inner, share, weights, width, first, count, other=None, other_first=0, tile=256):
    blocks, _, hidden = weights.shape
    at = lambda n: pl.BlockSpec((tile, n), lambda i: (i + first // tile, 0))
    row = pl.BlockSpec((tile, width), lambda i: (i, 0))
    add = pl.BlockSpec((tile, width), lambda i: (i + other_first // tile, 0))
    others = [] if other is None else [other]
    return pl.pallas_call(
        output_kernel,
        grid=(count // tile,),
        in_specs=[at(hidden), at(1)] + [add] * len(others) + [pl.BlockSpec(memory_space=pl.ANY)],
        out_specs=row,
        out_shape=jax.ShapeDtypeStruct((count, width), BF16),
        scratch_shapes=[
            pltpu.VMEM((blocks, width // blocks, hidden), BF16),
            pltpu.SemaphoreType.DMA,
        ],
        compiler_params=pltpu.CompilerParams(vmem_limit_bytes=56 << 20),
        cost_estimate=BRIEF,
        name="expert_out",
    )(inner, share[:, None], *others, weights)


def arrange_kernel(depth_ref, *refs, offsets):
    out_ref = refs[-1]
    for ref, offset in zip(refs, offsets):

        @pl.when(pl.program_id(0) == depth_ref[0] + offset)
        def _(ref=ref):
            out_ref[0] = ref[...]


def arrange(depth, below, above):
    blocks, rows, width = below[0].shape
    chips = len(below)
    offsets = [0] + [-i for i in range(1, chips)] + list(range(1, chips))

    def of(offset):
        def at(q, b, depth_ref):
            turn = depth_ref[0] + offset
            return (jnp.where(q == turn, b, jnp.where(q < turn, 0, blocks - 1)), 0, 0)

        return pl.BlockSpec((1, rows, width), at)

    whole = pl.pallas_call(
        functools.partial(arrange_kernel, offsets=offsets),
        grid_spec=pltpu.PrefetchScalarGridSpec(
            num_scalar_prefetch=1,
            grid=(chips, blocks),
            in_specs=[of(offset) for offset in offsets],
            out_specs=pl.BlockSpec((1, 1, rows, width), lambda q, b, depth_ref: (b, q, 0, 0)),
        ),
        out_shape=jax.ShapeDtypeStruct((blocks, chips, rows, width), below[0].dtype),
        cost_estimate=BRIEF,
        name="arrange",
    )(depth.astype(jnp.int32).reshape(1), *below, *above[1:])
    return whole.reshape(-1, width)


def wgrad_kernel(x_ref, g_ref, o_ref):
    o_ref[...] = mm(x_ref[...], g_ref[...], 0, 0).astype(BF16)

def wgrad_call(x, g, tile=384):
    rows, width = x.shape
    hidden = g.shape[1]
    return pl.pallas_call(
        wgrad_kernel,
        grid=(width // tile,),
        in_specs=[pl.BlockSpec((rows, tile), lambda i: (0, i)), pl.BlockSpec((rows, hidden), lambda i: (0, 0), pipeline_mode=pl.Buffered(1))],
        out_specs=pl.BlockSpec((tile, hidden), lambda i: (i, 0)),
        out_shape=jax.ShapeDtypeStruct((width, hidden), BF16),
        compiler_params=pltpu.CompilerParams(vmem_limit_bytes=56 << 20),
        cost_estimate=BRIEF,
        name="weight_grad",
    )(x, g)


def resid_backward_kernel(tok_ref, att_ref, gn_ref, cot_ref, gain_ref, resid_grad_ref, att_grad_ref, part_ref):
    resid = tok_ref[...].astype(F32) + RESIDUAL_SCALE * att_ref[...].astype(F32)
    inverse = lax.rsqrt(jnp.mean(resid * resid, -1, keepdims=True) + EPS)
    grad = gn_ref[...].astype(F32)
    scaled = gain_ref[...] * grad
    mean = jnp.mean(scaled * resid, -1, keepdims=True)
    out = cot_ref[...].astype(F32) + inverse * scaled - resid * (inverse * inverse * inverse * mean)
    resid_grad_ref[...] = out
    att_grad_ref[...] = (RESIDUAL_SCALE * out).astype(BF16)

    @pl.when(pl.program_id(0) == 0)
    def _():
        part_ref[...] = jnp.zeros_like(part_ref)

    part_ref[...] += jnp.sum(grad * resid * inverse, 0, keepdims=True)


def resid_backward(tokens, attn_total, grad_n2, cotangent, gain, tile=128):
    rows, width = tokens.shape
    row = pl.BlockSpec((tile, width), lambda i: (i, 0))
    line = pl.BlockSpec((1, width), lambda i: (0, 0))
    return pl.pallas_call(
        resid_backward_kernel,
        grid=(rows // tile,),
        in_specs=[row] * 4 + [line],
        out_specs=[row, row, line],
        out_shape=[
            jax.ShapeDtypeStruct((rows, width), F32),
            jax.ShapeDtypeStruct((rows, width), BF16),
            jax.ShapeDtypeStruct((1, width), F32),
        ],
        cost_estimate=BRIEF,
        name="resid_backward",
    )(tokens, attn_total, grad_n2, cotangent, gain[None, :])


def pair_grad_kernel(a_ref, b_ref, c_ref, d_ref, o_ref):
    cut = b_ref.shape[1]
    o_ref[:, :cut] = mm(a_ref[...], b_ref[...], 0, 0).astype(BF16)
    o_ref[:, cut:] = mm(c_ref[...], d_ref[...], 0, 0).astype(BF16)


def pair_grad(a, b, c, d, tile=384):
    rows, width = a.shape
    total = b.shape[1] + d.shape[1]
    part = pl.BlockSpec((rows, tile), lambda i: (0, i))
    whole = lambda x: pl.BlockSpec(x.shape, lambda i: (0, 0))
    return pl.pallas_call(
        pair_grad_kernel,
        grid=(width // tile,),
        in_specs=[part, whole(b), part, whole(d)],
        out_specs=pl.BlockSpec((tile, total), lambda i: (i, 0)),
        out_shape=jax.ShapeDtypeStruct((width, total), BF16),
        compiler_params=pltpu.CompilerParams(vmem_limit_bytes=48 << 20),
        cost_estimate=BRIEF,
        name="pair_grad",
    )(a, b, c, d)


def norm_backward(inputs, inverse, gain, grad_normed):
    scaled = gain[None, :] * grad_normed
    gain_grad = jnp.sum(grad_normed * inputs * inverse[:, None], 0)
    input_part = inverse[:, None] * scaled - inputs * (inverse**3)[:, None] * jnp.mean(
        scaled * inputs, -1, keepdims=True
    )
    return (gain_grad, input_part)


def together(*values):
    return lax.optimization_barrier(values)


def after(value, *earlier):
    return lax.optimization_barrier((value, *earlier))[0]


class Direct:
    parts = 1

    def __init__(self, axes):
        self.axes = axes

    def order(self, share):
        return share.reshape(-1)

    def spread(self, x):
        whole = lax.all_gather(x, self.axes, axis=0, tiled=True)
        return (lambda *values: values), (lambda: whole), (lambda x: [x])

    def exchange(self, x, core):
        whole = lax.all_gather(x, self.axes, axis=0, tiled=True)
        size = whole.shape[0] // 4
        sums, kept = [], ()
        for i in range(4):
            *kept, part = core(
                whole[i * size : (i + 1) * size], tuple(range(4 * i, 4 * i + 4)), kept
            )
            sums.append(part)
        scatter = lambda x: lax.psum_scatter(x, self.axes, scatter_dimension=0, tiled=True)
        return kept, (lambda work: (scatter(jnp.concatenate(sums, 0)), work(None)))

    def scatter(self, odd, even, work):
        done = work(odd)
        whole = lax.psum_scatter(odd, self.axes, scatter_dimension=0, tiled=True)
        return done, (lambda *values: values), (lambda hold: whole)


class Paired:
    near = (0, 4, 2, 6, 1, 5, 3, 7)
    parts = 2

    def move(self, x, bits):
        return lax.ppermute(x, GROUP, [(j, j ^ bits) for j in range(8)])

    def order(self, share):
        me = lax.axis_index(GROUP)
        return share[jnp.bitwise_xor(me, jnp.array(self.near, jnp.int32))].reshape(-1)

    def pair(self, a, b):
        both = a if b is None else jnp.concatenate([a, b], 0)
        return jnp.concatenate([both, self.move(both, 1)], 0)

    def merge(self, group):
        half = group.shape[0] // 4
        both = group[: 2 * half] + self.move(group[2 * half :], 1)
        return both[:half], both[half:]

    def exchange(self, x, core):
        half = x.shape[0] // 2
        lo, hi = x[:half], x[half:]
        x_lo, y_hi = self.move(lo, 4), self.move(hi, 2)
        *kept, out0 = core(self.pair(x, None), (0, 1, 8, 9), ())
        out0, x_lo, y_hi = together(out0, x_lo, y_hi)
        d_lo, d_hi = self.move(x_lo, 2), self.move(y_hi, 4)
        x_hi, y_lo = self.move(after(hi, out0), 4), self.move(after(lo, out0), 2)
        *kept, out1 = core(self.pair(x_lo, y_hi), (2, 5, 10, 13), kept)
        out1, d_lo, d_hi = together(out1, d_lo, d_hi)
        third = self.pair(d_lo, d_hi)
        third, px_lo, py_hi, p_lo, p_hi = together(third, *self.merge(out1), *self.merge(out0))
        px_lo, py_hi = self.move(px_lo, 4), self.move(py_hi, 2)
        *kept, out2 = core(third, (6, 7, 14, 15), kept)
        out2, x_hi, y_lo, px_lo, py_hi = together(out2, x_hi, y_lo, px_lo, py_hi)
        fourth = self.pair(x_hi, y_lo)
        fourth, pd_lo, pd_hi = together(fourth, *self.merge(out2))
        pd_lo, pd_hi = self.move(pd_lo, 4), self.move(pd_hi, 2)
        *kept, out3 = core(fourth, (3, 4, 11, 12), kept)
        out3, pd_lo, pd_hi = together(out3, pd_lo, pd_hi)

        def finish(work):
            px_hi, py_lo = self.merge(out3)
            px_hi, py_lo = together(px_hi + pd_hi, py_lo + pd_lo)
            done = work(px_hi)
            px_hi, py_lo = self.move(px_hi, 4), self.move(py_lo, 2)
            px_hi, py_lo, done = together(px_hi, py_lo, done)
            return jnp.concatenate([p_lo + px_lo + py_lo, p_hi + px_hi + py_hi], 0), done

        return kept, finish

    def spread(self, x):
        rows = x.shape[0] // 4
        depth = lax.axis_index("tp")
        mine = lax.dynamic_slice_in_dim(x, depth * rows, rows, 0)
        here = jnp.stack([mine, self.move(mine, 4), self.move(mine, 2), self.move(mine, 6)], 0)
        below, above = [here], [here]

        def step(*values):
            if len(below) == 1:
                values = together(here, *values)
                below[0] = above[0] = values[0]
                values = values[1:]
            else:
                values = together(below[-1], above[-1], *values)
                below[-1], above[-1] = values[:2]
                values = values[2:]
            if len(below) < 4:
                below.append(lax.ppermute(below[-1], "tp", [(0, 1), (1, 2), (2, 3)]))
                above.append(lax.ppermute(above[-1], "tp", [(3, 2), (2, 1), (1, 0)]))
            return values

        def finish():
            return arrange(depth, below, above)

        def share_out(whole):
            return [whole, self.move(whole, 1)]

        return step, finish, share_out

    def scatter(self, odd, even, work):
        other = self.move(odd, 1)
        size = other.shape[0] // 4
        half = size // 2
        rows = lambda i, n, hold: even(i * size, n * size, hold, other)
        last = rows(3, 1, None)
        d_lo, d_hi = last[:half], last[half:]
        middle = rows(1, 2, together(d_lo, d_hi)[0])
        x_lo, x_hi, y_lo, y_hi = (middle[i * half : (i + 1) * half] for i in range(4))
        hold, x_lo, x_hi, y_lo, y_hi = together(middle, x_lo, x_hi, y_lo, y_hi)
        done0 = work(hold)
        d_lo, d_hi = self.move(d_lo, 4), self.move(d_hi, 2)
        x_lo, y_hi = self.move(x_lo, 4), self.move(y_hi, 2)
        d_lo, d_hi, x_lo, y_hi, done0 = together(d_lo, d_hi, x_lo, y_hi, done0)
        x_hi, y_lo = together(x_hi + d_hi, y_lo + d_lo)
        moved = [self.move(x_hi, 4), self.move(y_lo, 2)]

        def settle(*values):
            values = together(*moved, *values)
            moved[:] = values[:2]
            return values[2:]

        def total(hold):
            first = rows(0, 1, hold)
            lo, hi = first[:half] + x_lo, first[half:] + y_hi
            return jnp.concatenate([lo + moved[1], hi + moved[0]], 0)

        return done0, settle, total


def make_body(experts, ep_axes, rest, tokens_by):
    def fetch(*weights):
        if rest is None:
            return lax.all_to_all(jnp.concatenate(weights, 1), ep_axes, 0, 0, tiled=True)
        found = (lax.all_to_all(weight, ep_axes, 0, 0, tiled=True) for weight in weights)
        return jnp.concatenate(
            [lax.all_gather(weight, rest, axis=1, tiled=True) for weight in found], 1
        )

    def halves(blocks):
        count = blocks.shape[1] if rest is None else blocks.shape[1] // lax.axis_size(rest)
        split = blocks.reshape(-1, count, blocks.shape[2])
        cut = count // 2
        return tuple(
            part.reshape(experts, -1, blocks.shape[2]) for part in (split[:, :cut], split[:, cut:])
        )

    def send(blocks):
        if rest is not None:
            blocks = lax.psum_scatter(blocks, rest, scatter_dimension=1, tiled=True)
        return lax.all_to_all(blocks, ep_axes, 0, 0, tiled=True)

    def give_back(grad):
        return send(grad.reshape(experts, -1, grad.shape[-1]))

    def body(
        hidden_in,
        out_cotangent,
        attn_gain,
        qkv_weight,
        out_weight,
        ffn_gain,
        gate_weight,
        up_weight,
        down_weight,
        expert_ids,
        route_weights,
    ):
        tokens = hidden_in[0].astype(F32)
        tok_count, width = tokens.shape
        shard = qkv_weight.shape[0]
        local_width = qkv_weight.shape[2]
        ctx = lax.axis_index("ctx")

        qkv_mat = lax.all_gather(
            qkv_weight.reshape(shard, 3 * local_width), GROUP, axis=0, tiled=True
        )
        cot_step, cot_finish, cot_share = tokens_by.spread(out_cotangent[0])
        small = jnp.concatenate(
            [
                attn_gain.astype(F32),
                ffn_gain.astype(F32),
                expert_ids[0].astype(F32).reshape(-1),
                route_weights[0].reshape(-1),
            ]
        )
        small = jnp.broadcast_to(small, (lax.axis_size(GROUP), 1, small.shape[0]))
        small = lax.all_to_all(small, GROUP, 0, 0, tiled=True)[:, 0]
        cut = shard // 2 if rest is None else 0
        small, *early = cot_step(small, down_weight.swapaxes(1, 2), gate_weight[:, :cut])
        first = fetch(*early) if cut else fetch(early[0])
        (small,) = cot_step(small)
        qkv_mat, small = together(qkv_mat, small)
        gain_one = small[:, :shard].reshape(-1)
        gain_two = small[:, shard : 2 * shard].reshape(-1)
        routes = small[:, 2 * shard :].reshape(-1, 2, tok_count, expert_ids.shape[2])
        if rest is not None:
            routes = routes.reshape(experts, -1, *routes.shape[1:])
            routes = lax.dynamic_index_in_dim(routes, lax.axis_index(rest), 1, keepdims=False)
        mine = lax.axis_index(ep_axes).astype(F32)
        share = jnp.sum(jnp.where(routes[:, 0] == mine, routes[:, 1], 0.0), -1)
        share = tokens_by.order(share)

        half = HEAD_DIM // 2
        positions = ctx * tok_count + jnp.arange(tok_count, dtype=jnp.int32)
        freqs = ROPE_BASE ** (-2.0 * jnp.arange(half, dtype=F32) / HEAD_DIM)
        angles = positions.astype(F32)[:, None] * freqs[None, :]
        cosine, sine = jnp.cos(angles), jnp.sin(angles)
        cosine = jnp.concatenate([cosine] * 4, 1)
        sine = jnp.concatenate([-sine, sine] * 2, 1)
        inverse1 = lax.rsqrt(jnp.mean(tokens * tokens, -1) + EPS)
        normed1 = (tokens * inverse1[:, None] * gain_one[None, :]).astype(BF16)
        query, kv_here = rope(mm(normed1, qkv_mat, 1, 0), cosine, sine, local_width)

        (kv_here,) = cot_step(kv_here)
        kv_all = lax.all_gather(kv_here, "ctx", axis=0, tiled=True)
        cot_step(kv_here)
        kv_all, first, cot_all = together(kv_all, first, cot_finish())

        out_full = lax.all_gather(after(out_weight, kv_all), GROUP, axis=1, tiled=True)
        gate_rest = fetch(after(gate_weight[:, cut:], kv_all))
        block = ctx.astype(jnp.int32).reshape(1)
        attended, log_norm = attn_fwd(block, query, kv_all)
        part_out = mm(attended, out_full, 1, 0).astype(BF16)
        attn_total = lax.psum(part_out, "tp")
        gate_rest, up_in = together(gate_rest, after(up_weight, part_out))
        up_w = fetch(up_in)
        grad_y, grad_inner = grad_inner_call(cot_share(after(cot_all, part_out)), share, first)
        attn_total, grad_inner = together(attn_total, grad_inner)
        resid = tokens + RESIDUAL_SCALE * attn_total.astype(F32)
        inverse2 = lax.rsqrt(jnp.mean(resid * resid, -1) + EPS)
        normed2 = (resid * inverse2[:, None] * gain_two[None, :]).astype(BF16)

        kept, finish = tokens_by.exchange(
            normed2,
            lambda x, blocks, earlier: expert_core(
                x, grad_inner, first, gate_rest, up_w, blocks, tuple(earlier)
            ),
        )
        inner, grad_gate, grad_up, normed_all = kept
        count = inner.shape[0] // tokens_by.parts

        def outputs(start, size, hold=None, other=None):
            rows = inner if hold is None else after(inner, hold)
            return output_call(rows, share, first, width, start, size, other, start)

        grad_n2, odd_y = finish(lambda hold: outputs(inner.shape[0] - count, count, hold))

        grad_n2 = lax.psum(grad_n2, "tp")
        def down_work(hold):
            grad = wgrad_call(after(grad_y, hold), inner)
            return together(*halves(grad.reshape(experts, -1, inner.shape[1])))

        (down_lo, down_hi), mixed_settle, mixed_total = tokens_by.scatter(odd_y, outputs, down_work)
        down_lo = send(down_lo)
        grad_n2, down_hi = together(grad_n2, down_hi)

        grad_resid, grad_att, ffn_part = resid_backward(
            hidden_in[0], attn_total, grad_n2, out_cotangent[0], gain_two
        )
        grad_attended = mm(grad_att, out_full, 1, 1).astype(BF16)
        grad_query, kv_grad = attn_bwd(block, query, kv_all, attended, grad_attended, log_norm)
        kv_grad, down_lo, down_hi = mixed_settle(kv_grad, down_lo, down_hi)
        kv_grad_here = lax.psum_scatter(kv_grad, "ctx", scatter_dimension=0, tiled=True)
        down_hi = send(down_hi)
        gate_grad = wgrad_call(after(normed_all, kv_grad), grad_gate)
        kv_grad_here, gate_grad, down_hi = together(kv_grad_here, gate_grad, down_hi)
        down_weight_grad = jnp.concatenate([down_lo, down_hi], 1)

        grad_proj = rope_back(grad_query, kv_grad_here, cosine, sine)
        part_n1 = mm(grad_proj, qkv_mat, 1, 1).astype(BF16)
        grad_n1 = lax.psum(part_n1, "tp")
        gate_weight_grad = give_back(after(gate_grad, part_n1))
        up_grad = wgrad_call(after(normed_all, part_n1), grad_up)
        mixed = mixed_total(part_n1)
        weight_part = pair_grad(after(normed1, part_n1), grad_proj, grad_att, attended)
        grad_n1, gate_weight_grad, up_grad, mixed, weight_part = together(
            grad_n1, gate_weight_grad, up_grad, mixed, weight_part
        )

        up_weight_grad = give_back(up_grad)
        mixed = lax.psum(mixed, "tp")
        mixed, up_weight_grad, weight_part = together(mixed, up_weight_grad, weight_part)
        weight_grad = lax.psum_scatter(weight_part, GROUP, scatter_dimension=0, tiled=True)
        weight_grad = weight_grad.astype(F32)
        block_out = (resid + RESIDUAL_SCALE * mixed.astype(F32)).astype(BF16)
        attn_part, input_part = norm_backward(tokens, inverse1, gain_one, grad_n1.astype(F32))
        input_grad = grad_resid + input_part
        parts = jnp.stack([attn_part, ffn_part[0]], 0).reshape(2, -1, shard).swapaxes(0, 1)
        gain_grads = jnp.sum(lax.all_to_all(parts, GROUP, 0, 0, tiled=True), 0)
        return (
            block_out[None],
            input_grad[None],
            gain_grads[0],
            weight_grad[:, : 3 * local_width].reshape(shard, 3, local_width),
            weight_grad[:, 3 * local_width :].T,
            gain_grads[1],
            gate_weight_grad.astype(F32),
            up_weight_grad.astype(F32),
            down_weight_grad.astype(F32).swapaxes(1, 2),
        )

    return body


def solution(mesh):
    experts = 8
    sizes = (mesh.shape["fsdp"], mesh.shape["ctx"])
    if sizes == (2, 4) and mesh.shape["tp"] == 4:
        ep_axes, rest, tokens_by = GROUP, None, Paired()
    elif sizes[0] * sizes[1] == experts:
        ep_axes, rest, tokens_by = GROUP, None, Direct(GROUP)
    else:
        assert sizes[0] == experts
        ep_axes, rest, tokens_by = ("fsdp",), "ctx", Direct(("fsdp",))
    in_specs = (
        P("fsdp", "ctx", None),
        P("fsdp", "ctx", None),
        P(GROUP),
        P(GROUP, None, "tp"),
        P("tp", GROUP),
        P(GROUP),
        P(None, GROUP, "tp"),
        P(None, GROUP, "tp"),
        P(None, "tp", GROUP),
        P("fsdp", "ctx", None),
        P("fsdp", "ctx", None),
    )
    out_specs = (
        P("fsdp", "ctx", None),
        P("fsdp", "ctx", None),
        P(GROUP),
        P(GROUP, None, "tp"),
        P("tp", GROUP),
        P(GROUP),
        P(None, GROUP, "tp"),
        P(None, GROUP, "tp"),
        P(None, "tp", GROUP),
    )
    body = make_body(experts, ep_axes, rest, tokens_by)
    return jax.shard_map(body, mesh=mesh, in_specs=in_specs, out_specs=out_specs, check_vma=False)
```

```python
import functools
import math

import jax
import jax.numpy as jnp
from jax import lax
from jax.experimental import pallas as pl
from jax.experimental.pallas import tpu as pltpu
from jax.sharding import PartitionSpec as P

HEAD_DIM = 64
EPS = 1e-05
RESIDUAL_SCALE = 1.4 / math.sqrt(40.0)
ROPE_BASE = 10000.0
GROUP = ("fsdp", "ctx")
BF16 = jnp.bfloat16
F32 = jnp.float32


def mm(a, b, ca, cb):
    return lax.dot_general(a, b, (((ca,), (cb,)), ((), ())), preferred_element_type=F32)


BRIEF = pl.CostEstimate(flops=1 << 20, bytes_accessed=1 << 16, transcendentals=0)


def swap_halves(x):
    lane = lax.broadcasted_iota(jnp.int32, x.shape, 1)
    return jnp.where(lane % 64 < 32, pltpu.roll(x, 96, 1), pltpu.roll(x, 32, 1))

def rope_store(proj, cosine, sine, q_ref, kv_ref):
    width = q_ref.shape[1]
    parts = []
    for j in range(2 * width // 128):
        x = proj[:, 128 * j : 128 * (j + 1)]
        parts.append((x * cosine + swap_halves(x) * sine).astype(BF16))
    both = jnp.concatenate(parts, 1)
    q_ref[...] = both[:, :width]
    kv_ref[:, :width] = both[:, width:]
    kv_ref[:, width:] = proj[:, 2 * width :].astype(BF16)


def rope_back_kernel(dq_ref, dkv_ref, cos_ref, sin_ref, out_ref):
    width = dq_ref.shape[1]
    cosine, sine = cos_ref[...], sin_ref[...]
    both = jnp.concatenate([dq_ref[...], dkv_ref[:, :width].astype(F32)], 1)
    for j in range(2 * width // 128):
        x = both[:, 128 * j : 128 * (j + 1)]
        out_ref[:, 128 * j : 128 * (j + 1)] = (x * cosine - swap_halves(x) * sine).astype(BF16)
    out_ref[:, 2 * width :] = dkv_ref[:, width:]

def rope_back(dq, dkv, cosine, sine, tile=256):
    rows, width = dq.shape
    return pl.pallas_call(
        rope_back_kernel,
        grid=(rows // tile,),
        in_specs=[
            pl.BlockSpec((tile, width), lambda i: (i, 0)),
            pl.BlockSpec((tile, 2 * width), lambda i: (i, 0)),
            pl.BlockSpec((tile, 128), lambda i: (i, 0)),
            pl.BlockSpec((tile, 128), lambda i: (i, 0)),
        ],
        out_specs=pl.BlockSpec((tile, 3 * width), lambda i: (i, 0)),
        out_shape=jax.ShapeDtypeStruct((rows, 3 * width), BF16),
        cost_estimate=BRIEF,
        name="rope_back",
    )(dq, dkv, cosine, sine)

SCALE = HEAD_DIM ** -0.5
NEG = -1e30

def attn_fwd_kernel(c_ref, q_ref, kv_ref, o_ref, lse_ref, *, kb):
    rows, width = q_ref.shape
    heads = width // HEAD_DIM
    steps = rows // kb
    c = c_ref[0]
    for h in range(heads):
        lanes = slice(h * HEAD_DIM, (h + 1) * HEAD_DIM)
        vlanes = slice(width + h * HEAD_DIM, width + (h + 1) * HEAD_DIM)
        q = q_ref[:, lanes] * SCALE

        def block(j, carry, masked, q=q, lanes=lanes, vlanes=vlanes):
            top, total, acc = carry
            at = pl.ds(pl.multiple_of(j * kb, kb), kb)
            s = mm(kv_ref[at, lanes], q, 1, 1)
            if masked is not None:
                key = lax.broadcasted_iota(jnp.int32, s.shape, 0) + masked * kb
                s = jnp.where(key <= lax.broadcasted_iota(jnp.int32, s.shape, 1), s, NEG)
            new_top = jnp.maximum(top, jnp.max(s, 0, keepdims=True))
            p = jnp.exp(s - new_top)
            alpha = jnp.exp(top - new_top)
            total = total * alpha + jnp.sum(p, 0, keepdims=True)
            acc = acc * alpha + mm(kv_ref[at, vlanes], p.astype(BF16), 0, 0)
            return new_top, total, acc

        carry = (jnp.full((1, rows), NEG, F32), jnp.zeros((1, rows), F32), jnp.zeros((HEAD_DIM, rows), F32))
        carry = lax.fori_loop(0, c * steps, lambda j, x: block(j, x, None), carry)
        for i in range(steps):
            carry = block(c * steps + i, carry, i)
        top, total, acc = carry
        o_ref[:, lanes] = (acc / total).T.astype(BF16)
        lse_ref[h : h + 1, :] = top + jnp.log(total)

def attn_fwd(c, q, kv, kb=512):
    rows, width = q.shape
    heads = width // HEAD_DIM
    n = rows * kv.shape[0] * heads
    return pl.pallas_call(
        functools.partial(attn_fwd_kernel, kb=kb),
        in_specs=[pl.BlockSpec(memory_space=pltpu.SMEM), pl.BlockSpec(memory_space=pltpu.VMEM), pl.BlockSpec(memory_space=pltpu.VMEM)],
        out_specs=[pl.BlockSpec(memory_space=pltpu.VMEM), pl.BlockSpec(memory_space=pltpu.VMEM)],
        out_shape=[jax.ShapeDtypeStruct((rows, width), BF16), jax.ShapeDtypeStruct((heads, rows), F32)],
        cost_estimate=BRIEF,
        name="attn_fwd",
    )(c, q, kv)

def attn_bwd_kernel(c_ref, q_ref, kv_ref, o_ref, do_ref, lse_ref, dq_ref, dkv_ref, *, kb):
    rows, width = q_ref.shape
    heads = width // HEAD_DIM
    steps = rows // kb
    c = c_ref[0]
    total_steps = kv_ref.shape[0] // kb

    def clear(j, x):
        at = pl.ds(pl.multiple_of(j * kb, kb), kb)
        dkv_ref[at, :] = jnp.zeros((kb, 2 * width), BF16)
        return x

    lax.fori_loop((c + 1) * steps, total_steps, clear, 0)
    for h in range(heads):
        lanes = slice(h * HEAD_DIM, (h + 1) * HEAD_DIM)
        vlanes = slice(width + h * HEAD_DIM, width + (h + 1) * HEAD_DIM)
        q = q_ref[:, lanes] * SCALE
        do = do_ref[:, lanes]
        lse = lse_ref[h : h + 1, :]
        prod = do.astype(F32) * o_ref[:, lanes].astype(F32)
        delta = jnp.sum(prod.T, 0, keepdims=True)

        def block(j, dq, masked, q=q, do=do, lse=lse, delta=delta, lanes=lanes, vlanes=vlanes):
            at = pl.ds(pl.multiple_of(j * kb, kb), kb)
            k = kv_ref[at, lanes]
            s = mm(k, q, 1, 1)
            if masked is not None:
                key = lax.broadcasted_iota(jnp.int32, s.shape, 0) + masked * kb
                s = jnp.where(key <= lax.broadcasted_iota(jnp.int32, s.shape, 1), s, NEG)
            p = jnp.exp(s - lse)
            dp = mm(kv_ref[at, vlanes], do, 1, 1)
            ds = (p * (dp - delta)).astype(BF16)
            dkv_ref[at, vlanes] = mm(p.astype(BF16), do, 1, 0).astype(BF16)
            dkv_ref[at, lanes] = mm(ds, q, 1, 0).astype(BF16)
            return dq + mm(k, ds, 0, 0)

        dq = jnp.zeros((HEAD_DIM, rows), F32)
        dq = lax.fori_loop(0, c * steps, lambda j, x: block(j, x, None), dq)
        for i in range(steps):
            dq = block(c * steps + i, dq, i)
        dq_ref[:, lanes] = dq.T * SCALE

def attn_bwd(c, q, kv, o, do, lse, kb=512):
    rows, width = q.shape
    heads = width // HEAD_DIM
    n = rows * kv.shape[0] * heads
    vm = pl.BlockSpec(memory_space=pltpu.VMEM)
    return pl.pallas_call(
        functools.partial(attn_bwd_kernel, kb=kb),
        in_specs=[pl.BlockSpec(memory_space=pltpu.SMEM)] + [vm] * 5,
        out_specs=[vm, vm],
        out_shape=[jax.ShapeDtypeStruct((rows, width), F32), jax.ShapeDtypeStruct(kv.shape, BF16)],
        cost_estimate=pl.CostEstimate(flops=1 << 37, bytes_accessed=1 << 24, transcendentals=n),
        name="attn_bwd",
    )(c, q, kv, o, do, lse)


def expert_kernel(*refs):
    x_ref, gi_ref, first_hbm, up_hbm = refs[:4]
    inner_ref, gg_ref, gu_ref, x_out_ref, gn_ref, gate_v, up_v, sems = refs[-8:]
    gate_copy = pltpu.make_async_copy(first_hbm.at[:, gate_v.shape[1] :], gate_v, sems.at[0])
    up_copy = pltpu.make_async_copy(up_hbm, up_v, sems.at[1])
    first = pl.program_id(0) == 0

    @pl.when(first)
    def _():
        gate_copy.start()
        up_copy.start()
        gate_copy.wait()

    x = x_ref[...]
    x_out_ref[...] = x
    gate = mm(x, rows_of(gate_v), 1, 0)

    @pl.when(first)
    def _():
        up_copy.wait()

    up = mm(x, rows_of(up_v), 1, 0)
    gi = gi_ref[...].astype(F32)
    sigma = jax.nn.sigmoid(gate)
    active = gate * sigma
    inner_ref[...] = (active * up).astype(BF16)
    gg = (gi * up * sigma * (1.0 + gate * (1.0 - sigma))).astype(BF16)
    gu = (gi * active).astype(BF16)
    gg_ref[...] = gg
    gu_ref[...] = gu
    gn_ref[...] = (mm(gg, rows_of(gate_v), 1, 1) + mm(gu, rows_of(up_v), 1, 1)).astype(BF16)


def expert_core(x, gi, first, up_w, blocks, earlier):
    rows, width = x.shape
    shards, shard, hidden = up_w.shape
    tile = rows // len(blocks)
    total = gi.shape[0]

    def place(i):
        at = jnp.int32(blocks[0])
        for k, b in enumerate(blocks[1:]):
            at = jnp.where(i == k + 1, jnp.int32(b), at)
        return (at, 0)

    group = pl.BlockSpec((tile, width), lambda i: (i, 0))
    hbm = pl.BlockSpec(memory_space=pl.ANY)
    in_place = pl.BlockSpec((tile, hidden), place)
    return pl.pallas_call(
        expert_kernel,
        grid=(len(blocks),),
        in_specs=[group, in_place, hbm, hbm] + [hbm] * len(earlier),
        out_specs=[in_place, in_place, in_place, pl.BlockSpec((tile, width), place), group],
        out_shape=[jax.ShapeDtypeStruct((total, hidden), BF16)] * 3
        + [jax.ShapeDtypeStruct((total, width), BF16), jax.ShapeDtypeStruct((rows, width), BF16)],
        input_output_aliases={4 + k: k for k in range(len(earlier))},
        scratch_shapes=[
            pltpu.VMEM((shards, shard, hidden), BF16),
            pltpu.VMEM((shards, shard, hidden), BF16),
            pltpu.SemaphoreType.DMA((2,)),
        ],
        compiler_params=pltpu.CompilerParams(vmem_limit_bytes=60 << 20),
        cost_estimate=pl.CostEstimate(
            flops=8 * rows * width * hidden,
            bytes_accessed=4 * width * hidden + rows * (6 * width + 8 * hidden),
            transcendentals=rows * hidden,
        ),
        name="expert_core",
    )(x, gi, first, up_w, *earlier)


def rows_of(ref):
    return ref[...].reshape(-1, ref.shape[-1])


def grad_inner_kernel(*refs, tiles):
    *parts, share_ref, first_hbm, gy_ref, gi_ref, down_v, sem = refs
    i = pl.program_id(0)
    copy = pltpu.make_async_copy(first_hbm.at[:, : down_v.shape[1]], down_v, sem)

    @pl.when(i == 0)
    def _():
        copy.start()

    for k, part in enumerate(parts):

        @pl.when((i >= k * tiles) & (i < (k + 1) * tiles))
        def _(part=part):
            gy_ref[...] = (share_ref[...] * (RESIDUAL_SCALE * part[...].astype(F32))).astype(BF16)

    @pl.when(i == 0)
    def _():
        copy.wait()

    gi_ref[...] = mm(gy_ref[...], rows_of(down_v), 1, 0).astype(BF16)

def grad_inner_call(parts, share, first, tile=256):
    rows, width = parts[0].shape
    blocks, _, hidden = first.shape
    total = rows * len(parts)
    tiles = rows // tile
    row = lambda n: pl.BlockSpec((tile, n), lambda i: (i, 0))
    of = lambda k: pl.BlockSpec((tile, width), lambda i: (jnp.clip(i - k * tiles, 0, tiles - 1), 0))
    return pl.pallas_call(
        functools.partial(grad_inner_kernel, tiles=tiles),
        grid=(total // tile,),
        in_specs=[of(k) for k in range(len(parts))] + [row(1), pl.BlockSpec(memory_space=pl.ANY)],
        out_specs=[row(width), row(hidden)],
        out_shape=[jax.ShapeDtypeStruct((total, width), BF16), jax.ShapeDtypeStruct((total, hidden), BF16)],
        scratch_shapes=[
            pltpu.VMEM((blocks, width // blocks, hidden), BF16),
            pltpu.SemaphoreType.DMA,
        ],
        compiler_params=pltpu.CompilerParams(vmem_limit_bytes=56 << 20),
        cost_estimate=BRIEF,
        name="grad_inner",
    )(*parts, share[:, None], first)


def output_kernel(*refs, pieces):
    inner_ref, share_ref = refs[:2]
    first_hbm, *y_refs, down_v, sem = refs[-pieces - 3 :]
    i = pl.program_id(0)
    copy = pltpu.make_async_copy(first_hbm.at[:, : down_v.shape[1]], down_v, sem)

    @pl.when(i == 0)
    def _():
        copy.start()
        copy.wait()

    y = share_ref[...] * mm(inner_ref[...], rows_of(down_v), 1, 1)
    if len(refs) == pieces + 6:
        y = y + refs[2][...].astype(F32)
    y = y.astype(BF16)
    for k, y_ref in enumerate(y_refs):

        @pl.when(i * pieces // pl.num_programs(0) == k)
        def _(y_ref=y_ref):
            y_ref[...] = y


def output_call(inner, share, weights, width, start, count, other=None, pieces=1, tile=256):
    blocks, _, hidden = weights.shape
    at = lambda n: pl.BlockSpec((tile, n), lambda i: (i + start // tile, 0))
    others = [] if other is None else [other]
    if pieces == 1:
        out = pl.BlockSpec((tile, width), lambda i: (i, 0))
    else:
        out = pl.BlockSpec((tile, width), lambda i: (0, 0))
    return pl.pallas_call(
        functools.partial(output_kernel, pieces=pieces),
        grid=(count // tile,),
        in_specs=[at(hidden), at(1)] + [at(width)] * len(others) + [pl.BlockSpec(memory_space=pl.ANY)],
        out_specs=[out] * pieces,
        out_shape=[jax.ShapeDtypeStruct((count // pieces, width), BF16)] * pieces,
        scratch_shapes=[
            pltpu.VMEM((blocks, width // blocks, hidden), BF16),
            pltpu.SemaphoreType.DMA,
        ],
        compiler_params=pltpu.CompilerParams(vmem_limit_bytes=56 << 20),
        cost_estimate=BRIEF,
        name="expert_out",
    )(inner, share[:, None], *others, weights)


def arrange_kernel(depth_ref, *refs, offsets):
    out_ref = refs[-1]
    for ref, offset in zip(refs, offsets):

        @pl.when(pl.program_id(0) == depth_ref[0] + offset)
        def _(ref=ref):
            out_ref[0] = ref[...]


def arrange(depth, below, above):
    blocks, rows, width = below[0].shape
    chips = len(below)
    offsets = [0] + [-i for i in range(1, chips)] + list(range(1, chips))

    def of(offset):
        def at(q, b, depth_ref):
            turn = depth_ref[0] + offset
            return (jnp.where(q == turn, b, jnp.where(q < turn, 0, blocks - 1)), 0, 0)

        return pl.BlockSpec((1, rows, width), at)

    whole = pl.pallas_call(
        functools.partial(arrange_kernel, offsets=offsets),
        grid_spec=pltpu.PrefetchScalarGridSpec(
            num_scalar_prefetch=1,
            grid=(chips, blocks),
            in_specs=[of(offset) for offset in offsets],
            out_specs=pl.BlockSpec((1, 1, rows, width), lambda q, b, depth_ref: (b, q, 0, 0)),
        ),
        out_shape=jax.ShapeDtypeStruct((blocks, chips, rows, width), below[0].dtype),
        cost_estimate=BRIEF,
        name="arrange",
    )(depth.astype(jnp.int32).reshape(1), *below, *above[1:])
    return whole.reshape(-1, width)


def wgrad_kernel(x_ref, g_ref, o_ref):
    o_ref[...] = mm(x_ref[...], g_ref[...], 0, 0).astype(BF16)

def wgrad_call(x, g, tile=384):
    rows, width = x.shape
    hidden = g.shape[1]
    return pl.pallas_call(
        wgrad_kernel,
        grid=(width // tile,),
        in_specs=[pl.BlockSpec((rows, tile), lambda i: (0, i)), pl.BlockSpec((rows, hidden), lambda i: (0, 0), pipeline_mode=pl.Buffered(1))],
        out_specs=pl.BlockSpec((tile, hidden), lambda i: (i, 0)),
        out_shape=jax.ShapeDtypeStruct((width, hidden), BF16),
        compiler_params=pltpu.CompilerParams(vmem_limit_bytes=56 << 20),
        cost_estimate=BRIEF,
        name="weight_grad",
    )(x, g)


def wgrad_halves_kernel(x_ref, g_ref, lo_ref, hi_ref):
    grad = mm(x_ref[...], g_ref[...], 0, 0).astype(BF16)
    cut = lo_ref.shape[1]
    for b in range(lo_ref.shape[0]):
        lo_ref[b] = grad[2 * b * cut : (2 * b + 1) * cut]
        hi_ref[b] = grad[(2 * b + 1) * cut : (2 * b + 2) * cut]


def wgrad_halves(x, g, blocks, step=4):
    rows, width = x.shape
    hidden = g.shape[1]
    cut = width // blocks // 2
    half = pl.BlockSpec((step, cut, hidden), lambda i: (i, 0, 0))
    return pl.pallas_call(
        wgrad_halves_kernel,
        grid=(blocks // step,),
        in_specs=[
            pl.BlockSpec((rows, step * 2 * cut), lambda i: (0, i)),
            pl.BlockSpec((rows, hidden), lambda i: (0, 0), pipeline_mode=pl.Buffered(1)),
        ],
        out_specs=[half, half],
        out_shape=[jax.ShapeDtypeStruct((blocks, cut, hidden), BF16)] * 2,
        compiler_params=pltpu.CompilerParams(vmem_limit_bytes=60 << 20),
        cost_estimate=BRIEF,
        name="weight_grad",
    )(x, g)


def resid_backward_kernel(tok_ref, att_ref, gn_ref, cot_ref, gain_ref, resid_grad_ref, att_grad_ref, part_ref):
    resid = tok_ref[...].astype(F32) + RESIDUAL_SCALE * att_ref[...].astype(F32)
    inverse = lax.rsqrt(jnp.mean(resid * resid, -1, keepdims=True) + EPS)
    grad = gn_ref[...].astype(F32)
    scaled = gain_ref[...] * grad
    mean = jnp.mean(scaled * resid, -1, keepdims=True)
    out = cot_ref[...].astype(F32) + inverse * scaled - resid * (inverse * inverse * inverse * mean)
    resid_grad_ref[...] = out
    att_grad_ref[...] = (RESIDUAL_SCALE * out).astype(BF16)

    @pl.when(pl.program_id(0) == 0)
    def _():
        part_ref[...] = jnp.zeros_like(part_ref)

    part_ref[...] += jnp.sum(grad * resid * inverse, 0, keepdims=True)


def resid_backward(tokens, attn_total, grad_n2, cotangent, gain, tile=128):
    rows, width = tokens.shape
    row = pl.BlockSpec((tile, width), lambda i: (i, 0))
    line = pl.BlockSpec((1, width), lambda i: (0, 0))
    return pl.pallas_call(
        resid_backward_kernel,
        grid=(rows // tile,),
        in_specs=[row] * 4 + [line],
        out_specs=[row, row, line],
        out_shape=[
            jax.ShapeDtypeStruct((rows, width), F32),
            jax.ShapeDtypeStruct((rows, width), BF16),
            jax.ShapeDtypeStruct((1, width), F32),
        ],
        cost_estimate=BRIEF,
        name="resid_backward",
    )(tokens, attn_total, grad_n2, cotangent, gain[None, :])


def pair_grad_kernel(a_ref, b_ref, c_ref, d_ref, o_ref):
    cut = b_ref.shape[1]
    o_ref[:, :cut] = mm(a_ref[...], b_ref[...], 0, 0).astype(BF16)
    o_ref[:, cut:] = mm(c_ref[...], d_ref[...], 0, 0).astype(BF16)


def pair_grad(a, b, c, d, tile=384):
    rows, width = a.shape
    total = b.shape[1] + d.shape[1]
    part = pl.BlockSpec((rows, tile), lambda i: (0, i))
    whole = lambda x: pl.BlockSpec(x.shape, lambda i: (0, 0))
    return pl.pallas_call(
        pair_grad_kernel,
        grid=(width // tile,),
        in_specs=[part, whole(b), part, whole(d)],
        out_specs=pl.BlockSpec((tile, total), lambda i: (i, 0)),
        out_shape=jax.ShapeDtypeStruct((width, total), BF16),
        compiler_params=pltpu.CompilerParams(vmem_limit_bytes=48 << 20),
        cost_estimate=BRIEF,
        name="pair_grad",
    )(a, b, c, d)


def attn_in_kernel(tok_ref, gain_ref, weight_ref, cos_ref, sin_ref, normed_ref, q_ref, kv_ref):
    tokens = tok_ref[...].astype(F32)
    inverse = lax.rsqrt(jnp.mean(tokens * tokens, -1, keepdims=True) + EPS)
    normed_ref[...] = (tokens * inverse * gain_ref[...]).astype(BF16)
    rope_store(mm(normed_ref[...], weight_ref[...], 1, 0), cos_ref[...], sin_ref[...], q_ref, kv_ref)


def attn_in(tokens, gain, weight, cosine, sine, tile=256):
    rows, width = tokens.shape
    local = weight.shape[1] // 3
    row = lambda n: pl.BlockSpec((tile, n), lambda i: (i, 0))
    return pl.pallas_call(
        attn_in_kernel,
        grid=(rows // tile,),
        in_specs=[
            row(width),
            pl.BlockSpec((1, width), lambda i: (0, 0)),
            pl.BlockSpec(weight.shape, lambda i: (0, 0), pipeline_mode=pl.Buffered(1)),
            row(128),
            row(128),
        ],
        out_specs=[row(width), row(local), row(2 * local)],
        out_shape=[
            jax.ShapeDtypeStruct((rows, width), BF16),
            jax.ShapeDtypeStruct((rows, local), BF16),
            jax.ShapeDtypeStruct((rows, 2 * local), BF16),
        ],
        compiler_params=pltpu.CompilerParams(vmem_limit_bytes=48 << 20),
        cost_estimate=BRIEF,
        name="attn_in",
    )(tokens, gain[None, :], weight, cosine, sine)


def norm_backward(inputs, inverse, gain, grad_normed):
    scaled = gain[None, :] * grad_normed
    gain_grad = jnp.sum(grad_normed * inputs * inverse[:, None], 0)
    input_part = inverse[:, None] * scaled - inputs * (inverse**3)[:, None] * jnp.mean(
        scaled * inputs, -1, keepdims=True
    )
    return (gain_grad, input_part)


def together(*values):
    return lax.optimization_barrier(values)


def after(value, *earlier):
    return lax.optimization_barrier((value, *earlier))[0]


class Direct:
    parts = 1

    def __init__(self, axes):
        self.axes = axes

    def order(self, share):
        return share.reshape(-1)

    def spread(self, x):
        whole = lax.all_gather(x, self.axes, axis=0, tiled=True)
        return (lambda *values: values), (lambda: whole), (lambda x: [x])

    def exchange(self, x, core):
        whole = lax.all_gather(x, self.axes, axis=0, tiled=True)
        size = whole.shape[0] // 4
        sums, kept = [], ()
        for i in range(4):
            *kept, part = core(
                whole[i * size : (i + 1) * size], tuple(range(4 * i, 4 * i + 4)), kept
            )
            sums.append(part)
        whole = lax.psum_scatter(jnp.concatenate(sums, 0), self.axes, scatter_dimension=0, tiled=True)
        return kept, (lambda work: (whole, work(whole)[0]))

    def scatter(self, odd, even, work):
        done = work(odd)[0]
        whole = lax.psum_scatter(odd[0], self.axes, scatter_dimension=0, tiled=True)
        return done, (lambda *values: values), (lambda: whole)


class Paired:
    near = (0, 4, 2, 6, 1, 5, 3, 7)
    parts = 2

    def move(self, x, bits):
        return lax.ppermute(x, GROUP, [(j, j ^ bits) for j in range(8)])

    def order(self, share):
        me = lax.axis_index(GROUP)
        return share[jnp.bitwise_xor(me, jnp.array(self.near, jnp.int32))].reshape(-1)

    def pair(self, a, b):
        both = a if b is None else jnp.concatenate([a, b], 0)
        return jnp.concatenate([both, self.move(both, 1)], 0)

    def merge(self, group):
        half = group.shape[0] // 4
        both = group[: 2 * half] + self.move(group[2 * half :], 1)
        return both[:half], both[half:]

    def exchange(self, x, core):
        half = x.shape[0] // 2
        lo, hi = x[:half], x[half:]
        x_lo, y_hi = self.move(lo, 4), self.move(hi, 2)
        *kept, out0 = core(self.pair(x, None), (0, 1, 8, 9), ())
        out0, x_lo, y_hi = together(out0, x_lo, y_hi)
        d_lo, d_hi = self.move(x_lo, 2), self.move(y_hi, 4)
        hi, lo, out0 = together(hi, lo, out0)
        x_hi, y_lo = self.move(hi, 4), self.move(lo, 2)
        *kept, out1 = core(self.pair(x_lo, y_hi), (2, 5, 10, 13), kept)
        out1, d_lo, d_hi = together(out1, d_lo, d_hi)
        third = self.pair(d_lo, d_hi)
        third, px_lo, py_hi, p_lo, p_hi = together(third, *self.merge(out1), *self.merge(out0))
        px_lo, py_hi = self.move(px_lo, 4), self.move(py_hi, 2)
        *kept, out2 = core(third, (6, 7, 14, 15), kept)
        out2, x_hi, y_lo, px_lo, py_hi = together(out2, x_hi, y_lo, px_lo, py_hi)
        fourth = self.pair(x_hi, y_lo)
        fourth, pd_lo, pd_hi = together(fourth, *self.merge(out2))
        pd_lo, pd_hi = self.move(pd_lo, 4), self.move(pd_hi, 2)
        *kept, out3 = core(fourth, (3, 4, 11, 12), kept)
        out3, pd_lo, pd_hi = together(out3, pd_lo, pd_hi)

        def finish(work):
            px_hi, py_lo = self.merge(out3)
            done, px_hi = work(px_hi + pd_hi)
            py_lo = py_lo + pd_lo
            px_hi, py_lo = self.move(px_hi, 4), self.move(py_lo, 2)
            px_hi, py_lo, done = together(px_hi, py_lo, done)
            return jnp.concatenate([p_lo + px_lo + py_lo, p_hi + px_hi + py_hi], 0), done

        return kept, finish

    def spread(self, x):
        rows = x.shape[0] // 4
        depth = lax.axis_index("tp")
        mine = lax.dynamic_slice_in_dim(x, depth * rows, rows, 0)
        here = jnp.stack([mine, self.move(mine, 4), self.move(mine, 2), self.move(mine, 6)], 0)
        below, above = [here], [here]

        def step(*values):
            if len(below) == 1:
                values = together(here, *values)
                below[0] = above[0] = values[0]
                values = values[1:]
            else:
                values = together(below[-1], above[-1], *values)
                below[-1], above[-1] = values[:2]
                values = values[2:]
            if len(below) < 4:
                below.append(lax.ppermute(below[-1], "tp", [(0, 1), (1, 2), (2, 3)]))
                above.append(lax.ppermute(above[-1], "tp", [(3, 2), (2, 1), (1, 0)]))
            return values

        def finish():
            return arrange(depth, below, above)

        def share_out(whole):
            return [whole, self.move(whole, 1)]

        return step, finish, share_out

    def carry(self, x, y, d):
        moved = [self.move(d[0], 4), self.move(d[1], 2), self.move(x[0], 4), self.move(y[1], 2)]

        def hold(*values):
            values = together(*moved, *values)
            count = len(moved)
            moved[:] = values[:count]
            return values[count:]

        def settle(*values):
            values = together(*moved, *values)
            if len(moved) == 4:
                d_lo, d_hi, x_lo, y_hi = values[:4]
                x_hi, y_lo = self.move(x[1] + d_hi, 4), self.move(y[0] + d_lo, 2)
                moved[:] = [x_hi, y_lo, x_lo, y_hi, d_lo]
                return values[4:]
            moved[:] = values[:5]
            return values[5:]

        def arrived(own):
            x_hi, y_lo, x_lo, y_hi, _ = moved
            return jnp.concatenate([own[0] + x_lo + y_lo, own[1] + x_hi + y_hi], 0)

        return hold, settle, arrived

    def scatter(self, odd, even, work):
        other = self.move(odd[0], 1)
        size = other.shape[0] // 4
        d, hold = even(3 * size, size, other)
        middle, hold = even(size, 2 * size, other, d[0])
        x_lo, x_hi, y_lo, y_hi = middle
        done, y_hi = work(y_hi)
        hold, settle, arrived = self.carry((x_lo, x_hi), (y_lo, y_hi), (hold, d[1]))
        done = hold(*done)
        return done, settle, (lambda: arrived(even(0, size, other)[0]))


def make_body(experts, ep_axes, rest, tokens_by):
    def fetch(*weights):
        if rest is None:
            return lax.all_to_all(jnp.concatenate(weights, 1), ep_axes, 0, 0, tiled=True)
        found = (lax.all_to_all(weight, ep_axes, 0, 0, tiled=True) for weight in weights)
        return jnp.concatenate(
            [lax.all_gather(weight, rest, axis=1, tiled=True) for weight in found], 1
        )

    def halves(blocks):
        count = blocks.shape[1] if rest is None else blocks.shape[1] // lax.axis_size(rest)
        split = blocks.reshape(-1, count, blocks.shape[2])
        cut = count // 2
        return tuple(
            part.reshape(experts, -1, blocks.shape[2]) for part in (split[:, :cut], split[:, cut:])
        )

    def send(blocks):
        if rest is not None:
            blocks = lax.psum_scatter(blocks, rest, scatter_dimension=1, tiled=True)
        return lax.all_to_all(blocks, ep_axes, 0, 0, tiled=True)

    def give_back(grad):
        return send(grad.reshape(experts, -1, grad.shape[-1]))

    def body(
        hidden_in,
        out_cotangent,
        attn_gain,
        qkv_weight,
        out_weight,
        ffn_gain,
        gate_weight,
        up_weight,
        down_weight,
        expert_ids,
        route_weights,
    ):
        tokens = hidden_in[0].astype(F32)
        tok_count, width = tokens.shape
        shard = qkv_weight.shape[0]
        local_width = qkv_weight.shape[2]
        ctx = lax.axis_index("ctx")

        qkv_mat = lax.all_gather(
            qkv_weight.reshape(shard, 3 * local_width), GROUP, axis=0, tiled=True
        )
        cot_step, cot_finish, cot_share = tokens_by.spread(out_cotangent[0])
        small = jnp.concatenate(
            [
                attn_gain.astype(F32),
                ffn_gain.astype(F32),
                expert_ids[0].astype(F32).reshape(-1),
                route_weights[0].reshape(-1),
            ]
        )
        small = jnp.broadcast_to(small, (lax.axis_size(GROUP), 1, small.shape[0]))
        small = lax.all_to_all(small, GROUP, 0, 0, tiled=True)[:, 0]
        (early,) = together(jnp.concatenate([down_weight.swapaxes(1, 2), gate_weight], 1))
        small, early = cot_step(small, early)
        first = fetch(early) if rest is None else fetch(early[:, :shard], early[:, shard:])
        qkv_mat, small = together(qkv_mat, small)
        gain_one = small[:, :shard].reshape(-1)
        gain_two = small[:, shard : 2 * shard].reshape(-1)
        routes = small[:, 2 * shard :].reshape(-1, 2, tok_count, expert_ids.shape[2])
        if rest is not None:
            routes = routes.reshape(experts, -1, *routes.shape[1:])
            routes = lax.dynamic_index_in_dim(routes, lax.axis_index(rest), 1, keepdims=False)
        mine = lax.axis_index(ep_axes).astype(F32)
        share = jnp.sum(jnp.where(routes[:, 0] == mine, routes[:, 1], 0.0), -1)
        share = tokens_by.order(share)

        half = HEAD_DIM // 2
        positions = ctx * tok_count + jnp.arange(tok_count, dtype=jnp.int32)
        freqs = ROPE_BASE ** (-2.0 * jnp.arange(half, dtype=F32) / HEAD_DIM)
        angles = positions.astype(F32)[:, None] * freqs[None, :]
        cosine, sine = jnp.cos(angles), jnp.sin(angles)
        cosine = jnp.concatenate([cosine] * 4, 1)
        sine = jnp.concatenate([-sine, sine] * 2, 1)
        inverse1 = lax.rsqrt(jnp.mean(tokens * tokens, -1) + EPS)
        normed1, query, kv_here = attn_in(hidden_in[0], gain_one, qkv_mat, cosine, sine)

        kv_all = lax.all_gather(kv_here, "ctx", axis=0, tiled=True)
        cot_step(kv_here)
        cot_step()

        out_full = lax.all_gather(after(out_weight, kv_all), GROUP, axis=1, tiled=True)
        block = ctx.astype(jnp.int32).reshape(1)
        attended, log_norm = attn_fwd(block, query, kv_all)
        (attended,) = cot_step(attended)
        attended, cot_all, first = together(attended, cot_finish(), first)
        part_out = mm(attended, out_full, 1, 0).astype(BF16)
        attn_total = lax.psum(part_out, "tp")
        up_w = fetch(after(up_weight, part_out))
        grad_y, grad_inner = grad_inner_call(cot_share(after(cot_all, part_out)), share, first)
        attn_total, grad_inner = together(attn_total, grad_inner)
        resid = tokens + RESIDUAL_SCALE * attn_total.astype(F32)
        inverse2 = lax.rsqrt(jnp.mean(resid * resid, -1) + EPS)
        normed2 = (resid * inverse2[:, None] * gain_two[None, :]).astype(BF16)

        kept, finish = tokens_by.exchange(
            normed2,
            lambda x, blocks, earlier: expert_core(
                x, grad_inner, first, up_w, blocks, tuple(earlier)
            ),
        )
        inner, grad_gate, grad_up, normed_all = kept
        count = inner.shape[0] // tokens_by.parts

        def outputs(start, size, other=None, hold=None):
            rows, hold = (inner, None) if hold is None else together(inner, hold)
            pieces = 1 if other is None else size // 256
            return output_call(rows, share, first, width, start, size, other, pieces), hold

        grad_n2, odd_y = finish(lambda hold: outputs(inner.shape[0] - count, count, None, hold))

        grad_n2 = lax.psum(grad_n2, "tp")
        def down_work(hold):
            rows, hold = together(grad_y, hold)
            if rest is None:
                return wgrad_halves(rows, inner, experts), hold
            return halves(wgrad_call(rows, inner).reshape(experts, -1, inner.shape[1])), hold

        (down_lo, down_hi), mixed_settle, mixed_total = tokens_by.scatter(odd_y, outputs, down_work)
        down_lo = send(down_lo)
        grad_n2, down_hi = mixed_settle(grad_n2, down_hi)

        grad_resid, grad_att, ffn_part = resid_backward(
            hidden_in[0], attn_total, grad_n2, out_cotangent[0], gain_two
        )
        grad_attended = mm(grad_att, out_full, 1, 1).astype(BF16)
        grad_query, kv_grad = attn_bwd(block, query, kv_all, attended, grad_attended, log_norm)
        kv_grad, down_lo, down_hi, normed_all = mixed_settle(kv_grad, down_lo, down_hi, normed_all)
        kv_grad_here = lax.psum_scatter(kv_grad, "ctx", scatter_dimension=0, tiled=True)
        down_hi = send(down_hi)
        gate_grad = wgrad_call(normed_all, grad_gate)
        mixed = mixed_total()
        kv_grad_here, gate_grad, mixed, down_hi = together(
            kv_grad_here, gate_grad, mixed, down_hi
        )
        down_weight_grad = jnp.concatenate([down_lo, down_hi], 1)

        grad_proj = rope_back(grad_query, kv_grad_here, cosine, sine)
        part_n1 = mm(grad_proj, qkv_mat, 1, 1).astype(BF16)
        grad_n1, mixed = lax.psum((part_n1, mixed), "tp")
        gate_weight_grad = give_back(after(gate_grad, part_n1))
        up_grad = wgrad_call(after(normed_all, part_n1), grad_up)
        weight_part = pair_grad(after(normed1, part_n1), grad_proj, grad_att, attended)
        up_grad, weight_part, gate_weight_grad = together(up_grad, weight_part, gate_weight_grad)
        up_weight_grad = give_back(up_grad)
        grad_n1, mixed, up_weight_grad = together(grad_n1, mixed, up_weight_grad)

        weight_grad = lax.psum_scatter(weight_part, GROUP, scatter_dimension=0, tiled=True)
        weight_grad = weight_grad.astype(F32)
        block_out = (resid + RESIDUAL_SCALE * mixed.astype(F32)).astype(BF16)
        attn_part, input_part = norm_backward(tokens, inverse1, gain_one, grad_n1.astype(F32))
        input_grad = grad_resid + input_part
        parts = jnp.stack([attn_part, ffn_part[0]], 0).reshape(2, -1, shard).swapaxes(0, 1)
        gain_grads = jnp.sum(lax.all_to_all(parts, GROUP, 0, 0, tiled=True), 0)
        return (
            block_out[None],
            input_grad[None],
            gain_grads[0],
            weight_grad[:, : 3 * local_width].reshape(shard, 3, local_width),
            weight_grad[:, 3 * local_width :].T,
            gain_grads[1],
            gate_weight_grad.astype(F32),
            up_weight_grad.astype(F32),
            down_weight_grad.astype(F32).swapaxes(1, 2),
        )

    return body


def solution(mesh):
    experts = 8
    sizes = (mesh.shape["fsdp"], mesh.shape["ctx"])
    if sizes == (2, 4) and mesh.shape["tp"] == 4:
        ep_axes, rest, tokens_by = GROUP, None, Paired()
    elif sizes[0] * sizes[1] == experts:
        ep_axes, rest, tokens_by = GROUP, None, Direct(GROUP)
    else:
        assert sizes[0] == experts
        ep_axes, rest, tokens_by = ("fsdp",), "ctx", Direct(("fsdp",))
    in_specs = (
        P("fsdp", "ctx", None),
        P("fsdp", "ctx", None),
        P(GROUP),
        P(GROUP, None, "tp"),
        P("tp", GROUP),
        P(GROUP),
        P(None, GROUP, "tp"),
        P(None, GROUP, "tp"),
        P(None, "tp", GROUP),
        P("fsdp", "ctx", None),
        P("fsdp", "ctx", None),
    )
    out_specs = (
        P("fsdp", "ctx", None),
        P("fsdp", "ctx", None),
        P(GROUP),
        P(GROUP, None, "tp"),
        P("tp", GROUP),
        P(GROUP),
        P(None, GROUP, "tp"),
        P(None, GROUP, "tp"),
        P(None, "tp", GROUP),
    )
    body = make_body(experts, ep_axes, rest, tokens_by)
    return jax.shard_map(body, mesh=mesh, in_specs=in_specs, out_specs=out_specs, check_vma=False)
```

```python
import functools
import math

import jax
import jax.numpy as jnp
from jax import lax
from jax.experimental import pallas as pl
from jax.experimental.pallas import tpu as pltpu
from jax.sharding import PartitionSpec as P

HEAD_DIM = 64
EPS = 1e-05
RESIDUAL_SCALE = 1.4 / math.sqrt(40.0)
ROPE_BASE = 10000.0
GROUP = ("fsdp", "ctx")
BF16 = jnp.bfloat16
F32 = jnp.float32


def mm(a, b, ca, cb):
    return lax.dot_general(a, b, (((ca,), (cb,)), ((), ())), preferred_element_type=F32)


BRIEF = pl.CostEstimate(flops=1 << 20, bytes_accessed=1 << 16, transcendentals=0)


def swap_halves(x):
    lane = lax.broadcasted_iota(jnp.int32, x.shape, 1)
    return jnp.where(lane % 64 < 32, pltpu.roll(x, 96, 1), pltpu.roll(x, 32, 1))

def rope_store(proj, cosine, sine, q_ref, kv_ref):
    width = q_ref.shape[1]
    parts = []
    for j in range(2 * width // 128):
        x = proj[:, 128 * j : 128 * (j + 1)]
        parts.append((x * cosine + swap_halves(x) * sine).astype(BF16))
    both = jnp.concatenate(parts, 1)
    q_ref[...] = both[:, :width]
    kv_ref[:, :width] = both[:, width:]
    kv_ref[:, width:] = proj[:, 2 * width :].astype(BF16)


def rope_back_kernel(dq_ref, dkv_ref, cos_ref, sin_ref, out_ref):
    width = dq_ref.shape[1]
    cosine, sine = cos_ref[...], sin_ref[...]
    both = jnp.concatenate([dq_ref[...], dkv_ref[:, :width].astype(F32)], 1)
    for j in range(2 * width // 128):
        x = both[:, 128 * j : 128 * (j + 1)]
        out_ref[:, 128 * j : 128 * (j + 1)] = (x * cosine - swap_halves(x) * sine).astype(BF16)
    out_ref[:, 2 * width :] = dkv_ref[:, width:]

def rope_back(dq, dkv, cosine, sine, tile=256):
    rows, width = dq.shape
    return pl.pallas_call(
        rope_back_kernel,
        grid=(rows // tile,),
        in_specs=[
            pl.BlockSpec((tile, width), lambda i: (i, 0)),
            pl.BlockSpec((tile, 2 * width), lambda i: (i, 0)),
            pl.BlockSpec((tile, 128), lambda i: (i, 0)),
            pl.BlockSpec((tile, 128), lambda i: (i, 0)),
        ],
        out_specs=pl.BlockSpec((tile, 3 * width), lambda i: (i, 0)),
        out_shape=jax.ShapeDtypeStruct((rows, 3 * width), BF16),
        cost_estimate=BRIEF,
        name="rope_back",
    )(dq, dkv, cosine, sine)

SCALE = HEAD_DIM ** -0.5
NEG = -1e30

def attn_fwd_kernel(c_ref, q_ref, kv_ref, o_ref, lse_ref, *, kb):
    rows, width = q_ref.shape
    heads = width // HEAD_DIM
    steps = rows // kb
    c = c_ref[0]
    for h in range(heads):
        lanes = slice(h * HEAD_DIM, (h + 1) * HEAD_DIM)
        vlanes = slice(width + h * HEAD_DIM, width + (h + 1) * HEAD_DIM)
        q = q_ref[:, lanes] * SCALE

        def block(j, carry, masked, q=q, lanes=lanes, vlanes=vlanes):
            top, total, acc = carry
            at = pl.ds(pl.multiple_of(j * kb, kb), kb)
            s = mm(kv_ref[at, lanes], q, 1, 1)
            if masked is not None:
                key = lax.broadcasted_iota(jnp.int32, s.shape, 0) + masked * kb
                s = jnp.where(key <= lax.broadcasted_iota(jnp.int32, s.shape, 1), s, NEG)
            new_top = jnp.maximum(top, jnp.max(s, 0, keepdims=True))
            p = jnp.exp(s - new_top)
            alpha = jnp.exp(top - new_top)
            total = total * alpha + jnp.sum(p, 0, keepdims=True)
            acc = acc * alpha + mm(kv_ref[at, vlanes], p.astype(BF16), 0, 0)
            return new_top, total, acc

        carry = (jnp.full((1, rows), NEG, F32), jnp.zeros((1, rows), F32), jnp.zeros((HEAD_DIM, rows), F32))
        carry = lax.fori_loop(0, c * steps, lambda j, x: block(j, x, None), carry)
        for i in range(steps):
            carry = block(c * steps + i, carry, i)
        top, total, acc = carry
        o_ref[:, lanes] = (acc / total).T.astype(BF16)
        lse_ref[h : h + 1, :] = top + jnp.log(total)

def attn_fwd(c, q, kv, kb=512):
    rows, width = q.shape
    heads = width // HEAD_DIM
    n = rows * kv.shape[0] * heads
    return pl.pallas_call(
        functools.partial(attn_fwd_kernel, kb=kb),
        in_specs=[pl.BlockSpec(memory_space=pltpu.SMEM), pl.BlockSpec(memory_space=pltpu.VMEM), pl.BlockSpec(memory_space=pltpu.VMEM)],
        out_specs=[pl.BlockSpec(memory_space=pltpu.VMEM), pl.BlockSpec(memory_space=pltpu.VMEM)],
        out_shape=[jax.ShapeDtypeStruct((rows, width), BF16), jax.ShapeDtypeStruct((heads, rows), F32)],
        cost_estimate=BRIEF,
        name="attn_fwd",
    )(c, q, kv)

def attn_bwd_kernel(c_ref, q_ref, kv_ref, o_ref, do_ref, lse_ref, dq_ref, dkv_ref, *, kb):
    rows, width = q_ref.shape
    heads = width // HEAD_DIM
    steps = rows // kb
    c = c_ref[0]
    total_steps = kv_ref.shape[0] // kb

    def clear(j, x):
        at = pl.ds(pl.multiple_of(j * kb, kb), kb)
        dkv_ref[at, :] = jnp.zeros((kb, 2 * width), BF16)
        return x

    lax.fori_loop((c + 1) * steps, total_steps, clear, 0)
    for h in range(heads):
        lanes = slice(h * HEAD_DIM, (h + 1) * HEAD_DIM)
        vlanes = slice(width + h * HEAD_DIM, width + (h + 1) * HEAD_DIM)
        q = q_ref[:, lanes] * SCALE
        do = do_ref[:, lanes]
        lse = lse_ref[h : h + 1, :]
        prod = do.astype(F32) * o_ref[:, lanes].astype(F32)
        delta = jnp.sum(prod.T, 0, keepdims=True)

        def block(j, dq, masked, q=q, do=do, lse=lse, delta=delta, lanes=lanes, vlanes=vlanes):
            at = pl.ds(pl.multiple_of(j * kb, kb), kb)
            k = kv_ref[at, lanes]
            s = mm(k, q, 1, 1)
            if masked is not None:
                key = lax.broadcasted_iota(jnp.int32, s.shape, 0) + masked * kb
                s = jnp.where(key <= lax.broadcasted_iota(jnp.int32, s.shape, 1), s, NEG)
            p = jnp.exp(s - lse)
            dp = mm(kv_ref[at, vlanes], do, 1, 1)
            ds = (p * (dp - delta)).astype(BF16)
            dkv_ref[at, vlanes] = mm(p.astype(BF16), do, 1, 0).astype(BF16)
            dkv_ref[at, lanes] = mm(ds, q, 1, 0).astype(BF16)
            return dq + mm(k, ds, 0, 0)

        dq = jnp.zeros((HEAD_DIM, rows), F32)
        dq = lax.fori_loop(0, c * steps, lambda j, x: block(j, x, None), dq)
        for i in range(steps):
            dq = block(c * steps + i, dq, i)
        dq_ref[:, lanes] = dq.T * SCALE

def attn_bwd(c, q, kv, o, do, lse, kb=512):
    rows, width = q.shape
    heads = width // HEAD_DIM
    n = rows * kv.shape[0] * heads
    vm = pl.BlockSpec(memory_space=pltpu.VMEM)
    return pl.pallas_call(
        functools.partial(attn_bwd_kernel, kb=kb),
        in_specs=[pl.BlockSpec(memory_space=pltpu.SMEM)] + [vm] * 5,
        out_specs=[vm, vm],
        out_shape=[jax.ShapeDtypeStruct((rows, width), F32), jax.ShapeDtypeStruct(kv.shape, BF16)],
        cost_estimate=pl.CostEstimate(flops=1 << 37, bytes_accessed=1 << 24, transcendentals=n),
        name="attn_bwd",
    )(c, q, kv, o, do, lse)


def expert_kernel(*refs):
    x_ref, gi_ref, first_hbm, up_hbm = refs[:4]
    inner_ref, gg_ref, gu_ref, x_out_ref, gn_ref, gate_v, up_v, sems = refs[-8:]
    gate_copy = pltpu.make_async_copy(first_hbm.at[:, gate_v.shape[1] :], gate_v, sems.at[0])
    up_copy = pltpu.make_async_copy(up_hbm, up_v, sems.at[1])
    first = pl.program_id(0) == 0

    @pl.when(first)
    def _():
        gate_copy.start()
        up_copy.start()
        gate_copy.wait()

    x = x_ref[...]
    x_out_ref[...] = x
    gate = mm(x, rows_of(gate_v), 1, 0)

    @pl.when(first)
    def _():
        up_copy.wait()

    up = mm(x, rows_of(up_v), 1, 0)
    gi = gi_ref[...].astype(F32)
    sigma = jax.nn.sigmoid(gate)
    active = gate * sigma
    inner_ref[...] = (active * up).astype(BF16)
    gg = (gi * up * sigma * (1.0 + gate * (1.0 - sigma))).astype(BF16)
    gu = (gi * active).astype(BF16)
    gg_ref[...] = gg
    gu_ref[...] = gu
    gn_ref[...] = (mm(gg, rows_of(gate_v), 1, 1) + mm(gu, rows_of(up_v), 1, 1)).astype(BF16)


def expert_core(x, gi, first, up_w, blocks, earlier):
    rows, width = x.shape
    shards, shard, hidden = up_w.shape
    tile = rows // len(blocks)
    total = gi.shape[0]

    def place(i):
        at = jnp.int32(blocks[0])
        for k, b in enumerate(blocks[1:]):
            at = jnp.where(i == k + 1, jnp.int32(b), at)
        return (at, 0)

    group = pl.BlockSpec((tile, width), lambda i: (i, 0))
    hbm = pl.BlockSpec(memory_space=pl.ANY)
    in_place = pl.BlockSpec((tile, hidden), place)
    return pl.pallas_call(
        expert_kernel,
        grid=(len(blocks),),
        in_specs=[group, in_place, hbm, hbm] + [hbm] * len(earlier),
        out_specs=[in_place, in_place, in_place, pl.BlockSpec((tile, width), place), group],
        out_shape=[jax.ShapeDtypeStruct((total, hidden), BF16)] * 3
        + [jax.ShapeDtypeStruct((total, width), BF16), jax.ShapeDtypeStruct((rows, width), BF16)],
        input_output_aliases={4 + k: k for k in range(len(earlier))},
        scratch_shapes=[
            pltpu.VMEM((shards, shard, hidden), BF16),
            pltpu.VMEM((shards, shard, hidden), BF16),
            pltpu.SemaphoreType.DMA((2,)),
        ],
        compiler_params=pltpu.CompilerParams(vmem_limit_bytes=60 << 20),
        cost_estimate=pl.CostEstimate(
            flops=8 * rows * width * hidden,
            bytes_accessed=4 * width * hidden + rows * (6 * width + 8 * hidden),
            transcendentals=rows * hidden,
        ),
        name="expert_core",
    )(x, gi, first, up_w, *earlier)


def rows_of(ref):
    return ref[...].reshape(-1, ref.shape[-1])


def grad_inner_kernel(*refs, tiles):
    *parts, share_ref, first_hbm, gy_ref, gi_ref, down_v, sem = refs
    i = pl.program_id(0)
    copy = pltpu.make_async_copy(first_hbm.at[:, : down_v.shape[1]], down_v, sem)

    @pl.when(i == 0)
    def _():
        copy.start()

    for k, part in enumerate(parts):

        @pl.when((i >= k * tiles) & (i < (k + 1) * tiles))
        def _(part=part):
            gy_ref[...] = (share_ref[...] * (RESIDUAL_SCALE * part[...].astype(F32))).astype(BF16)

    @pl.when(i == 0)
    def _():
        copy.wait()

    gi_ref[...] = mm(gy_ref[...], rows_of(down_v), 1, 0).astype(BF16)

def grad_inner_call(parts, share, first, tile=256):
    rows, width = parts[0].shape
    blocks, _, hidden = first.shape
    total = rows * len(parts)
    tiles = rows // tile
    row = lambda n: pl.BlockSpec((tile, n), lambda i: (i, 0))
    of = lambda k: pl.BlockSpec((tile, width), lambda i: (jnp.clip(i - k * tiles, 0, tiles - 1), 0))
    return pl.pallas_call(
        functools.partial(grad_inner_kernel, tiles=tiles),
        grid=(total // tile,),
        in_specs=[of(k) for k in range(len(parts))] + [row(1), pl.BlockSpec(memory_space=pl.ANY)],
        out_specs=[row(width), row(hidden)],
        out_shape=[jax.ShapeDtypeStruct((total, width), BF16), jax.ShapeDtypeStruct((total, hidden), BF16)],
        scratch_shapes=[
            pltpu.VMEM((blocks, width // blocks, hidden), BF16),
            pltpu.SemaphoreType.DMA,
        ],
        compiler_params=pltpu.CompilerParams(vmem_limit_bytes=56 << 20),
        cost_estimate=BRIEF,
        name="grad_inner",
    )(*parts, share[:, None], first)


def output_kernel(*refs, pieces):
    inner_ref, share_ref = refs[:2]
    first_hbm, *y_refs, down_v, sem = refs[-pieces - 3 :]
    i = pl.program_id(0)
    copy = pltpu.make_async_copy(first_hbm.at[:, : down_v.shape[1]], down_v, sem)

    @pl.when(i == 0)
    def _():
        copy.start()
        copy.wait()

    y = share_ref[...] * mm(inner_ref[...], rows_of(down_v), 1, 1)
    if len(refs) == pieces + 6:
        y = y + refs[2][...].astype(F32)
    y = y.astype(BF16)
    for k, y_ref in enumerate(y_refs):

        @pl.when(i * pieces // pl.num_programs(0) == k)
        def _(y_ref=y_ref):
            y_ref[...] = y


def output_call(inner, share, weights, width, start, count, other=None, pieces=1, tile=256):
    blocks, _, hidden = weights.shape
    at = lambda n: pl.BlockSpec((tile, n), lambda i: (i + start // tile, 0))
    others = [] if other is None else [other]
    if pieces == 1:
        out = pl.BlockSpec((tile, width), lambda i: (i, 0))
    else:
        out = pl.BlockSpec((tile, width), lambda i: (0, 0))
    return pl.pallas_call(
        functools.partial(output_kernel, pieces=pieces),
        grid=(count // tile,),
        in_specs=[at(hidden), at(1)] + [at(width)] * len(others) + [pl.BlockSpec(memory_space=pl.ANY)],
        out_specs=[out] * pieces,
        out_shape=[jax.ShapeDtypeStruct((count // pieces, width), BF16)] * pieces,
        scratch_shapes=[
            pltpu.VMEM((blocks, width // blocks, hidden), BF16),
            pltpu.SemaphoreType.DMA,
        ],
        compiler_params=pltpu.CompilerParams(vmem_limit_bytes=56 << 20),
        cost_estimate=BRIEF,
        name="expert_out",
    )(inner, share[:, None], *others, weights)


def arrange_kernel(depth_ref, *refs, offsets):
    out_ref = refs[-1]
    for ref, offset in zip(refs, offsets):

        @pl.when(pl.program_id(0) == depth_ref[0] + offset)
        def _(ref=ref):
            out_ref[0] = ref[...]


def arrange(depth, below, above):
    blocks, rows, width = below[0].shape
    chips = len(below)
    offsets = [0] + [-i for i in range(1, chips)] + list(range(1, chips))

    def of(offset):
        def at(q, b, depth_ref):
            turn = depth_ref[0] + offset
            return (jnp.where(q == turn, b, jnp.where(q < turn, 0, blocks - 1)), 0, 0)

        return pl.BlockSpec((1, rows, width), at)

    whole = pl.pallas_call(
        functools.partial(arrange_kernel, offsets=offsets),
        grid_spec=pltpu.PrefetchScalarGridSpec(
            num_scalar_prefetch=1,
            grid=(chips, blocks),
            in_specs=[of(offset) for offset in offsets],
            out_specs=pl.BlockSpec((1, 1, rows, width), lambda q, b, depth_ref: (b, q, 0, 0)),
        ),
        out_shape=jax.ShapeDtypeStruct((blocks, chips, rows, width), below[0].dtype),
        cost_estimate=BRIEF,
        name="arrange",
    )(depth.astype(jnp.int32).reshape(1), *below, *above[1:])
    return whole.reshape(-1, width)


def wgrad_kernel(x_ref, g_ref, o_ref):
    o_ref[...] = mm(x_ref[...], g_ref[...], 0, 0).astype(BF16)

def wgrad_call(x, g, tile=384):
    rows, width = x.shape
    hidden = g.shape[1]
    return pl.pallas_call(
        wgrad_kernel,
        grid=(width // tile,),
        in_specs=[pl.BlockSpec((rows, tile), lambda i: (0, i)), pl.BlockSpec((rows, hidden), lambda i: (0, 0), pipeline_mode=pl.Buffered(1))],
        out_specs=pl.BlockSpec((tile, hidden), lambda i: (i, 0)),
        out_shape=jax.ShapeDtypeStruct((width, hidden), BF16),
        compiler_params=pltpu.CompilerParams(vmem_limit_bytes=56 << 20),
        cost_estimate=BRIEF,
        name="weight_grad",
    )(x, g)


def wgrad_halves_kernel(x_ref, g_ref, lo_ref, hi_ref):
    grad = mm(x_ref[...], g_ref[...], 0, 0).astype(BF16)
    cut = lo_ref.shape[1]
    for b in range(lo_ref.shape[0]):
        lo_ref[b] = grad[2 * b * cut : (2 * b + 1) * cut]
        hi_ref[b] = grad[(2 * b + 1) * cut : (2 * b + 2) * cut]


def wgrad_halves(x, g, blocks, step=4):
    rows, width = x.shape
    hidden = g.shape[1]
    cut = width // blocks // 2
    half = pl.BlockSpec((step, cut, hidden), lambda i: (i, 0, 0))
    return pl.pallas_call(
        wgrad_halves_kernel,
        grid=(blocks // step,),
        in_specs=[
            pl.BlockSpec((rows, step * 2 * cut), lambda i: (0, i)),
            pl.BlockSpec((rows, hidden), lambda i: (0, 0), pipeline_mode=pl.Buffered(1)),
        ],
        out_specs=[half, half],
        out_shape=[jax.ShapeDtypeStruct((blocks, cut, hidden), BF16)] * 2,
        compiler_params=pltpu.CompilerParams(vmem_limit_bytes=60 << 20),
        cost_estimate=BRIEF,
        name="weight_grad",
    )(x, g)


def resid_backward_kernel(tok_ref, att_ref, gn_ref, cot_ref, gain_ref, resid_grad_ref, att_grad_ref, part_ref):
    resid = tok_ref[...].astype(F32) + RESIDUAL_SCALE * att_ref[...].astype(F32)
    inverse = lax.rsqrt(jnp.mean(resid * resid, -1, keepdims=True) + EPS)
    grad = gn_ref[...].astype(F32)
    scaled = gain_ref[...] * grad
    mean = jnp.mean(scaled * resid, -1, keepdims=True)
    out = cot_ref[...].astype(F32) + inverse * scaled - resid * (inverse * inverse * inverse * mean)
    resid_grad_ref[...] = out
    att_grad_ref[...] = (RESIDUAL_SCALE * out).astype(BF16)

    @pl.when(pl.program_id(0) == 0)
    def _():
        part_ref[...] = jnp.zeros_like(part_ref)

    part_ref[...] += jnp.sum(grad * resid * inverse, 0, keepdims=True)


def resid_backward(tokens, attn_total, grad_n2, cotangent, gain, tile=128):
    rows, width = tokens.shape
    row = pl.BlockSpec((tile, width), lambda i: (i, 0))
    line = pl.BlockSpec((1, width), lambda i: (0, 0))
    return pl.pallas_call(
        resid_backward_kernel,
        grid=(rows // tile,),
        in_specs=[row] * 4 + [line],
        out_specs=[row, row, line],
        out_shape=[
            jax.ShapeDtypeStruct((rows, width), F32),
            jax.ShapeDtypeStruct((rows, width), BF16),
            jax.ShapeDtypeStruct((1, width), F32),
        ],
        cost_estimate=BRIEF,
        name="resid_backward",
    )(tokens, attn_total, grad_n2, cotangent, gain[None, :])


def pair_grad_kernel(a_ref, b_ref, c_ref, d_ref, o_ref):
    cut = b_ref.shape[1]
    o_ref[:, :cut] = mm(a_ref[...], b_ref[...], 0, 0).astype(BF16)
    o_ref[:, cut:] = mm(c_ref[...], d_ref[...], 0, 0).astype(BF16)


def pair_grad(a, b, c, d, tile=384):
    rows, width = a.shape
    total = b.shape[1] + d.shape[1]
    part = pl.BlockSpec((rows, tile), lambda i: (0, i))
    whole = lambda x: pl.BlockSpec(x.shape, lambda i: (0, 0))
    return pl.pallas_call(
        pair_grad_kernel,
        grid=(width // tile,),
        in_specs=[part, whole(b), part, whole(d)],
        out_specs=pl.BlockSpec((tile, total), lambda i: (i, 0)),
        out_shape=jax.ShapeDtypeStruct((width, total), BF16),
        compiler_params=pltpu.CompilerParams(vmem_limit_bytes=48 << 20),
        cost_estimate=BRIEF,
        name="pair_grad",
    )(a, b, c, d)


def attn_in_kernel(tok_ref, gain_ref, weight_ref, cos_ref, sin_ref, normed_ref, q_ref, kv_ref):
    tokens = tok_ref[...].astype(F32)
    inverse = lax.rsqrt(jnp.mean(tokens * tokens, -1, keepdims=True) + EPS)
    normed_ref[...] = (tokens * inverse * gain_ref[...]).astype(BF16)
    rope_store(mm(normed_ref[...], weight_ref[...], 1, 0), cos_ref[...], sin_ref[...], q_ref, kv_ref)


def attn_in(tokens, gain, weight, cosine, sine, tile=256):
    rows, width = tokens.shape
    local = weight.shape[1] // 3
    row = lambda n: pl.BlockSpec((tile, n), lambda i: (i, 0))
    return pl.pallas_call(
        attn_in_kernel,
        grid=(rows // tile,),
        in_specs=[
            row(width),
            pl.BlockSpec((1, width), lambda i: (0, 0)),
            pl.BlockSpec(weight.shape, lambda i: (0, 0), pipeline_mode=pl.Buffered(1)),
            row(128),
            row(128),
        ],
        out_specs=[row(width), row(local), row(2 * local)],
        out_shape=[
            jax.ShapeDtypeStruct((rows, width), BF16),
            jax.ShapeDtypeStruct((rows, local), BF16),
            jax.ShapeDtypeStruct((rows, 2 * local), BF16),
        ],
        compiler_params=pltpu.CompilerParams(vmem_limit_bytes=48 << 20),
        cost_estimate=BRIEF,
        name="attn_in",
    )(tokens, gain[None, :], weight, cosine, sine)


def norm_backward(inputs, inverse, gain, grad_normed):
    scaled = gain[None, :] * grad_normed
    gain_grad = jnp.sum(grad_normed * inputs * inverse[:, None], 0)
    input_part = inverse[:, None] * scaled - inputs * (inverse**3)[:, None] * jnp.mean(
        scaled * inputs, -1, keepdims=True
    )
    return (gain_grad, input_part)


def together(*values):
    return lax.optimization_barrier(values)


def after(value, *earlier):
    return lax.optimization_barrier((value, *earlier))[0]


class Direct:
    parts = 1

    def __init__(self, axes):
        self.axes = axes

    def order(self, share):
        return share.reshape(-1)

    def spread(self, x):
        whole = lax.all_gather(x, self.axes, axis=0, tiled=True)
        return (lambda *values: values), (lambda: whole), (lambda x: [x])

    def exchange(self, x, core):
        whole = lax.all_gather(x, self.axes, axis=0, tiled=True)
        size = whole.shape[0] // 4
        sums, kept = [], ()
        for i in range(4):
            *kept, part = core(
                whole[i * size : (i + 1) * size], tuple(range(4 * i, 4 * i + 4)), kept
            )
            sums.append(part)
        whole = lax.psum_scatter(jnp.concatenate(sums, 0), self.axes, scatter_dimension=0, tiled=True)
        return kept, (lambda work: (whole, work(whole)[0]))

    def scatter(self, odd, even, work):
        done = work(odd)[0]
        whole = lax.psum_scatter(odd[0], self.axes, scatter_dimension=0, tiled=True)
        return done, (lambda *values: values), (lambda: whole)


class Paired:
    near = (0, 4, 2, 6, 1, 5, 3, 7)
    parts = 2

    def move(self, x, bits):
        return lax.ppermute(x, GROUP, [(j, j ^ bits) for j in range(8)])

    def order(self, share):
        me = lax.axis_index(GROUP)
        return share[jnp.bitwise_xor(me, jnp.array(self.near, jnp.int32))].reshape(-1)

    def pair(self, a, b):
        both = a if b is None else jnp.concatenate([a, b], 0)
        return jnp.concatenate([both, self.move(both, 1)], 0)

    def merge(self, group):
        half = group.shape[0] // 4
        both = group[: 2 * half] + self.move(group[2 * half :], 1)
        return both[:half], both[half:]

    def exchange(self, x, core):
        half = x.shape[0] // 2
        lo, hi = x[:half], x[half:]
        x_lo, y_hi = self.move(lo, 4), self.move(hi, 2)
        *kept, out0 = core(self.pair(x, None), (0, 1, 8, 9), ())
        out0, x_lo, y_hi = together(out0, x_lo, y_hi)
        d_lo, d_hi = self.move(x_lo, 2), self.move(y_hi, 4)
        hi, lo, out0 = together(hi, lo, out0)
        x_hi, y_lo = self.move(hi, 4), self.move(lo, 2)
        *kept, out1 = core(self.pair(x_lo, y_hi), (2, 5, 10, 13), kept)
        out1, d_lo, d_hi = together(out1, d_lo, d_hi)
        third = self.pair(d_lo, d_hi)
        third, px_lo, py_hi, p_lo, p_hi = together(third, *self.merge(out1), *self.merge(out0))
        px_lo, py_hi = self.move(px_lo, 4), self.move(py_hi, 2)
        *kept, out2 = core(third, (6, 7, 14, 15), kept)
        out2, x_hi, y_lo, px_lo, py_hi = together(out2, x_hi, y_lo, px_lo, py_hi)
        fourth = self.pair(x_hi, y_lo)
        fourth, pd_lo, pd_hi = together(fourth, *self.merge(out2))
        pd_lo, pd_hi = self.move(pd_lo, 4), self.move(pd_hi, 2)
        *kept, out3 = core(fourth, (3, 4, 11, 12), kept)
        out3, pd_lo, pd_hi = together(out3, pd_lo, pd_hi)

        def finish(work):
            px_hi, py_lo = self.merge(out3)
            done, px_hi = work(px_hi + pd_hi)
            py_lo = py_lo + pd_lo
            px_hi, py_lo = self.move(px_hi, 4), self.move(py_lo, 2)
            px_hi, py_lo, done = together(px_hi, py_lo, done)
            return jnp.concatenate([p_lo + px_lo + py_lo, p_hi + px_hi + py_hi], 0), done

        return kept, finish

    def spread(self, x):
        rows = x.shape[0] // 4
        depth = lax.axis_index("tp")
        mine = lax.dynamic_slice_in_dim(x, depth * rows, rows, 0)
        here = jnp.stack([mine, self.move(mine, 4), self.move(mine, 2), self.move(mine, 6)], 0)
        below, above = [here], [here]

        def step(*values):
            if len(below) == 1:
                values = together(here, *values)
                below[0] = above[0] = values[0]
                values = values[1:]
            else:
                values = together(below[-1], above[-1], *values)
                below[-1], above[-1] = values[:2]
                values = values[2:]
            if len(below) < 4:
                below.append(lax.ppermute(below[-1], "tp", [(0, 1), (1, 2), (2, 3)]))
                above.append(lax.ppermute(above[-1], "tp", [(3, 2), (2, 1), (1, 0)]))
            return values

        def finish():
            return arrange(depth, below, above)

        def share_out(whole):
            return [whole, self.move(whole, 1)]

        return step, finish, share_out

    def carry(self, x, y, d):
        moved = [self.move(d[0], 4), self.move(d[1], 2), self.move(x[0], 4), self.move(y[1], 2)]

        def hold(*values):
            values = together(*moved, *values)
            count = len(moved)
            moved[:] = values[:count]
            return values[count:]

        def settle(*values):
            values = together(*moved, *values)
            if len(moved) == 4:
                d_lo, d_hi, x_lo, y_hi = values[:4]
                x_hi, y_lo = self.move(x[1] + d_hi, 4), self.move(y[0] + d_lo, 2)
                moved[:] = [x_hi, y_lo, x_lo, y_hi, d_lo]
                return values[4:]
            moved[:] = values[:5]
            return values[5:]

        def arrived(own):
            x_hi, y_lo, x_lo, y_hi, _ = moved
            return jnp.concatenate([own[0] + x_lo + y_lo, own[1] + x_hi + y_hi], 0)

        return hold, settle, arrived

    def scatter(self, odd, even, work):
        other = self.move(odd[0], 1)
        size = other.shape[0] // 4
        d, hold = even(3 * size, size, other)
        middle, hold = even(size, 2 * size, other, d[0])
        x_lo, x_hi, y_lo, y_hi = middle
        done, y_hi = work(y_hi)
        hold, settle, arrived = self.carry((x_lo, x_hi), (y_lo, y_hi), (hold, d[1]))
        done = hold(*done)
        return done, settle, (lambda: arrived(even(0, size, other)[0]))


def make_body(experts, ep_axes, rest, tokens_by):
    def fetch(*weights):
        if rest is None:
            return lax.all_to_all(jnp.concatenate(weights, 1), ep_axes, 0, 0, tiled=True)
        found = (lax.all_to_all(weight, ep_axes, 0, 0, tiled=True) for weight in weights)
        return jnp.concatenate(
            [lax.all_gather(weight, rest, axis=1, tiled=True) for weight in found], 1
        )

    def halves(blocks):
        count = blocks.shape[1] if rest is None else blocks.shape[1] // lax.axis_size(rest)
        split = blocks.reshape(-1, count, blocks.shape[2])
        cut = count // 2
        return tuple(
            part.reshape(experts, -1, blocks.shape[2]) for part in (split[:, :cut], split[:, cut:])
        )

    def send(blocks):
        if rest is not None:
            blocks = lax.psum_scatter(blocks, rest, scatter_dimension=1, tiled=True)
        return lax.all_to_all(blocks, ep_axes, 0, 0, tiled=True)

    def give_back(grad):
        return send(grad.reshape(experts, -1, grad.shape[-1]))

    def body(
        hidden_in,
        out_cotangent,
        attn_gain,
        qkv_weight,
        out_weight,
        ffn_gain,
        gate_weight,
        up_weight,
        down_weight,
        expert_ids,
        route_weights,
    ):
        tokens = hidden_in[0].astype(F32)
        tok_count, width = tokens.shape
        shard = qkv_weight.shape[0]
        local_width = qkv_weight.shape[2]
        ctx = lax.axis_index("ctx")

        qkv_mat = lax.all_gather(
            qkv_weight.reshape(shard, 3 * local_width), GROUP, axis=0, tiled=True
        )
        cot_step, cot_finish, cot_share = tokens_by.spread(out_cotangent[0])
        small = jnp.concatenate(
            [
                attn_gain.astype(F32),
                ffn_gain.astype(F32),
                expert_ids[0].astype(F32).reshape(-1),
                route_weights[0].reshape(-1),
            ]
        )
        small = jnp.broadcast_to(small, (lax.axis_size(GROUP), 1, small.shape[0]))
        small = lax.all_to_all(small, GROUP, 0, 0, tiled=True)[:, 0]
        (early,) = together(jnp.concatenate([down_weight.swapaxes(1, 2), gate_weight], 1))
        small, early = cot_step(small, early)
        first = fetch(early) if rest is None else fetch(early[:, :shard], early[:, shard:])
        qkv_mat, small = together(qkv_mat, small)
        gain_one = small[:, :shard].reshape(-1)
        gain_two = small[:, shard : 2 * shard].reshape(-1)
        routes = small[:, 2 * shard :].reshape(-1, 2, tok_count, expert_ids.shape[2])
        if rest is not None:
            routes = routes.reshape(experts, -1, *routes.shape[1:])
            routes = lax.dynamic_index_in_dim(routes, lax.axis_index(rest), 1, keepdims=False)
        mine = lax.axis_index(ep_axes).astype(F32)
        share = jnp.sum(jnp.where(routes[:, 0] == mine, routes[:, 1], 0.0), -1)
        share = tokens_by.order(share)

        half = HEAD_DIM // 2
        positions = ctx * tok_count + jnp.arange(tok_count, dtype=jnp.int32)
        freqs = ROPE_BASE ** (-2.0 * jnp.arange(half, dtype=F32) / HEAD_DIM)
        angles = positions.astype(F32)[:, None] * freqs[None, :]
        cosine, sine = jnp.cos(angles), jnp.sin(angles)
        cosine = jnp.concatenate([cosine] * 4, 1)
        sine = jnp.concatenate([-sine, sine] * 2, 1)
        inverse1 = lax.rsqrt(jnp.mean(tokens * tokens, -1) + EPS)
        normed1, query, kv_here = attn_in(hidden_in[0], gain_one, qkv_mat, cosine, sine)

        kv_all = lax.all_gather(kv_here, "ctx", axis=0, tiled=True)
        cot_step(kv_here)
        cot_step()

        out_full = lax.all_gather(after(out_weight, kv_all), GROUP, axis=1, tiled=True)
        block = ctx.astype(jnp.int32).reshape(1)
        attended, log_norm = attn_fwd(block, query, kv_all)
        (attended,) = cot_step(attended)
        attended, cot_all, first = together(attended, cot_finish(), first)
        part_out = mm(attended, out_full, 1, 0).astype(BF16)
        attn_total = lax.psum(part_out, "tp")
        up_w = fetch(after(up_weight, part_out))
        grad_y, grad_inner = grad_inner_call(cot_share(after(cot_all, part_out)), share, first)
        attn_total, grad_inner = together(attn_total, grad_inner)
        resid = tokens + RESIDUAL_SCALE * attn_total.astype(F32)
        inverse2 = lax.rsqrt(jnp.mean(resid * resid, -1) + EPS)
        normed2 = (resid * inverse2[:, None] * gain_two[None, :]).astype(BF16)

        kept, finish = tokens_by.exchange(
            normed2,
            lambda x, blocks, earlier: expert_core(
                x, grad_inner, first, up_w, blocks, tuple(earlier)
            ),
        )
        inner, grad_gate, grad_up, normed_all = kept
        count = inner.shape[0] // tokens_by.parts

        def outputs(start, size, other=None, hold=None):
            rows, hold = (inner, None) if hold is None else together(inner, hold)
            pieces = 1 if other is None else size // 256
            return output_call(rows, share, first, width, start, size, other, pieces), hold

        grad_n2, odd_y = finish(lambda hold: outputs(inner.shape[0] - count, count, None, hold))

        grad_n2 = lax.psum(grad_n2, "tp")
        def down_work(hold):
            rows, hold = together(grad_y, hold)
            if rest is None:
                return wgrad_halves(rows, inner, experts), hold
            return halves(wgrad_call(rows, inner).reshape(experts, -1, inner.shape[1])), hold

        (down_lo, down_hi), mixed_settle, mixed_total = tokens_by.scatter(odd_y, outputs, down_work)
        down_lo = send(down_lo)
        grad_n2, down_hi = mixed_settle(grad_n2, down_hi)

        grad_resid, grad_att, ffn_part = resid_backward(
            hidden_in[0], attn_total, grad_n2, out_cotangent[0], gain_two
        )
        grad_attended = mm(grad_att, out_full, 1, 1).astype(BF16)
        grad_query, kv_grad = attn_bwd(block, query, kv_all, attended, grad_attended, log_norm)
        kv_grad, down_lo, down_hi, normed_all = mixed_settle(kv_grad, down_lo, down_hi, normed_all)
        kv_grad_here = lax.psum_scatter(kv_grad, "ctx", scatter_dimension=0, tiled=True)
        mixed = mixed_total()
        kv_grad_here, mixed = together(kv_grad_here, mixed)

        grad_proj = rope_back(grad_query, kv_grad_here, cosine, sine)
        part_n1 = mm(grad_proj, qkv_mat, 1, 1).astype(BF16)
        grad_n1, mixed = lax.psum((part_n1, mixed), "tp")
        down_hi = send(after(down_hi, part_n1))
        gate_grad = wgrad_call(after(normed_all, part_n1), grad_gate)
        weight_part = pair_grad(after(normed1, part_n1), grad_proj, grad_att, attended)
        gate_grad, down_hi, weight_part = together(gate_grad, down_hi, weight_part)
        down_weight_grad = jnp.concatenate([down_lo, down_hi], 1)
        gate_weight_grad = give_back(gate_grad)
        up_grad = wgrad_call(after(normed_all, gate_grad), grad_up)
        up_grad, gate_weight_grad = together(up_grad, gate_weight_grad)
        up_weight_grad = give_back(up_grad)
        grad_n1, mixed, up_weight_grad = together(grad_n1, mixed, up_weight_grad)

        weight_grad = lax.psum_scatter(weight_part, GROUP, scatter_dimension=0, tiled=True)
        weight_grad = weight_grad.astype(F32)
        block_out = (resid + RESIDUAL_SCALE * mixed.astype(F32)).astype(BF16)
        attn_part, input_part = norm_backward(tokens, inverse1, gain_one, grad_n1.astype(F32))
        input_grad = grad_resid + input_part
        parts = jnp.stack([attn_part, ffn_part[0]], 0).reshape(2, -1, shard).swapaxes(0, 1)
        gain_grads = jnp.sum(lax.all_to_all(parts, GROUP, 0, 0, tiled=True), 0)
        return (
            block_out[None],
            input_grad[None],
            gain_grads[0],
            weight_grad[:, : 3 * local_width].reshape(shard, 3, local_width),
            weight_grad[:, 3 * local_width :].T,
            gain_grads[1],
            gate_weight_grad.astype(F32),
            up_weight_grad.astype(F32),
            down_weight_grad.astype(F32).swapaxes(1, 2),
        )

    return body


def solution(mesh):
    experts = 8
    sizes = (mesh.shape["fsdp"], mesh.shape["ctx"])
    if sizes == (2, 4) and mesh.shape["tp"] == 4:
        ep_axes, rest, tokens_by = GROUP, None, Paired()
    elif sizes[0] * sizes[1] == experts:
        ep_axes, rest, tokens_by = GROUP, None, Direct(GROUP)
    else:
        assert sizes[0] == experts
        ep_axes, rest, tokens_by = ("fsdp",), "ctx", Direct(("fsdp",))
    in_specs = (
        P("fsdp", "ctx", None),
        P("fsdp", "ctx", None),
        P(GROUP),
        P(GROUP, None, "tp"),
        P("tp", GROUP),
        P(GROUP),
        P(None, GROUP, "tp"),
        P(None, GROUP, "tp"),
        P(None, "tp", GROUP),
        P("fsdp", "ctx", None),
        P("fsdp", "ctx", None),
    )
    out_specs = (
        P("fsdp", "ctx", None),
        P("fsdp", "ctx", None),
        P(GROUP),
        P(GROUP, None, "tp"),
        P("tp", GROUP),
        P(GROUP),
        P(None, GROUP, "tp"),
        P(None, GROUP, "tp"),
        P(None, "tp", GROUP),
    )
    body = make_body(experts, ep_axes, rest, tokens_by)
    return jax.shard_map(body, mesh=mesh, in_specs=in_specs, out_specs=out_specs, check_vma=False)
```
